256 devices in a mesh: seq: 64 (over z_lo, x, y), tp: 4 (over z_hi, core).
Axes of the slice: x: 4, y: 4, z: 8 (z_hi: 2, z_lo: 4; z = z_hi * 4 + z_lo), core: 2. Of those that a mesh axis runs over, the one named last changes fastest.
Arguments:
- byte_states: bfloat16 [16384, 1024], P('seq'), may hold values from -6 to 6
- enc_gain: bfloat16 [1024], replicated, may hold values from 0.25 to 1.75
- enc_qkv: bfloat16 [3, 1024, 1024], P(None, None, 'tp')
- enc_proj_out: bfloat16 [1024, 1024], P('tp'), may hold values from -0.1875 to 0.1875
- starts: int32 [64, 64], P('seq'), may hold values from 0 to 16384, as said below
- counts: int32 [64], P('seq'), may hold values from 32 to 64, as said below
- lift: bfloat16 [1024, 4096], P(None, 'tp')
- cross_kv: bfloat16 [2, 1024, 4096], P(None, None, 'tp')
- latent_gain: bfloat16 [4096], replicated, may hold values from 0.25 to 1.75
- lat_qkv: bfloat16 [3, 4096, 2048], P(None, 'seq', 'tp')
- lat_proj_out: bfloat16 [2048, 4096], P('tp', 'seq'), may hold values from -0.75 to 0.75
Outputs:
- byte_out: bfloat16 [16384, 1024], P('seq')
- latent_out: bfloat16 [4096, 4096], P('seq', 'tp')
The draws below stay inside these ranges and needn't reach their ends.
Inputs may be any that keep to these rules, and one draw needn't show every extreme that they name: `starts`: row s lists in increasing order the first byte (counted over all 16384 bytes) of each patch beginning in bytes s * 256 to (s + 1) * 256 - 1, then 16384 in unused places. Byte 0 begins a patch; every row's first patch begins fewer than 8 bytes into its block, and in some row exactly 7 bytes in. counts[s] is the number of patches listed in row s of starts; some row holds 64.
All inputs are finite; a program needn't handle non-finite values.
Results may differ from the reference program's by a relative error of at most 0.018.
Values may be sent and summed in bfloat16 or wider, within the bound.
No kernel may reach another device: no remote copies, remote signals or barrier semaphores. Data moves between devices by JAX's collectives and lax.ppermute only.
A program may use at most 128 MiB of HBM per device.

```python
import math
import jax
import jax.numpy as jnp
from jax import lax

DE = 1024
EH = 64
D = 4096
HD = 128
HL = 16
WIN = 512
SPILL = 8
B_DEV = 256
BYTES = 16384
P_CAP = 64
C_MIN = 32
N_SEQ = 64


def patch_table(key):
    stream = jax.random.fold_in(key, 11)
    split_keys = jax.random.split(stream, 5)
    spill_row = jax.random.randint(split_keys[0], (), 1, N_SEQ)
    full_row = (spill_row + jax.random.randint(split_keys[1], (), 1, N_SEQ)) % N_SEQ
    spread = P_CAP - C_MIN
    first_draw = jax.random.randint(split_keys[2], (N_SEQ,), 0, spread + 1)
    second_draw = jax.random.randint(split_keys[3], (N_SEQ,), 0, spread + 1)
    amounts = P_CAP - first_draw * second_draw // spread
    row_ids = jnp.arange(N_SEQ, dtype=jnp.int32)
    amounts = jnp.where(row_ids == full_row, P_CAP, jnp.where(row_ids == spill_row, C_MIN, amounts))
    slot_ids = jnp.arange(P_CAP, dtype=jnp.int32)
    lower_edge = slot_ids[None, :] * B_DEV // amounts[:, None]
    upper_edge = (slot_ids[None, :] + 1) * B_DEV // amounts[:, None]
    span_sizes = jnp.maximum(upper_edge - lower_edge, 1)
    jitter = jax.random.randint(split_keys[4], (N_SEQ, P_CAP), 0, span_sizes)
    first_col = slot_ids[None, :] == 0
    jitter = jnp.where(first_col & (row_ids[:, None] == spill_row), span_sizes - 1, jitter)
    jitter = jnp.where(first_col & (row_ids[:, None] == 0), 0, jitter)
    start_table = jnp.where(slot_ids[None, :] < amounts[:, None], row_ids[:, None] * B_DEV + lower_edge + jitter, BYTES)
    return (start_table.astype(jnp.int32), amounts.astype(jnp.int32))


def draw_starts(key, part):
    return patch_table(key)[0]


def draw_counts(key, part):
    return patch_table(key)[1]


def weight_block(key, shape, fan_in):
    multiplier = 1.0 / math.sqrt(fan_in)
    return jax.random.truncated_normal(key, -4.0, 4.0, shape, jnp.float32) * multiplier


def draw_byte_states(key, part):
    independent = jax.random.normal(jax.random.fold_in(key, 21), (BYTES, DE), jnp.float32)
    values = independent
    return jnp.clip(values, -6.0, 6.0).astype(jnp.bfloat16)


def draw_enc_qkv(key, part):
    query_cols = weight_block(jax.random.fold_in(key, 31), (DE, DE), DE)
    key_cols = weight_block(jax.random.fold_in(key, 32), (DE, DE), DE)
    value_cols = weight_block(jax.random.fold_in(key, 33), (DE, DE), DE)
    return jnp.stack([query_cols, key_cols, value_cols]).astype(jnp.bfloat16)


def cross_tables(key):
    stream = jax.random.fold_in(key, 41)
    lift_cols = weight_block(jax.random.fold_in(stream, 1), (DE, D), DE)
    key_cols = weight_block(jax.random.fold_in(stream, 2), (DE, D), DE)
    value_cols = weight_block(jax.random.fold_in(stream, 3), (DE, D), DE)
    return (lift_cols, jnp.stack([key_cols, value_cols]))


def draw_lift(key, part):
    return cross_tables(key)[0].astype(jnp.bfloat16)


def draw_cross_kv(key, part):
    return cross_tables(key)[1].astype(jnp.bfloat16)


def draw_lat_qkv(key, part):
    query_cols = weight_block(jax.random.fold_in(key, 51), (D, HL * HD), D)
    key_cols = weight_block(jax.random.fold_in(key, 52), (D, HL * HD), D)
    value_cols = weight_block(jax.random.fold_in(key, 53), (D, HL * HD), D)
    return jnp.stack([query_cols, key_cols, value_cols]).astype(jnp.bfloat16)


def shard_levels(key, shape, pieces, low, high):
    loudness, own = 1.0, jax.random.fold_in(key, 6)
    for dim, blocks in pieces:
        heights = jnp.exp(jax.random.uniform(jax.random.fold_in(own, dim), (blocks,), jnp.float32, low / len(pieces), high / len(pieces)))
        loudness = loudness * jnp.repeat(heights, shape[dim] // blocks).reshape([-1 if axis == dim else 1 for axis in range(len(shape))])
    return loudness


def bell_draw(rng, shape, deviation, limit, cuts=(), held_as=jnp.bfloat16):
    result = jax.random.normal(rng, shape, jnp.float32) * deviation
    if len(cuts) > 0:
        result = shard_levels(rng, shape, cuts, -0.22, 0.18) * result
    return jnp.clip(result, min=-limit, max=limit).astype(held_as)


def setup_inputs(seed: int = 0) -> dict:
    splits = jax.random.split(jax.random.key(seed), 12)
    byte_states = draw_byte_states(jax.random.fold_in(splits[11], 71), 0)
    enc_gain = jnp.clip(1.0 + 0.15 * jax.random.normal(splits[1], (DE,), jnp.float32), 0.25, 1.75).astype(jnp.bfloat16)
    enc_qkv = draw_enc_qkv(jax.random.fold_in(splits[11], 71), 0)
    enc_proj_out = bell_draw(splits[3], (DE, DE), DE ** -0.5, 0.1875, ((0, 4),))
    starts = draw_starts(jax.random.fold_in(splits[11], 71), 0)
    counts = draw_counts(jax.random.fold_in(splits[11], 71), 0)
    lift = draw_lift(jax.random.fold_in(splits[11], 71), 0)
    cross_kv = draw_cross_kv(jax.random.fold_in(splits[11], 71), 0)
    latent_gain = jnp.clip(1.0 + 0.15 * jax.random.normal(splits[8], (D,), jnp.float32), 0.25, 1.75).astype(jnp.bfloat16)
    lat_qkv = draw_lat_qkv(jax.random.fold_in(splits[11], 71), 0)
    lat_proj_out = bell_draw(splits[10], (HL * HD, D), (HL * HD // 32) ** -0.5, 0.75, ((0, 4), (1, 64)))
    return dict(byte_states=byte_states, enc_gain=enc_gain, enc_qkv=enc_qkv, enc_proj_out=enc_proj_out, starts=starts, counts=counts, lift=lift, cross_kv=cross_kv, latent_gain=latent_gain, lat_qkv=lat_qkv, lat_proj_out=lat_proj_out)


epsilon = 1e-05
rope_base = 500000.0
far_position = 1 << 30

def rms_scale(values, gain_row):
    mean_square = lax.optimization_barrier(jnp.mean(values * values, axis=-1, keepdims=True))
    return values * lax.rsqrt(mean_square + epsilon) * gain_row

def masked_softmax(scores, allowed):
    scores = jnp.where(allowed, scores, -1e+30)
    largest = lax.optimization_barrier(jnp.max(scores, axis=-1, keepdims=True))
    raised = jnp.where(allowed, jnp.exp(scores - largest), 0.0)
    return raised / lax.optimization_barrier(jnp.sum(raised, axis=-1, keepdims=True))

def rotate(values, position):
    halfway = values.shape[-1] // 2
    frequency = jnp.power(rope_base, -2.0 * jnp.arange(halfway, dtype=jnp.float32) / values.shape[-1])
    angles = position.astype(jnp.float32)[:, None] * frequency[None, :]
    cosine = jnp.cos(angles)[:, None, :]
    sine_rows = jnp.sin(angles)[:, None, :]
    lower_half = values[..., :halfway]
    upper_half = values[..., halfway:]
    return jnp.concatenate([lower_half * cosine - upper_half * sine_rows, upper_half * cosine + lower_half * sine_rows], axis=-1)

def encoder_layer(byte_states, enc_gain, enc_qkv, enc_proj_out):
    states = byte_states.astype(jnp.float32)
    normed = rms_scale(states, enc_gain.astype(jnp.float32)).astype(jnp.bfloat16)
    projected = jnp.einsum('bd,idc->ibc', normed.astype(jnp.float32), enc_qkv.astype(jnp.float32)).astype(jnp.bfloat16)
    head_count = projected.shape[2] // EH
    padding = jnp.zeros((WIN, projected.shape[2]), jnp.bfloat16)
    key_rows = jnp.concatenate([padding, projected[1]], axis=0)
    value_rows = jnp.concatenate([padding, projected[2]], axis=0)

    def attend(block_id):
        opening = block_id * WIN
        queries = lax.dynamic_slice_in_dim(projected[0], opening, WIN, 0).reshape(WIN, head_count, EH).astype(jnp.float32)
        near_keys = lax.dynamic_slice_in_dim(key_rows, opening, 2 * WIN, 0).reshape(2 * WIN, head_count, EH).astype(jnp.float32)
        near_values = lax.dynamic_slice_in_dim(value_rows, opening, 2 * WIN, 0).reshape(2 * WIN, head_count, EH).astype(jnp.float32)
        scores = jnp.einsum('qhd,khd->hqk', queries, near_keys) * (1.0 / math.sqrt(EH))
        query_pos = opening + jnp.arange(WIN, dtype=jnp.int32)
        key_pos = opening - WIN + jnp.arange(2 * WIN, dtype=jnp.int32)
        allowed = (key_pos[None, :] <= query_pos[:, None]) & (key_pos[None, :] > query_pos[:, None] - WIN) & (key_pos[None, :] >= 0)
        weights = masked_softmax(scores, allowed[None]).astype(jnp.bfloat16)
        attended = jnp.einsum('hqk,khd->qhd', weights.astype(jnp.float32), near_values)
        return attended.reshape(WIN, head_count * EH).astype(jnp.bfloat16)
    attended = lax.map(attend, jnp.arange(BYTES // WIN, dtype=jnp.int32)).reshape(BYTES, -1)
    return (states + jnp.dot(attended, enc_proj_out, preferred_element_type=jnp.float32)).astype(jnp.bfloat16)

def patch_block(extended, first_byte, end_byte, in_use, anchor, lift, cross_kv):
    columns = anchor + jnp.arange(extended.shape[0], dtype=jnp.int32)
    inside = (columns[None, :] >= first_byte[:, None]) & (columns[None, :] < end_byte[:, None]) & in_use[:, None]
    member = inside.astype(jnp.bfloat16)
    totals = jnp.dot(member, extended, preferred_element_type=jnp.float32)
    lengths = jnp.maximum(lax.optimization_barrier(jnp.sum(inside.astype(jnp.float32), axis=1)), 1.0)
    pooled = (totals / lengths[:, None]).astype(jnp.bfloat16)
    lifted = jnp.dot(pooled, lift, preferred_element_type=jnp.float32)
    key_rows = jnp.dot(extended, cross_kv[0], preferred_element_type=jnp.float32).astype(jnp.bfloat16)
    value_rows = jnp.dot(extended, cross_kv[1], preferred_element_type=jnp.float32).astype(jnp.bfloat16)
    slot_total = first_byte.shape[0]
    head_count = lifted.shape[1] // HD
    queries = lifted.astype(jnp.bfloat16).reshape(slot_total, head_count, HD)
    scores = jnp.einsum('phd,khd->hpk', queries.astype(jnp.float32), key_rows.reshape(-1, head_count, HD).astype(jnp.float32)) * (1.0 / math.sqrt(HD))
    allowed = inside | (~in_use)[:, None] & (columns[None, :] == anchor)
    weights = masked_softmax(scores, allowed[None]).astype(jnp.bfloat16)
    crossed = jnp.einsum('hpk,khd->phd', weights.astype(jnp.float32), value_rows.reshape(-1, head_count, HD).astype(jnp.float32))
    crossed = crossed.reshape(slot_total, head_count * HD)
    return jnp.where(in_use[:, None], lifted + crossed, 0.0).astype(jnp.bfloat16)

def latent_layer(patch_rows, in_use, position, latent_gain, lat_qkv, lat_proj_out):
    states = patch_rows.astype(jnp.float32)
    normed = rms_scale(states, latent_gain.astype(jnp.float32)).astype(jnp.bfloat16)
    projected = jnp.einsum('pd,idc->ipc', normed.astype(jnp.float32), lat_qkv.astype(jnp.float32))
    row_total = patch_rows.shape[0]
    head_count = projected.shape[2] // HD
    queries = rotate(projected[0].reshape(row_total, head_count, HD), position).astype(jnp.bfloat16)
    key_rows = rotate(projected[1].reshape(row_total, head_count, HD), position).astype(jnp.bfloat16)
    value_rows = projected[2].reshape(row_total, head_count, HD).astype(jnp.bfloat16)
    key_pos = jnp.where(in_use, position, far_position)
    allowed = key_pos[None, :] <= position[:, None]

    def attend(head_rows):
        query_head, key_head, value_head = head_rows
        scores = jnp.dot(query_head, key_head.T, preferred_element_type=jnp.float32) * (1.0 / math.sqrt(HD))
        weights = masked_softmax(scores, allowed).astype(jnp.bfloat16)
        return jnp.dot(weights, value_head, preferred_element_type=jnp.float32).astype(jnp.bfloat16)
    attended = lax.map(attend, (queries.transpose(1, 0, 2), key_rows.transpose(1, 0, 2), value_rows.transpose(1, 0, 2)))
    attended = attended.transpose(1, 0, 2).reshape(row_total, head_count * HD)
    summed = states + jnp.dot(attended, lat_proj_out, preferred_element_type=jnp.float32)
    return jnp.where(in_use[:, None], summed, 0.0).astype(jnp.bfloat16)

def reference(byte_states, enc_gain, enc_qkv, enc_proj_out, starts, counts, lift, cross_kv, latent_gain, lat_qkv, lat_proj_out):
    encoded = encoder_layer(byte_states, enc_gain, enc_qkv, enc_proj_out)
    anchors = jnp.arange(N_SEQ, dtype=jnp.int32) * B_DEV
    first_local = starts[:, 0] - anchors
    next_first = jnp.concatenate([first_local[1:], jnp.zeros((1,), jnp.int32)])
    slot_ids = jnp.arange(P_CAP, dtype=jnp.int32)
    in_use = slot_ids[None, :] < counts[:, None]
    following = jnp.concatenate([starts[:, 1:], jnp.zeros((N_SEQ, 1), jnp.int32)], axis=1)
    patch_end = jnp.where(slot_ids[None, :] + 1 < counts[:, None], following, (anchors + B_DEV + next_first)[:, None])
    padded = jnp.concatenate([encoded, jnp.zeros((SPILL, DE), jnp.bfloat16)], axis=0)

    def one_shard(shard_items):
        anchor, first_byte, end_byte, shard_use = shard_items
        extended = lax.dynamic_slice_in_dim(padded, anchor, B_DEV + SPILL, 0)
        return patch_block(extended, first_byte, end_byte, shard_use, anchor, lift, cross_kv)
    patches = lax.map(one_shard, (anchors, starts, patch_end, in_use)).reshape(N_SEQ * P_CAP, -1)
    offsets = (jnp.cumsum(counts) - counts).astype(jnp.int32)
    position = (offsets[:, None] + slot_ids[None, :]).reshape(-1).astype(jnp.int32)
    latent = latent_layer(patches, in_use.reshape(-1), position, latent_gain, lat_qkv, lat_proj_out)
    return (encoded, latent)
```

```python
import math

import jax
import jax.numpy as jnp
from jax import lax
from jax.sharding import Mesh
from jax.sharding import PartitionSpec as P

EH = 64
HD = 128
WIN = 512
SPILL = 8
ZL, RX, RY, ZH, CO = ("z_lo", "ring_x", "ring_y", "z_hi", "core")
SEQ = (ZL, RX, RY)
TP = (ZH, CO)
ROWS = (RX, RY)
COLUMN = (ZL, ZH, CO)

epsilon = 1e-05
rope_base = 500000.0
far_position = 1 << 30
bf16 = jnp.bfloat16
f32 = jnp.float32


def shifted(value, axis, steps):
    count = lax.axis_size(axis)
    leading, last = (max(0, -steps), min(count, count - steps))
    return lax.ppermute(value, axis, [(source, source + steps) for source in range(leading, last)])


def exchanged(pieces, axis):
    return lax.all_to_all(pieces, axis, split_axis=0, concat_axis=0, tiled=True)


def gathered(value, axis):
    return exchanged(jnp.broadcast_to(value, (lax.axis_size(axis), *value.shape)), axis)


def rms_factor(values):
    return lax.rsqrt(jnp.mean(values * values, axis=-1, keepdims=True) + epsilon)


def masked_softmax(scores, allowed):
    scores = jnp.where(allowed, scores, -1e30)
    largest = jnp.max(scores, axis=-1, keepdims=True)
    raised = jnp.where(allowed, jnp.exp(scores - largest), 0.0)
    return raised / jnp.sum(raised, axis=-1, keepdims=True)


def rotate(values, position):
    halfway = values.shape[-1] // 2
    frequency = jnp.power(rope_base, -2.0 * jnp.arange(halfway, dtype=f32) / values.shape[-1])
    angles = position.astype(f32)[:, None] * frequency[None, :]
    cosine, sine = (jnp.cos(angles), jnp.sin(angles))
    lower, upper = (values[..., :halfway], values[..., halfway:])
    return jnp.concatenate(
        [lower * cosine - upper * sine, upper * cosine + lower * sine], axis=-1
    )


def encoder_heads(normed, weights):
    return jnp.einsum("bd,idc->ibc", normed, weights, preferred_element_type=f32).astype(bf16)


def encoder_attention(queries, keys_values, anchor):
    rows, width = queries.shape
    heads = width // EH
    spans = keys_values.shape[0]
    keys, values = (keys_values[:, :width], keys_values[:, width:])
    scores = jnp.einsum(
        "qhd,khd->hqk",
        queries.reshape(rows, heads, EH),
        keys.reshape(spans, heads, EH),
        preferred_element_type=f32,
    ) * (1.0 / math.sqrt(EH))
    query_pos = anchor + jnp.arange(rows, dtype=jnp.int32)
    key_pos = anchor - WIN + jnp.arange(spans, dtype=jnp.int32)
    allowed = (
        (key_pos[None, :] <= query_pos[:, None])
        & (key_pos[None, :] > query_pos[:, None] - WIN)
        & (key_pos[None, :] >= 0)
    )
    weights = masked_softmax(scores, allowed[None]).astype(bf16)
    attended = jnp.einsum(
        "hqk,khd->qhd", weights, values.reshape(spans, heads, EH), preferred_element_type=f32
    )
    return attended.reshape(rows, width).astype(bf16)


def patch_block(extended, first_byte, end_byte, in_use, anchor, lift, cross_kv):
    columns = anchor + jnp.arange(extended.shape[0], dtype=jnp.int32)
    inside = (
        (columns[None, :] >= first_byte[:, None])
        & (columns[None, :] < end_byte[:, None])
        & in_use[:, None]
    )
    member = inside.astype(bf16)
    totals = jnp.dot(member, extended, preferred_element_type=f32)
    lengths = jnp.maximum(jnp.sum(inside.astype(f32), axis=1), 1.0)
    pooled = (totals / lengths[:, None]).astype(bf16)
    lifted = jnp.dot(pooled, lift, preferred_element_type=f32)
    key_rows = jnp.dot(extended, cross_kv[0], preferred_element_type=f32).astype(bf16)
    value_rows = jnp.dot(extended, cross_kv[1], preferred_element_type=f32).astype(bf16)
    slot_total = first_byte.shape[0]
    head_count = lifted.shape[1] // HD
    queries = lifted.astype(bf16).reshape(slot_total, head_count, HD)
    scores = jnp.einsum(
        "phd,khd->hpk",
        queries,
        key_rows.reshape(-1, head_count, HD),
        preferred_element_type=f32,
    ) * (1.0 / math.sqrt(HD))
    allowed = inside | (~in_use)[:, None] & (columns[None, :] == anchor)
    weights = masked_softmax(scores, allowed[None]).astype(bf16)
    crossed = jnp.einsum(
        "hpk,khd->phd",
        weights,
        value_rows.reshape(-1, head_count, HD),
        preferred_element_type=f32,
    )
    crossed = crossed.reshape(slot_total, head_count * HD)
    return jnp.where(in_use[:, None], lifted + crossed, 0.0).astype(bf16)


def shards(
    byte_states,
    enc_gain,
    enc_qkv,
    enc_proj_out,
    starts,
    counts,
    lift,
    cross_kv,
    latent_gain,
    lat_qkv,
    lat_proj_out,
):
    byte_rows, byte_width = byte_states.shape
    slots = starts.shape[1]
    columns = lax.axis_size(ZL)
    tensor = lax.axis_size(TP)
    groups = lax.axis_size(ROWS)
    anchor = lax.axis_index(SEQ) * byte_rows
    local_starts = starts[0]
    patch_count = counts[0]
    slot_ids = jnp.arange(slots, dtype=jnp.int32)
    in_use = slot_ids < patch_count

    first_local = (local_starts[0] - anchor).astype(bf16)
    edge = jnp.concatenate(
        [byte_states[:SPILL], jnp.broadcast_to(first_local, (SPILL, byte_width))], axis=0
    )
    edge = shifted(edge, SEQ, -1)
    next_first = edge[SPILL, 0].astype(jnp.int32)

    gain = enc_gain.astype(f32)
    states = byte_states.astype(f32)
    own = encoder_heads((states * rms_factor(states) * gain).astype(bf16), enc_qkv)
    own_kv = jnp.concatenate([own[1], own[2]], axis=1)
    far_kv = shifted(own_kv, SEQ, 2)
    near_kv = shifted(own_kv, SEQ, 1)

    share, depth, inner = lat_qkv.shape
    by_head = lat_qkv.reshape(share * depth, columns, HD).transpose(1, 0, 2)
    mark = jnp.broadcast_to(counts.astype(bf16), (columns, 16, HD))
    by_head = exchanged(jnp.concatenate([by_head, mark], axis=1), ZL)
    by_head = gathered(by_head, ROWS)
    all_counts = by_head[:, :, share * depth, 0].astype(jnp.int32).T
    latent_in = by_head[:, :, : share * depth].reshape(groups, columns, share, depth, HD)
    latent_in = latent_in.transpose(1, 0, 3, 2, 4).reshape(-1, share * HD)
    latent_in = (latent_in.astype(f32) * latent_gain.astype(f32)[:, None]).astype(bf16)

    enc_out = gathered(gathered(enc_proj_out, ZH), CO)

    out_part = gathered(lat_proj_out.T, TP)
    turned = [
        (a * tensor + b, b * tensor + a) for a in range(columns) for b in range(tensor)
    ]
    out_part = lax.ppermute(out_part, COLUMN, turned)
    out_part = gathered(out_part, ROWS)

    extra = edge[:SPILL].astype(f32)
    more = encoder_heads((extra * rms_factor(extra) * gain).astype(bf16), enc_qkv)
    more_kv = jnp.concatenate([more[1], more[2]], axis=1)
    queries = jnp.concatenate([own[0], more[0]], axis=0)
    keys_values = jnp.concatenate([far_kv, near_kv, own_kv, more_kv], axis=0)
    attended = gathered(encoder_attention(queries, keys_values, anchor), TP)
    attended = attended.reshape(*(lax.axis_size(name) for name in TP), *attended.shape[1:])
    blended = jnp.einsum("zcbw,czwd->bd", attended, enc_out, preferred_element_type=f32)
    extended = (jnp.concatenate([states, extra], axis=0) + blended).astype(bf16)
    encoded = extended[:byte_rows]

    following = jnp.concatenate([local_starts[1:], jnp.zeros((1,), jnp.int32)])
    patch_end = jnp.where(slot_ids + 1 < patch_count, following, anchor + byte_rows + next_first)
    patches = patch_block(extended, local_starts, patch_end, in_use, anchor, lift, cross_kv)

    rows = gathered(gathered(patches, (ZL, ZH)), CO)
    rows = rows.reshape(2, columns, 2, slots, -1).transpose(1, 3, 2, 0, 4)
    rows = rows.reshape(columns * slots, -1)
    factor = rms_factor(rows.astype(f32))
    projected = jnp.dot(rows, latent_in, preferred_element_type=f32) * factor

    flat_counts = all_counts.reshape(-1)
    block_ids = jnp.arange(flat_counts.shape[0], dtype=jnp.int32)
    offsets = jnp.sum(
        jnp.where(block_ids[None, :] < block_ids[:, None], flat_counts[None, :], 0), axis=1
    ).reshape(columns, groups)
    own_offsets = lax.dynamic_slice_in_dim(offsets, lax.axis_index(ROWS), 1, axis=1)
    position = (own_offsets + slot_ids[None, :]).reshape(-1)
    key_pos = jnp.where(
        slot_ids < all_counts.T[:, :, None], offsets.T[:, :, None] + slot_ids, far_position
    ).reshape(-1)
    queries = rotate(projected[:, :HD], position).astype(bf16)
    keys = rotate(projected[:, HD : 2 * HD], position).astype(bf16)
    keys_values = jnp.concatenate([keys, projected[:, 2 * HD :].astype(bf16)], axis=1)
    keys_values = gathered(keys_values, ROWS).reshape(-1, 2 * HD)
    scores = jnp.dot(
        queries, keys_values[:, :HD].T, preferred_element_type=f32
    ) * (1.0 / math.sqrt(HD))
    allowed = key_pos[None, :] <= position[:, None]
    scores = jnp.where(allowed, scores, -1e30)
    largest = jnp.max(scores, axis=-1, keepdims=True)
    raised = jnp.where(allowed, jnp.exp(scores - largest), 0.0)
    weighted = jnp.dot(raised.astype(bf16), keys_values[:, HD:], preferred_element_type=f32)
    heads = (weighted / jnp.sum(raised, axis=-1, keepdims=True)).astype(bf16)

    heads = jnp.broadcast_to(
        heads.reshape(columns, 1, slots, HD), (columns, tensor, slots, HD)
    ).reshape(columns * tensor, slots, HD)
    heads = exchanged(heads, COLUMN).reshape(columns, tensor, slots, HD)
    heads = heads.transpose(2, 1, 0, 3).reshape(slots, tensor, columns * HD)
    reduced = jnp.einsum("ptk,gtjk->pgj", heads, out_part, preferred_element_type=f32)
    reduced = reduced.reshape(slots, -1)
    latent = jnp.where(in_use[:, None], patches.astype(f32) + reduced, 0.0).astype(bf16)
    return (encoded, latent)


def solution(mesh):
    finer = Mesh(mesh.devices.reshape(4, 4, 4, 2, 2), (*SEQ, *TP))
    in_specs = (
        P(SEQ, None),
        P(),
        P(None, None, TP),
        P(TP, None),
        P(SEQ, None),
        P(SEQ),
        P(None, TP),
        P(None, None, TP),
        P(),
        P(None, SEQ, TP),
        P(TP, SEQ),
    )
    out_specs = (P(SEQ, None), P(SEQ, TP))
    return jax.shard_map(
        shards, mesh=finer, in_specs=in_specs, out_specs=out_specs, check_vma=False
    )
```

```python
import math

import jax
import jax.numpy as jnp
from jax import lax
from jax.sharding import Mesh
from jax.sharding import PartitionSpec as P

EH = 64
HD = 128
WIN = 512
SPILL = 8
ZL, RX, RY, ZH, CO = ("z_lo", "ring_x", "ring_y", "z_hi", "core")
SEQ = (ZL, RX, RY)
TP = (ZH, CO)
ROWS = (RX, RY)
COLUMN = (ZL, ZH, CO)

epsilon = 1e-05
rope_base = 500000.0
far_position = 1 << 30
bf16 = jnp.bfloat16
f32 = jnp.float32


def shifted(value, axis, steps):
    count = lax.axis_size(axis)
    leading, last = (max(0, -steps), min(count, count - steps))
    return lax.ppermute(value, axis, [(source, source + steps) for source in range(leading, last)])


def exchanged(pieces, axis):
    return lax.all_to_all(pieces, axis, split_axis=0, concat_axis=0, tiled=True)


def gathered(value, axis):
    return exchanged(jnp.broadcast_to(value, (lax.axis_size(axis), *value.shape)), axis)


def rms_factor(values):
    return lax.rsqrt(jnp.mean(values * values, axis=-1, keepdims=True) + epsilon)


def masked_softmax(scores, allowed):
    scores = jnp.where(allowed, scores, -1e30)
    largest = jnp.max(scores, axis=-1, keepdims=True)
    raised = jnp.where(allowed, jnp.exp(scores - largest), 0.0)
    return raised / jnp.sum(raised, axis=-1, keepdims=True)


def rotate(values, position):
    halfway = values.shape[-1] // 2
    frequency = jnp.power(rope_base, -2.0 * jnp.arange(halfway, dtype=f32) / values.shape[-1])
    angles = position.astype(f32)[:, None] * frequency[None, :]
    cosine, sine = (jnp.cos(angles), jnp.sin(angles))
    lower, upper = (values[..., :halfway], values[..., halfway:])
    return jnp.concatenate(
        [lower * cosine - upper * sine, upper * cosine + lower * sine], axis=-1
    )


def encoder_heads(normed, weights):
    return jnp.einsum("bd,idc->ibc", normed, weights, preferred_element_type=f32).astype(bf16)


def encoder_attention(queries, keys_values, anchor):
    rows, width = queries.shape
    heads = width // EH
    spans = keys_values.shape[0]
    keys, values = (keys_values[:, :width], keys_values[:, width:])
    scores = jnp.einsum(
        "qhd,khd->hqk",
        queries.reshape(rows, heads, EH),
        keys.reshape(spans, heads, EH),
        preferred_element_type=f32,
    ) * (1.0 / math.sqrt(EH))
    query_pos = anchor + jnp.arange(rows, dtype=jnp.int32)
    key_pos = anchor - WIN + jnp.arange(spans, dtype=jnp.int32)
    allowed = (
        (key_pos[None, :] <= query_pos[:, None])
        & (key_pos[None, :] > query_pos[:, None] - WIN)
        & (key_pos[None, :] >= 0)
    )
    weights = masked_softmax(scores, allowed[None]).astype(bf16)
    attended = jnp.einsum(
        "hqk,khd->qhd", weights, values.reshape(spans, heads, EH), preferred_element_type=f32
    )
    return attended.reshape(rows, width).astype(bf16)


def patch_block(extended, first_byte, end_byte, in_use, anchor, lift, cross_kv):
    columns = anchor + jnp.arange(extended.shape[0], dtype=jnp.int32)
    inside = (
        (columns[None, :] >= first_byte[:, None])
        & (columns[None, :] < end_byte[:, None])
        & in_use[:, None]
    )
    member = inside.astype(bf16)
    totals = jnp.dot(member, extended, preferred_element_type=f32)
    lengths = jnp.maximum(jnp.sum(inside.astype(f32), axis=1), 1.0)
    pooled = (totals / lengths[:, None]).astype(bf16)
    lifted = jnp.dot(pooled, lift, preferred_element_type=f32)
    key_rows = jnp.dot(extended, cross_kv[0], preferred_element_type=f32).astype(bf16)
    value_rows = jnp.dot(extended, cross_kv[1], preferred_element_type=f32).astype(bf16)
    slot_total = first_byte.shape[0]
    head_count = lifted.shape[1] // HD
    queries = lifted.astype(bf16).reshape(slot_total, head_count, HD)
    scores = jnp.einsum(
        "phd,khd->hpk",
        queries,
        key_rows.reshape(-1, head_count, HD),
        preferred_element_type=f32,
    ) * (1.0 / math.sqrt(HD))
    allowed = inside | (~in_use)[:, None] & (columns[None, :] == anchor)
    weights = masked_softmax(scores, allowed[None]).astype(bf16)
    crossed = jnp.einsum(
        "hpk,khd->phd",
        weights,
        value_rows.reshape(-1, head_count, HD),
        preferred_element_type=f32,
    )
    crossed = crossed.reshape(slot_total, head_count * HD)
    return jnp.where(in_use[:, None], lifted + crossed, 0.0).astype(bf16)


def paired(value, axis):
    other = lax.ppermute(value, axis, [(0, 1), (1, 0)])
    first = lax.axis_index(axis) == 0
    return jnp.concatenate(
        [jnp.where(first, value, other), jnp.where(first, other, value)], axis=0
    )


def around_ring(value, axis):
    count = lax.axis_size(axis)
    return [value] + [
        lax.ppermute(value, axis, [((i + k) % count, i) for i in range(count)])
        for k in range(1, count)
    ]


def around_column(value):
    low, high = (lax.axis_size(ZL), lax.axis_size(ZH))
    count = low * high
    rows, width = value.shape

    def moved(part, step):
        named = lambda z: z % count % low * high + z % count // low
        return lax.ppermute(part, (ZL, ZH), [(named(z), named(z + step)) for z in range(count)])

    here = lax.axis_index(ZH) * low + lax.axis_index(ZL)
    whole = jnp.zeros((low * rows, high * width), value.dtype)

    def placed(whole, part, z, shift=0):
        z = lax.bitwise_and(z, count - 1)
        across = lax.bitwise_and(z, low - 1) * rows + shift
        down = lax.shift_right_logical(z, low.bit_length() - 1) * width
        return lax.dynamic_update_slice(whole, part, (across, down))

    whole = placed(whole, value, here)
    up = down = value
    for step in range(1, count // 2):
        up, down = (moved(up, 1), moved(down, -1))
        whole = placed(placed(whole, up, here + (count - step)), down, here + step)
    half = rows // 2
    up, down = (moved(up[:half], 1), moved(down[half:], -1))
    return placed(placed(whole, up, here + count // 2), down, here + count // 2, half)


def shards(
    byte_states,
    enc_gain,
    enc_qkv,
    enc_proj_out,
    starts,
    counts,
    lift,
    cross_kv,
    latent_gain,
    lat_qkv,
    lat_proj_out,
):
    byte_rows, byte_width = byte_states.shape
    slots = starts.shape[1]
    columns = lax.axis_size(ZL)
    tensor = lax.axis_size(TP)
    groups = lax.axis_size(ROWS)
    anchor = lax.axis_index(SEQ) * byte_rows
    local_starts = starts[0]
    patch_count = counts[0]
    slot_ids = jnp.arange(slots, dtype=jnp.int32)
    in_use = slot_ids < patch_count

    gain = enc_gain.astype(f32)
    states = byte_states.astype(f32)
    own = encoder_heads((states * rms_factor(states) * gain).astype(bf16), enc_qkv)
    own_kv = jnp.concatenate([own[1], own[2]], axis=1)
    far_kv = shifted(own_kv, SEQ, 2)
    near_kv = shifted(own_kv, SEQ, 1)

    first_local = (local_starts[0] - anchor).astype(bf16)
    edge = jnp.concatenate(
        [byte_states[:SPILL], jnp.broadcast_to(first_local, (SPILL, byte_width))], axis=0
    )
    edge = shifted(edge, SEQ, -1)
    next_first = edge[SPILL, 0].astype(jnp.int32)

    share, depth, inner = lat_qkv.shape
    _, lat_qkv, enc_proj_out = lax.optimization_barrier((own_kv, lat_qkv, enc_proj_out))
    mark = jnp.broadcast_to(counts.astype(bf16), (16, HD))
    by_head = jnp.stack(
        [
            jnp.concatenate(
                [lat_qkv[:, :, k * HD : (k + 1) * HD].reshape(share * depth, HD), mark], axis=0
            )
            for k in range(columns)
        ]
    )
    by_head = exchanged(by_head, ZL)
    by_head = gathered(by_head, ROWS)
    all_counts = by_head[:, :, share * depth, 0].astype(jnp.int32).T
    latent_in = by_head[:, :, : share * depth].reshape(groups, columns, share, depth, HD)
    latent_in = latent_in.transpose(1, 0, 3, 2, 4).reshape(-1, share * HD)
    latent_in = (latent_in.astype(f32) * latent_gain.astype(f32)[:, None]).astype(bf16)
    latent_in = latent_in.reshape(2, 2, -1, share * HD)
    core = lax.axis_index(CO)
    own_in, other_in = (
        lax.dynamic_index_in_dim(latent_in, which, axis=1, keepdims=False).reshape(-1, share * HD)
        for which in (core, 1 - core)
    )

    enc_out = paired(paired(enc_proj_out[None], ZH)[None], CO)

    extra = edge[:SPILL].astype(f32)
    more = encoder_heads((extra * rms_factor(extra) * gain).astype(bf16), enc_qkv)
    more_kv = jnp.concatenate([more[1], more[2]], axis=1)
    queries = jnp.concatenate([own[0], more[0]], axis=0)
    keys_values = jnp.concatenate([far_kv, near_kv, own_kv, more_kv], axis=0)
    attended = encoder_attention(queries, keys_values, anchor)
    _, lat_proj_out = lax.optimization_barrier((attended, lat_proj_out))
    attended = lax.all_gather(attended, TP)
    attended = attended.reshape(*(lax.axis_size(name) for name in TP), *attended.shape[1:])
    blended = jnp.einsum("zcbw,czwd->bd", attended, enc_out, preferred_element_type=f32)
    extended = (jnp.concatenate([states, extra], axis=0) + blended).astype(bf16)
    encoded = extended[:byte_rows]

    part = lat_proj_out.T
    pieces = []
    for k in range(tensor):
        turned = [
            (a * tensor + b, (b + k) % columns * tensor + a)
            for a in range(columns)
            for b in range(tensor)
        ]
        pieces.append(lax.ppermute(part, COLUMN, turned))
    out_part = lax.all_gather(jnp.stack(pieces), ROWS)

    following = jnp.concatenate([local_starts[1:], jnp.zeros((1,), jnp.int32)])
    patch_end = jnp.where(slot_ids + 1 < patch_count, following, anchor + byte_rows + next_first)
    patches = patch_block(extended, local_starts, patch_end, in_use, anchor, lift, cross_kv)

    own_rows = around_column(patches)
    other_rows = lax.ppermute(own_rows, CO, [(0, 1), (1, 0)])
    squares = sum(
        jnp.sum(jnp.square(part.astype(f32)), axis=1, keepdims=True)
        for part in (own_rows, other_rows)
    )
    factor = lax.rsqrt(squares / latent_gain.shape[0] + epsilon)
    projected = jnp.dot(own_rows, own_in, preferred_element_type=f32)
    projected = projected + jnp.dot(other_rows, other_in, preferred_element_type=f32)
    projected = projected * factor

    flat_counts = all_counts.reshape(-1)
    block_ids = jnp.arange(flat_counts.shape[0], dtype=jnp.int32)
    offsets = jnp.sum(
        jnp.where(block_ids[None, :] < block_ids[:, None], flat_counts[None, :], 0), axis=1
    ).reshape(columns, groups)
    grid = (columns, *(lax.axis_size(name) for name in ROWS))
    start = (0, *(lax.axis_index(name) for name in ROWS))
    seen_counts, seen_offsets = (
        lax.dynamic_slice(jnp.tile(part.reshape(grid), (1, 2, 2)), start, grid)
        for part in (all_counts, offsets)
    )
    position = (seen_offsets[:, 0, 0][:, None] + slot_ids[None, :]).reshape(-1)
    seen_counts, seen_offsets = (
        part.transpose(1, 2, 0).reshape(-1, 1) for part in (seen_counts, seen_offsets)
    )
    key_pos = jnp.where(
        slot_ids < seen_counts, seen_offsets + slot_ids, far_position
    ).reshape(-1)
    queries = rotate(projected[:, :HD], position).astype(bf16)
    keys = rotate(projected[:, HD : 2 * HD], position).astype(bf16)
    values = projected[:, 2 * HD :].astype(bf16)
    keys = jnp.stack(around_ring(jnp.stack(around_ring(keys, RY)), RX))
    values = jnp.stack(around_ring(jnp.stack(around_ring(values, RX)), RY), axis=1)
    keys, values = (part.reshape(-1, HD) for part in (keys, values))
    scores = jnp.dot(queries, keys.T, preferred_element_type=f32) * (1.0 / math.sqrt(HD))
    allowed = key_pos[None, :] <= position[:, None]
    scores = jnp.where(allowed, scores, -1e30)
    largest = jnp.max(scores, axis=-1, keepdims=True)
    raised = jnp.where(allowed, jnp.exp(scores - largest), 0.0)
    weighted = jnp.dot(raised.astype(bf16), values, preferred_element_type=f32)
    heads = (weighted / jnp.sum(raised, axis=-1, keepdims=True)).astype(bf16)

    heads = jnp.broadcast_to(
        heads.reshape(columns, 1, slots, HD), (columns, tensor, slots, HD)
    ).reshape(columns * tensor, slots, HD)
    heads = exchanged(heads, COLUMN).reshape(columns, tensor, slots, HD)
    heads = heads.transpose(1, 2, 0, 3).reshape(tensor, slots, columns * HD)
    heads = jnp.concatenate([heads[::-1], heads[::-1]], axis=0)
    heads = lax.dynamic_slice_in_dim(heads, columns - 1 - lax.axis_index(ZL), tensor, axis=0)
    reduced = jnp.einsum("tpk,gtjk->pgj", heads, out_part, preferred_element_type=f32)
    reduced = reduced.reshape(slots, -1)
    latent = jnp.where(in_use[:, None], patches.astype(f32) + reduced, 0.0).astype(bf16)
    return (encoded, latent)


def solution(mesh):
    finer = Mesh(mesh.devices.reshape(4, 4, 4, 2, 2), (*SEQ, *TP))
    in_specs = (
        P(SEQ, None),
        P(),
        P(None, None, TP),
        P(TP, None),
        P(SEQ, None),
        P(SEQ),
        P(None, TP),
        P(None, None, TP),
        P(),
        P(None, SEQ, TP),
        P(TP, SEQ),
    )
    out_specs = (P(SEQ, None), P(SEQ, TP))
    return jax.shard_map(
        shards, mesh=finer, in_specs=in_specs, out_specs=out_specs, check_vma=False
    )
```

```python
import math

import jax
import jax.numpy as jnp
from jax import lax
from jax.experimental import pallas as pl
from jax.experimental.pallas import tpu as pltpu
from jax.sharding import Mesh
from jax.sharding import PartitionSpec as P

EH = 64
HD = 128
WIN = 512
SPILL = 8
EDGE = 16
ZL, RX, RY, ZH, CO = ("z_lo", "ring_x", "ring_y", "z_hi", "core")
SEQ = (ZL, RX, RY)
TP = (ZH, CO)
ROWS = (RX, RY)
COLUMN = (ZL, ZH, CO)

epsilon = 1e-05
rope_base = 500000.0
far_position = 1 << 30
bf16 = jnp.bfloat16
f32 = jnp.float32
i32 = jnp.int32
NT = (((1,), (1,)), ((), ()))


def shifted(value, axis, steps):
    count = lax.axis_size(axis)
    leading, last = (max(0, -steps), min(count, count - steps))
    return lax.ppermute(value, axis, [(source, source + steps) for source in range(leading, last)])


def exchanged(pieces, axis):
    return lax.all_to_all(pieces, axis, split_axis=0, concat_axis=0, tiled=True)


def swapped(value, axis):
    return lax.ppermute(value, axis, [(0, 1), (1, 0)])


def around_ring(value, axis):
    count = lax.axis_size(axis)
    return [value] + [
        lax.ppermute(value, axis, [((i + k) % count, i) for i in range(count)])
        for k in range(1, count)
    ]


def around_column(value):
    low, high = (lax.axis_size(ZL), lax.axis_size(ZH))
    count = low * high

    def moved(part, step):
        named = lambda z: z % count % low * high + z % count // low
        return lax.ppermute(part, (ZL, ZH), [(named(z), named(z + step)) for z in range(count)])

    pieces = [(value, 0, 0)]
    up = down = value
    for step in range(1, count // 2):
        up, down = (moved(up, 1), moved(down, -1))
        pieces += [(up, count - step, 0), (down, step, 0)]
    half = value.shape[0] // 2
    pieces += [(moved(up[:half], 1), count // 2, 0), (moved(down[half:], -1), count // 2, half)]
    return pieces


def on_chip(kernel, outs, scratch=(), limit=48, **extra):
    return pl.pallas_call(
        kernel,
        out_shape=outs,
        scratch_shapes=list(scratch),
        compiler_params=pltpu.CompilerParams(vmem_limit_bytes=limit << 20),
        **extra,
    )


def blank(shape, dtype=bf16):
    return jax.ShapeDtypeStruct(shape, dtype)


def rms_factor(values):
    return lax.rsqrt(jnp.mean(values * values, axis=-1, keepdims=True) + epsilon)


def encoder_heads(normed, weights):
    return jnp.einsum("bd,idc->ibc", normed, weights, preferred_element_type=f32).astype(bf16)


def encoder_attention(own_q, more_q, far, near, own, more, anchor):
    rows, width = own_q.shape
    total = rows + EDGE
    spans = WIN + total
    padded = -(-spans // 128) * 128

    def kernel(anchor_ref, q_ref, mq_ref, far_ref, near_ref, own_ref, more_ref, out_ref, held):
        at = 0
        for part in (far_ref, near_ref, own_ref, more_ref):
            held[at : at + part.shape[0], :] = part[...]
            at += part.shape[0]
        held[at:, :] = jnp.zeros((padded - at, 2 * width), bf16)
        queries = jnp.concatenate([q_ref[...], mq_ref[...]], axis=0)
        row = lax.broadcasted_iota(i32, (total, padded), 0)
        column = lax.broadcasted_iota(i32, (total, padded), 1)
        allowed = (
            (column - WIN <= row) & (column > row) & (column >= WIN - anchor_ref[0])
        )
        lane = lax.broadcasted_iota(i32, (total, HD), 1)
        for pair in range(width // HD):
            span = slice(pair * HD, (pair + 1) * HD)
            keys = held[:, span]
            values = held[:, width + pair * HD : width + (pair + 1) * HD]
            both = queries[:, span]
            done = None
            for side in range(HD // EH):
                mine = (lane >= side * EH) & (lane < (side + 1) * EH)
                query = jnp.where(mine, both, jnp.zeros_like(both))
                scores = lax.dot_general(query, keys, NT, preferred_element_type=f32)
                scores = jnp.where(allowed, scores * (1.0 / math.sqrt(EH)), -1e30)
                largest = jnp.max(scores, axis=-1, keepdims=True)
                raised = jnp.where(allowed, jnp.exp(scores - largest), 0.0)
                weights = (raised / jnp.maximum(jnp.sum(raised, axis=-1, keepdims=True), 1e-30))
                result = jnp.dot(weights.astype(bf16), values, preferred_element_type=f32)
                done = result if done is None else jnp.where(mine, result, done)
            out_ref[:, span] = done.astype(bf16)

    whole = pl.BlockSpec(memory_space=pltpu.VMEM)
    return on_chip(
        kernel,
        blank((total, width)),
        [pltpu.VMEM((padded, 2 * width), bf16)],
        in_specs=[pl.BlockSpec(memory_space=pltpu.SMEM)] + [whole] * 6,
        out_specs=whole,
    )(anchor.reshape(1), own_q, more_q, far, near, own, more)


def encoder_output(states, edge, attended, parts):
    rows, width = states.shape

    def kernel(states_ref, edge_ref, attended_ref, own_ref, high_ref, side_ref, both_ref, out_ref):
        here = lax.axis_index(TP)
        total = jnp.zeros((rows + EDGE, width), f32)
        for turn, part in ((0, own_ref), (2, high_ref), (1, side_ref), (3, both_ref)):
            total += jnp.dot(
                attended_ref[lax.bitwise_xor(here, turn)], part[...], preferred_element_type=f32
            )
        out_ref[:rows, :] = (states_ref[...].astype(f32) + total[:rows]).astype(bf16)
        out_ref[rows:, :] = (edge_ref[...].astype(f32) + total[rows:]).astype(bf16)

    return on_chip(kernel, blank((rows + EDGE, width)))(states, edge, attended, *parts)


def patch_block(extended, first_byte, end_byte, in_use, anchor, lift, cross_kv):
    columns = anchor + jnp.arange(extended.shape[0], dtype=i32)
    inside = (
        (columns[None, :] >= first_byte[:, None])
        & (columns[None, :] < end_byte[:, None])
        & in_use[:, None]
    )
    member = inside.astype(bf16)
    totals = jnp.dot(member, extended, preferred_element_type=f32)
    lengths = jnp.maximum(jnp.sum(inside.astype(f32), axis=1), 1.0)
    pooled = (totals / lengths[:, None]).astype(bf16)
    lifted = jnp.dot(pooled, lift, preferred_element_type=f32)
    key_rows = jnp.dot(extended, cross_kv[0], preferred_element_type=f32).astype(bf16)
    value_rows = jnp.dot(extended, cross_kv[1], preferred_element_type=f32).astype(bf16)
    slot_total = first_byte.shape[0]
    head_count = lifted.shape[1] // HD
    queries = lifted.astype(bf16).reshape(slot_total, head_count, HD)
    scores = jnp.einsum(
        "phd,khd->hpk",
        queries,
        key_rows.reshape(-1, head_count, HD),
        preferred_element_type=f32,
    ) * (1.0 / math.sqrt(HD))
    allowed = inside | (~in_use)[:, None] & (columns[None, :] == anchor)
    scores = jnp.where(allowed, scores, -1e30)
    largest = jnp.max(scores, axis=-1, keepdims=True)
    raised = jnp.where(allowed, jnp.exp(scores - largest), 0.0)
    weights = (raised / jnp.sum(raised, axis=-1, keepdims=True)).astype(bf16)
    crossed = jnp.einsum(
        "hpk,khd->phd",
        weights,
        value_rows.reshape(-1, head_count, HD),
        preferred_element_type=f32,
    )
    crossed = crossed.reshape(slot_total, head_count * HD)
    return jnp.where(in_use[:, None], lifted + crossed, 0.0).astype(bf16)


def placed_rows(pieces):
    rows, width = pieces[0][0].shape
    low, high = (lax.axis_size(ZL), lax.axis_size(ZH))

    def kernel(*refs):
        *parts, out_ref = refs
        here = lax.axis_index(ZH) * low + lax.axis_index(ZL)
        for part, (_, distance, shift) in zip(parts, pieces):
            z = lax.bitwise_and(here + distance, low * high - 1)
            across = lax.bitwise_and(z, low - 1) * rows + shift
            down = lax.shift_right_logical(z, low.bit_length() - 1) * width
            out_ref[
                pl.ds(pl.multiple_of(across, 16), part.shape[0]),
                pl.ds(pl.multiple_of(down, 128), width),
            ] = part[...]

    return on_chip(kernel, blank((low * rows, high * width)))(*(part for part, *_ in pieces))


def placed_weights(pieces, depth):
    along, columns, _, wide = pieces[0].shape
    count = len(pieces)

    def kernel(*refs):
        *parts, out_ref = refs
        by_x, by_y, core = (lax.axis_index(name) for name in (RX, RY, CO))
        for k, part in enumerate(parts):
            y = lax.bitwise_and(by_y + k, count - 1)
            for j in range(along):
                x = lax.bitwise_and(by_x + j, along - 1)
                start = pl.multiple_of((x * count + y) * depth, depth)
                for side in range(2):
                    for high in range(2):
                        t = 2 * high + lax.bitwise_xor(core, side)
                        out_ref[side, high, pl.ds(start, depth), :] = part[j, t, :depth, :]

    return on_chip(kernel, blank((2, 2, along * count * depth, wide)))(*pieces)


def latent_heads(own_rows, other_rows, weights, cosine, sine):
    rows, width = own_rows.shape
    full = 2 * width

    def kernel(own_ref, other_ref, weights_ref, cosine_ref, sine_ref, q_ref, k_ref, v_ref):
        squares = jnp.zeros((rows, 1), f32)
        total = jnp.zeros((rows, 3 * HD), f32)
        half = width // 2
        for side, part in enumerate((own_ref, other_ref)):
            for high in range(2):
                values = part[:, high * half : (high + 1) * half]
                wide = values.astype(f32)
                squares += jnp.sum(wide * wide, axis=1, keepdims=True)
                total += jnp.dot(values, weights_ref[side, high], preferred_element_type=f32)
        total = total * lax.rsqrt(squares / full + epsilon)
        for which, out_ref in enumerate((q_ref, k_ref)):
            value = total[:, which * HD : (which + 1) * HD]
            turned = value * cosine_ref[...] + pltpu.roll(value, HD // 2, 1) * sine_ref[...]
            out_ref[...] = turned.astype(bf16)
        v_ref[...] = total[:, 2 * HD :].astype(bf16)

    return on_chip(kernel, [blank((rows, HD))] * 3)(
        own_rows, other_rows, weights, cosine, sine
    )


def latent_attention(queries, keys, values, position, key_pos):
    rows = queries.shape[0]
    n_x, n_y = (len(keys), len(values))

    def kernel(*refs):
        q_ref, pos_ref, key_pos_ref = refs[:3]
        key_refs, value_refs = (refs[3 : 3 + n_x], refs[3 + n_x : 3 + n_x + n_y])
        out_ref, held = refs[3 + n_x + n_y :]
        query = q_ref[...]
        position = pos_ref[...]
        top = jnp.full((rows, rows), -1e30, f32)
        for x in range(n_x):
            for y in range(n_y):
                scores = lax.dot_general(
                    query, key_refs[x][y], NT, preferred_element_type=f32
                ) * (1.0 / math.sqrt(HD))
                allowed = key_pos_ref[x * n_y + y : x * n_y + y + 1, :] <= position
                scores = jnp.where(allowed, scores, -1e30)
                held[x * n_y + y] = scores
                top = jnp.maximum(top, scores)
        largest = jnp.max(top, axis=-1, keepdims=True)
        total = jnp.zeros((rows, rows), f32)
        weighted = jnp.zeros((rows, HD), f32)
        for x in range(n_x):
            for y in range(n_y):
                raised = jnp.exp(held[x * n_y + y] - largest)
                total += raised
                weighted += jnp.dot(
                    raised.astype(bf16), value_refs[y][x], preferred_element_type=f32
                )
        out_ref[...] = (weighted / jnp.sum(total, axis=-1, keepdims=True)).astype(bf16)

    return on_chip(
        kernel, blank((rows, HD)), [pltpu.VMEM((n_x * n_y, rows, rows), f32)]
    )(queries, position, key_pos, *keys, *values)


def latent_output(heads, out_part, patches, counts):
    groups, tensor, cut, deep = out_part.shape
    slots, width = patches.shape
    columns = lax.axis_size(ZL)
    joined = 4

    def kernel(count_ref, heads_ref, part_ref, patches_ref, out_ref):
        here = lax.axis_index(ZL)
        total = jnp.zeros((slots, joined * cut), f32)
        for k in range(tensor):
            t = lax.bitwise_and(here + tensor - k, tensor - 1)
            head = jnp.concatenate(
                [heads_ref[zl * tensor + t] for zl in range(columns)], axis=1
            )
            part = part_ref[:, k].reshape(joined * cut, deep)
            total += lax.dot_general(head, part, NT, preferred_element_type=f32)
        used = lax.broadcasted_iota(i32, (slots, joined * cut), 0) < count_ref[0]
        latent = jnp.where(used, patches_ref[...].astype(f32) + total, 0.0)
        out_ref[...] = latent.astype(bf16)

    across = pl.BlockSpec((slots, joined * cut), lambda g: (0, g))
    return on_chip(
        kernel,
        blank((slots, width)),
        grid=(groups // joined,),
        in_specs=[
            pl.BlockSpec(memory_space=pltpu.SMEM),
            pl.BlockSpec(heads.shape, lambda g: (0, 0, 0)),
            pl.BlockSpec((joined, tensor, cut, deep), lambda g: (g, 0, 0, 0)),
            across,
        ],
        out_specs=across,
    )(counts, heads, out_part, patches)


def shards(
    byte_states,
    enc_gain,
    enc_qkv,
    enc_proj_out,
    starts,
    counts,
    lift,
    cross_kv,
    latent_gain,
    lat_qkv,
    lat_proj_out,
):
    byte_rows, byte_width = byte_states.shape
    slots = starts.shape[1]
    columns = lax.axis_size(ZL)
    tensor = lax.axis_size(TP)
    groups = lax.axis_size(ROWS)
    block = lax.axis_index(SEQ)
    anchor = block * byte_rows
    local_starts = starts[0]
    patch_count = counts[0]
    slot_ids = jnp.arange(slots, dtype=i32)
    in_use = slot_ids < patch_count

    gain = enc_gain.astype(f32)
    states = byte_states.astype(f32)
    own = encoder_heads((states * rms_factor(states) * gain).astype(bf16), enc_qkv)
    own_kv = jnp.concatenate([own[1], own[2]], axis=1)
    far_kv = shifted(own_kv, SEQ, 2)
    near_kv = shifted(own_kv, SEQ, 1)

    first_local = (local_starts[0] - anchor).astype(bf16)
    edge = jnp.concatenate(
        [
            byte_states[:SPILL],
            jnp.broadcast_to(first_local, (EDGE - SPILL, byte_width)),
        ],
        axis=0,
    )
    edge = shifted(edge, SEQ, -1)
    next_first = edge[SPILL, 0].astype(i32)

    share, depth, inner = lat_qkv.shape
    own_gain = lax.dynamic_slice_in_dim(latent_gain, block * depth, depth).astype(f32)
    scaled = (lat_qkv.astype(f32) * own_gain[:, None]).astype(bf16)
    mark = jnp.broadcast_to(counts.astype(bf16), (EDGE, share * HD))
    by_head = jnp.stack(
        [
            jnp.concatenate(
                [
                    jnp.concatenate(
                        [scaled[i, :, k * HD : (k + 1) * HD] for i in range(share)], axis=1
                    ),
                    mark,
                ],
                axis=0,
            )
            for k in range(columns)
        ]
    )
    by_head = exchanged(by_head, ZL)

    out_high = swapped(enc_proj_out, ZH)
    out_parts = (enc_proj_out, out_high, swapped(enc_proj_out, CO), swapped(out_high, CO))

    extra = edge.astype(f32)
    more = encoder_heads((extra * rms_factor(extra) * gain).astype(bf16), enc_qkv)
    more_kv = jnp.concatenate([more[1], more[2]], axis=1)
    more_kv, by_head = lax.optimization_barrier((more_kv, by_head))
    by_head = around_ring(jnp.stack(around_ring(by_head, RX)), RY)
    attended = encoder_attention(own[0], more[0], far_kv, near_kv, own_kv, more_kv, anchor)
    attended, lat_proj_out = lax.optimization_barrier((attended, lat_proj_out))
    attended = lax.all_gather(attended, TP)
    extended = encoder_output(byte_states, edge, attended, out_parts)
    encoded = extended[:byte_rows]

    part = lat_proj_out.T
    turned = [
        lax.ppermute(
            part,
            COLUMN,
            [
                (a * tensor + b, (b + k) % columns * tensor + a)
                for a in range(columns)
                for b in range(tensor)
            ],
        )
        for k in range(tensor)
    ]
    out_part = lax.all_gather(jnp.stack(turned), ROWS)

    following = jnp.concatenate([local_starts[1:], jnp.zeros((1,), i32)])
    patch_end = jnp.where(slot_ids + 1 < patch_count, following, anchor + byte_rows + next_first)
    patches = patch_block(extended, local_starts, patch_end, in_use, anchor, lift, cross_kv)

    all_counts = jnp.stack([piece[:, :, depth, 0] for piece in by_head], axis=1).astype(i32)
    grid = (*(lax.axis_size(name) for name in ROWS), columns)
    here = tuple(lax.axis_index(name) for name in ROWS)
    order = sum(
        stride
        * lax.bitwise_and(lax.broadcasted_iota(i32, grid, dim) + start, grid[dim] - 1)
        for dim, stride, start in ((0, grid[1], here[0]), (1, 1, here[1]), (2, groups, 0))
    ).reshape(-1)
    flat_counts = all_counts.reshape(-1)
    offsets = jnp.sum(jnp.where(order[None, :] < order[:, None], flat_counts[None, :], 0), axis=1)
    position = (offsets[:columns, None] + slot_ids[None, :]).reshape(-1)
    key_pos = jnp.where(
        slot_ids[None, :] < flat_counts[:, None], offsets[:, None] + slot_ids[None, :], far_position
    ).reshape(groups, columns * slots)
    halfway = HD // 2
    frequency = jnp.power(rope_base, -2.0 * jnp.arange(halfway, dtype=f32) / HD)
    angles = position.astype(f32)[:, None] * frequency[None, :]
    cosine, sine = (jnp.cos(angles), jnp.sin(angles))
    cosine = jnp.concatenate([cosine, cosine], axis=1)
    sine = jnp.concatenate([-sine, sine], axis=1)
    latent_in = placed_weights(by_head, depth)

    own_rows = placed_rows(around_column(patches))
    other_rows = swapped(own_rows, CO)
    queries, keys, values = latent_heads(own_rows, other_rows, latent_in, cosine, sine)
    keys = around_ring(jnp.stack(around_ring(keys, RY)), RX)
    values = around_ring(jnp.stack(around_ring(values, RX)), RY)
    heads = latent_attention(queries, keys, values, position[:, None], key_pos)

    heads = jnp.broadcast_to(
        heads.reshape(columns, 1, slots, HD), (columns, tensor, slots, HD)
    ).reshape(columns * tensor, slots, HD)
    heads = exchanged(heads, COLUMN)
    latent = latent_output(heads, out_part, patches, counts)
    return (encoded, latent)


def solution(mesh):
    finer = Mesh(mesh.devices.reshape(4, 4, 4, 2, 2), (*SEQ, *TP))
    in_specs = (
        P(SEQ, None),
        P(),
        P(None, None, TP),
        P(TP, None),
        P(SEQ, None),
        P(SEQ),
        P(None, TP),
        P(None, None, TP),
        P(),
        P(None, SEQ, TP),
        P(TP, SEQ),
    )
    out_specs = (P(SEQ, None), P(SEQ, TP))
    return jax.shard_map(
        shards, mesh=finer, in_specs=in_specs, out_specs=out_specs, check_vma=False
    )
```

```python
import math

import jax
import jax.numpy as jnp
from jax import lax
from jax.experimental import pallas as pl
from jax.experimental.pallas import tpu as pltpu
from jax.sharding import Mesh
from jax.sharding import PartitionSpec as P

EH = 64
HD = 128
WIN = 512
SPILL = 8
EDGE = 16
ZL, RX, RY, ZH, CO = ("z_lo", "ring_x", "ring_y", "z_hi", "core")
SEQ = (ZL, RX, RY)
TP = (ZH, CO)
ROWS = (RX, RY)
COLUMN = (ZL, ZH, CO)

epsilon = 1e-05
rope_base = 500000.0
far_position = 1 << 30
bf16 = jnp.bfloat16
f32 = jnp.float32
i32 = jnp.int32
NT = (((1,), (1,)), ((), ()))


def shifted(value, axis, steps):
    count = lax.axis_size(axis)
    leading, last = (max(0, -steps), min(count, count - steps))
    return lax.ppermute(value, axis, [(source, source + steps) for source in range(leading, last)])


def exchanged(pieces, axis):
    return lax.all_to_all(pieces, axis, split_axis=0, concat_axis=0, tiled=True)


def swapped(value, axis):
    return lax.ppermute(value, axis, [(0, 1), (1, 0)])


def gathered(value, axis):
    return exchanged(jnp.broadcast_to(value, (lax.axis_size(axis), *value.shape)), axis)


def around_ring(value, axis):
    count = lax.axis_size(axis)
    return [value] + [
        lax.ppermute(value, axis, [((i + k) % count, i) for i in range(count)])
        for k in range(1, count)
    ]


def near_ring(value, axis):
    count = lax.axis_size(axis)

    def moved(part, step):
        return lax.ppermute(part, axis, [(i, (i + step) % count) for i in range(count)])

    up, down = (moved(value, 1), moved(value, -1))
    half = value.shape[0] // 2
    return [
        (value, 0, 0),
        (up, count - 1, 0),
        (down, 1, 0),
        (moved(up[:half], 1), 2, 0),
        (moved(down[half:], -1), 2, half),
    ]


def around_column(value):
    low, high = (lax.axis_size(ZL), lax.axis_size(ZH))
    count = low * high

    def moved(part, step):
        named = lambda z: z % count % low * high + z % count // low
        return lax.ppermute(part, (ZL, ZH), [(named(z), named(z + step)) for z in range(count)])

    pieces = [(value, 0, 0)]
    up = down = value
    for step in range(1, count // 2):
        up, down = (moved(up, 1), moved(down, -1))
        pieces += [(up, count - step, 0), (down, step, 0)]
    half = value.shape[0] // 2
    pieces += [(moved(up[:half], 1), count // 2, 0), (moved(down[half:], -1), count // 2, half)]
    return pieces


def on_chip(kernel, outs, scratch=(), limit=48, **extra):
    return pl.pallas_call(
        kernel,
        out_shape=outs,
        scratch_shapes=list(scratch),
        compiler_params=pltpu.CompilerParams(vmem_limit_bytes=limit << 20),
        cost_estimate=pl.CostEstimate(flops=1 << 20, transcendentals=0, bytes_accessed=1 << 20),
        **extra,
    )


def blank(shape, dtype=bf16):
    return jax.ShapeDtypeStruct(shape, dtype)


def encoder_heads(states, gain, weights):
    rows, width = states.shape
    share, _, inner = weights.shape

    def kernel(states_ref, gain_ref, weights_ref, query_ref, keys_values_ref):
        values = states_ref[...].astype(f32)
        factor = lax.rsqrt(jnp.mean(values * values, axis=-1, keepdims=True) + epsilon)
        normed = (values * factor * gain_ref[...].astype(f32)).astype(bf16)
        for i in range(1, share):
            keys_values_ref[:, (i - 1) * inner : i * inner] = jnp.dot(
                normed, weights_ref[i], preferred_element_type=f32
            ).astype(bf16)
        query_ref[...] = jnp.dot(normed, weights_ref[0], preferred_element_type=f32).astype(bf16)

    return on_chip(kernel, [blank((rows, inner)), blank((rows, (share - 1) * inner))])(
        states, gain.reshape(1, width), weights
    )


def encoder_attention(own_q, more_q, far, near, own, more, anchor):
    rows, width = own_q.shape
    total = rows + EDGE
    spans = WIN + total
    padded = -(-spans // 128) * 128

    def kernel(anchor_ref, q_ref, mq_ref, far_ref, near_ref, own_ref, more_ref, out_ref, held):
        at = 0
        for part in (far_ref, near_ref, own_ref, more_ref):
            held[at : at + part.shape[0], :] = part[...]
            at += part.shape[0]
        held[at:, :] = jnp.zeros((padded - at, 2 * width), bf16)
        queries = jnp.concatenate([q_ref[...], mq_ref[...]], axis=0)
        row = lax.broadcasted_iota(i32, (total, padded), 0)
        column = lax.broadcasted_iota(i32, (total, padded), 1)
        allowed = (
            (column - WIN <= row) & (column > row) & (column >= WIN - anchor_ref[0])
        )
        lane = lax.broadcasted_iota(i32, (total, HD), 1)
        for pair in range(width // HD):
            span = slice(pair * HD, (pair + 1) * HD)
            keys = held[:, span]
            values = held[:, width + pair * HD : width + (pair + 1) * HD]
            both = queries[:, span]
            done = None
            for side in range(HD // EH):
                mine = (lane >= side * EH) & (lane < (side + 1) * EH)
                query = jnp.where(mine, both, jnp.zeros_like(both))
                scores = lax.dot_general(query, keys, NT, preferred_element_type=f32)
                scores = jnp.where(allowed, scores * (1.0 / math.sqrt(EH)), -1e30)
                largest = jnp.max(scores, axis=-1, keepdims=True)
                raised = jnp.where(allowed, jnp.exp(scores - largest), 0.0)
                weights = (raised / jnp.maximum(jnp.sum(raised, axis=-1, keepdims=True), 1e-30))
                result = jnp.dot(weights.astype(bf16), values, preferred_element_type=f32)
                done = result if done is None else jnp.where(mine, result, done)
            out_ref[:, span] = done.astype(bf16)

    whole = pl.BlockSpec(memory_space=pltpu.VMEM)
    return on_chip(
        kernel,
        blank((total, width)),
        [pltpu.VMEM((padded, 2 * width), bf16)],
        in_specs=[pl.BlockSpec(memory_space=pltpu.SMEM)] + [whole] * 6,
        out_specs=whole,
    )(anchor.reshape(1), own_q, more_q, far, near, own, more)


def encoder_output(states, edge, attended, parts):
    rows, width = states.shape
    count = len(parts)

    def kernel(states_ref, edge_ref, *refs):
        attended_refs, part_refs, out_ref = (refs[:count], refs[count:-1], refs[-1])
        total = jnp.zeros((rows + EDGE, width), f32)
        for piece, part in zip(attended_refs, part_refs):
            total += jnp.dot(piece[...], part[...], preferred_element_type=f32)
        out_ref[:rows, :] = (states_ref[...].astype(f32) + total[:rows]).astype(bf16)
        out_ref[rows:, :] = (edge_ref[...].astype(f32) + total[rows:]).astype(bf16)

    return on_chip(kernel, blank((rows + EDGE, width)))(states, edge, *attended, *parts)


def patch_block(extended, bounds, lift, cross_kv):
    spans = extended.shape[0]
    slots = bounds.shape[0]
    width = lift.shape[1]

    def kernel(extended_ref, bounds_ref, lift_ref, cross_ref, out_ref):
        column = lax.broadcasted_iota(i32, (slots, spans), 1)
        first, after, seen, used = (bounds_ref[:, k : k + 1] for k in range(4))
        rows = extended_ref[...]
        inside = (column >= first) & (column < after)
        allowed = (column >= first) & (column < seen)
        member = jnp.where(inside, 1.0, 0.0).astype(bf16)
        lengths = jnp.maximum(after - first, 1).astype(f32)
        pooled = (jnp.dot(member, rows, preferred_element_type=f32) / lengths).astype(bf16)
        lifted = jnp.dot(pooled, lift_ref[...], preferred_element_type=f32)
        query = lifted.astype(bf16)
        keys = jnp.dot(rows, cross_ref[0], preferred_element_type=f32).astype(bf16)
        values = jnp.dot(rows, cross_ref[1], preferred_element_type=f32).astype(bf16)
        for head in range(width // HD):
            span = slice(head * HD, (head + 1) * HD)
            scores = lax.dot_general(
                query[:, span], keys[:, span], NT, preferred_element_type=f32
            ) * (1.0 / math.sqrt(HD))
            scores = jnp.where(allowed, scores, -1e30)
            largest = jnp.max(scores, axis=-1, keepdims=True)
            raised = jnp.where(allowed, jnp.exp(scores - largest), 0.0)
            weights = (raised / jnp.sum(raised, axis=-1, keepdims=True)).astype(bf16)
            crossed = jnp.dot(weights, values[:, span], preferred_element_type=f32)
            total = jnp.where(used > 0, lifted[:, span] + crossed, 0.0)
            out_ref[:, span] = total.astype(bf16)

    return on_chip(kernel, blank((slots, width)))(extended, bounds, lift, cross_kv)


def placed_rows(pieces):
    rows, width = pieces[0][0].shape
    low, high = (lax.axis_size(ZL), lax.axis_size(ZH))

    def kernel(*refs):
        *parts, out_ref = refs
        here = lax.axis_index(ZH) * low + lax.axis_index(ZL)
        for part, (_, distance, shift) in zip(parts, pieces):
            z = lax.bitwise_and(here + distance, low * high - 1)
            across = lax.bitwise_and(z, low - 1) * rows + shift
            down = lax.shift_right_logical(z, low.bit_length() - 1) * width
            out_ref[
                pl.ds(pl.multiple_of(across, 16), part.shape[0]),
                pl.ds(pl.multiple_of(down, 128), width),
            ] = part[...]

    return on_chip(kernel, blank((low * rows, high * width)))(*(part for part, *_ in pieces))


def placed_weights(pieces, depth):
    along, _, _, wide = pieces[0][0].shape
    count = lax.axis_size(RY)

    def kernel(*refs):
        *parts, out_ref = refs
        by_x, by_y, core = (lax.axis_index(name) for name in (RX, RY, CO))
        for part, (_, distance, shift) in zip(parts, pieces):
            y = lax.bitwise_and(by_y + distance, count - 1)
            for j in range(part.shape[0]):
                x = lax.bitwise_and(by_x + shift + j, along - 1)
                start = pl.multiple_of((x * count + y) * depth, depth)
                for side in range(2):
                    for high in range(2):
                        t = 2 * high + lax.bitwise_xor(core, side)
                        out_ref[side, high, pl.ds(start, depth), :] = part[j, t, :depth, :]

    return on_chip(kernel, blank((2, 2, along * count * depth, wide)))(
        *(part for part, *_ in pieces)
    )


def latent_heads(own_rows, other_rows, weights, cosine, sine):
    rows, width = own_rows.shape
    full = 2 * width

    def kernel(own_ref, other_ref, weights_ref, cosine_ref, sine_ref, q_ref, k_ref, v_ref):
        squares = jnp.zeros((rows, 1), f32)
        total = jnp.zeros((rows, 3 * HD), f32)
        half = width // 2
        for side, part in enumerate((own_ref, other_ref)):
            for high in range(2):
                values = part[:, high * half : (high + 1) * half]
                wide = values.astype(f32)
                squares += jnp.sum(wide * wide, axis=1, keepdims=True)
                total += jnp.dot(values, weights_ref[side, high], preferred_element_type=f32)
        total = total * lax.rsqrt(squares / full + epsilon)
        for which, out_ref in enumerate((q_ref, k_ref)):
            value = total[:, which * HD : (which + 1) * HD]
            turned = value * cosine_ref[...] + pltpu.roll(value, HD // 2, 1) * sine_ref[...]
            out_ref[...] = turned.astype(bf16)
        v_ref[...] = total[:, 2 * HD :].astype(bf16)

    return on_chip(kernel, [blank((rows, HD))] * 3)(
        own_rows, other_rows, weights, cosine, sine
    )


def latent_attention(queries, keys, values, position, key_pos):
    rows = queries.shape[0]
    n_x, n_y = (len(keys), len(values))

    def kernel(*refs):
        q_ref, pos_ref, key_pos_ref = refs[:3]
        key_refs, value_refs = (refs[3 : 3 + n_x], refs[3 + n_x : 3 + n_x + n_y])
        out_ref, held = refs[3 + n_x + n_y :]
        query = q_ref[...]
        position = pos_ref[...]
        top = jnp.full((rows, rows), -1e30, f32)
        for x in range(n_x):
            for y in range(n_y):
                scores = lax.dot_general(
                    query, key_refs[x][y], NT, preferred_element_type=f32
                ) * (1.0 / math.sqrt(HD))
                allowed = key_pos_ref[x * n_y + y : x * n_y + y + 1, :] <= position
                scores = jnp.where(allowed, scores, -1e30)
                held[x * n_y + y] = scores
                top = jnp.maximum(top, scores)
        largest = jnp.max(top, axis=-1, keepdims=True)
        total = jnp.zeros((rows, rows), f32)
        weighted = jnp.zeros((rows, HD), f32)
        for x in range(n_x):
            for y in range(n_y):
                raised = jnp.exp(held[x * n_y + y] - largest)
                total += raised
                weighted += jnp.dot(
                    raised.astype(bf16), value_refs[y][x], preferred_element_type=f32
                )
        out_ref[...] = (weighted / jnp.sum(total, axis=-1, keepdims=True)).astype(bf16)

    return on_chip(
        kernel, blank((rows, HD)), [pltpu.VMEM((n_x * n_y, rows, rows), f32)]
    )(queries, position, key_pos, *keys, *values)


def latent_output(heads, out_part, patches, counts):
    groups, tensor, cut, deep = out_part.shape
    slots, width = patches.shape
    columns = lax.axis_size(ZL)
    joined = 4

    def kernel(count_ref, heads_ref, part_ref, patches_ref, out_ref):
        total = jnp.zeros((slots, joined * cut), f32)
        for t in range(tensor):
            head = jnp.concatenate(
                [heads_ref[zl * tensor + t] for zl in range(columns)], axis=1
            )
            part = part_ref[:, t].reshape(joined * cut, deep)
            total += lax.dot_general(head, part, NT, preferred_element_type=f32)
        used = lax.broadcasted_iota(i32, (slots, joined * cut), 0) < count_ref[0]
        latent = jnp.where(used, patches_ref[...].astype(f32) + total, 0.0)
        out_ref[...] = latent.astype(bf16)

    across = pl.BlockSpec((slots, joined * cut), lambda g: (0, g))
    return on_chip(
        kernel,
        blank((slots, width)),
        grid=(groups // joined,),
        in_specs=[
            pl.BlockSpec(memory_space=pltpu.SMEM),
            pl.BlockSpec(heads.shape, lambda g: (0, 0, 0)),
            pl.BlockSpec((joined, tensor, cut, deep), lambda g: (g, 0, 0, 0)),
            across,
        ],
        out_specs=across,
    )(counts, heads, out_part, patches)


def gathered_counts(pieces, depth):
    own, last, first, far, far_too = (part[:, :, depth, 0] for part, *_ in pieces)
    return jnp.stack([own, first, jnp.concatenate([far, far_too]), last], axis=1).astype(i32)


def shards(
    byte_states,
    enc_gain,
    enc_qkv,
    enc_proj_out,
    starts,
    counts,
    lift,
    cross_kv,
    latent_gain,
    lat_qkv,
    lat_proj_out,
):
    byte_rows, byte_width = byte_states.shape
    slots = starts.shape[1]
    columns = lax.axis_size(ZL)
    tensor = lax.axis_size(TP)
    groups = lax.axis_size(ROWS)
    block = lax.axis_index(SEQ)
    anchor = block * byte_rows
    local_starts = starts[0]
    patch_count = counts[0]
    slot_ids = jnp.arange(slots, dtype=i32)
    in_use = slot_ids < patch_count

    own_q, own_kv = encoder_heads(byte_states, enc_gain, enc_qkv)
    far_kv = shifted(own_kv, SEQ, 2)
    near_kv = shifted(own_kv, SEQ, 1)

    first_local = (local_starts[0] - anchor).astype(bf16)
    edge = jnp.concatenate(
        [
            byte_states[:SPILL],
            jnp.broadcast_to(first_local, (EDGE - SPILL, byte_width)),
        ],
        axis=0,
    )
    edge = shifted(edge, SEQ, -1)
    next_first = edge[SPILL, 0].astype(i32)

    share, depth, inner = lat_qkv.shape
    own_kv, lat_qkv, enc_proj_out = lax.optimization_barrier((own_kv, lat_qkv, enc_proj_out))
    own_gain = lax.dynamic_slice_in_dim(latent_gain, block * depth, depth).astype(f32)
    scaled = (lat_qkv.astype(f32) * own_gain[:, None]).astype(bf16)
    mark = jnp.broadcast_to(counts.astype(bf16), (EDGE, share * HD))
    by_head = jnp.stack(
        [
            jnp.concatenate(
                [
                    jnp.concatenate(
                        [scaled[i, :, k * HD : (k + 1) * HD] for i in range(share)], axis=1
                    ),
                    mark,
                ],
                axis=0,
            )
            for k in range(columns)
        ]
    )
    by_head = exchanged(by_head, ZL)

    out_high = swapped(enc_proj_out, ZH)
    out_side = swapped(enc_proj_out, CO)

    more_q, more_kv = encoder_heads(edge, enc_gain, enc_qkv)
    more_kv, by_head, out_side = lax.optimization_barrier((more_kv, by_head, out_side))
    attended = encoder_attention(own_q, more_q, far_kv, near_kv, own_kv, more_kv, anchor)
    attended, out_high, lat_proj_out = lax.optimization_barrier(
        (attended, out_high, lat_proj_out)
    )
    out_both = swapped(out_high, CO)
    high, side = (swapped(attended, ZH), swapped(attended, CO))
    both = swapped(high, CO)
    by_head = jnp.stack(around_ring(by_head, RX))
    out_part = gathered(lat_proj_out.T, TP)
    side, both, by_head, out_part = lax.optimization_barrier((side, both, by_head, out_part))
    by_head = near_ring(by_head, RY)
    turned = [
        (a * tensor + b, b * tensor + a) for a in range(columns) for b in range(tensor)
    ]
    out_part = lax.ppermute(out_part, COLUMN, turned)
    extended = encoder_output(
        byte_states,
        edge,
        (attended, high, side, both),
        (enc_proj_out, out_high, out_side, out_both),
    )
    encoded = extended[:byte_rows]

    following = jnp.concatenate([local_starts[1:], jnp.zeros((1,), i32)])
    patch_end = jnp.where(slot_ids + 1 < patch_count, following, anchor + byte_rows + next_first)
    first, after = (jnp.where(in_use, end - anchor, 0) for end in (local_starts, patch_end))
    used = in_use.astype(i32)
    bounds = jnp.stack([first, after, jnp.where(in_use, after, 1), used], axis=1)
    patches = patch_block(extended, bounds, lift, cross_kv)
    patches, out_part = lax.optimization_barrier((patches, out_part))
    out_part = gathered(out_part, ROWS)

    all_counts = gathered_counts(by_head, depth)
    grid = (*(lax.axis_size(name) for name in ROWS), columns)
    here = tuple(lax.axis_index(name) for name in ROWS)
    order = sum(
        stride
        * lax.bitwise_and(lax.broadcasted_iota(i32, grid, dim) + start, grid[dim] - 1)
        for dim, stride, start in ((0, grid[1], here[0]), (1, 1, here[1]), (2, groups, 0))
    ).reshape(-1)
    flat_counts = all_counts.reshape(-1)
    offsets = jnp.sum(jnp.where(order[None, :] < order[:, None], flat_counts[None, :], 0), axis=1)
    position = (offsets[:columns, None] + slot_ids[None, :]).reshape(-1)
    key_pos = jnp.where(
        slot_ids[None, :] < flat_counts[:, None], offsets[:, None] + slot_ids[None, :], far_position
    ).reshape(groups, columns * slots)
    halfway = HD // 2
    frequency = jnp.power(rope_base, -2.0 * jnp.arange(halfway, dtype=f32) / HD)
    angles = position.astype(f32)[:, None] * frequency[None, :]
    cosine, sine = (jnp.cos(angles), jnp.sin(angles))
    cosine = jnp.concatenate([cosine, cosine], axis=1)
    sine = jnp.concatenate([-sine, sine], axis=1)
    latent_in = placed_weights(by_head, depth)

    own_rows = placed_rows(around_column(patches))
    own_rows, latent_in = lax.optimization_barrier((own_rows, latent_in))
    other_rows = swapped(own_rows, CO)
    queries, keys, values = latent_heads(own_rows, other_rows, latent_in, cosine, sine)
    keys = around_ring(jnp.stack(around_ring(keys, RY)), RX)
    values = around_ring(jnp.stack(around_ring(values, RX)), RY)
    heads = latent_attention(queries, keys, values, position[:, None], key_pos)
    heads, out_part = lax.optimization_barrier((heads, out_part))

    heads = jnp.broadcast_to(
        heads.reshape(columns, 1, slots, HD), (columns, tensor, slots, HD)
    ).reshape(columns * tensor, slots, HD)
    heads = exchanged(heads, COLUMN)
    latent = latent_output(heads, out_part, patches, counts)
    return (encoded, latent)


def solution(mesh):
    finer = Mesh(mesh.devices.reshape(4, 4, 4, 2, 2), (*SEQ, *TP))
    in_specs = (
        P(SEQ, None),
        P(),
        P(None, None, TP),
        P(TP, None),
        P(SEQ, None),
        P(SEQ),
        P(None, TP),
        P(None, None, TP),
        P(),
        P(None, SEQ, TP),
        P(TP, SEQ),
    )
    out_specs = (P(SEQ, None), P(SEQ, TP))
    return jax.shard_map(
        shards, mesh=finer, in_specs=in_specs, out_specs=out_specs, check_vma=False
    )
```

```python
import math

import jax
import jax.numpy as jnp
from jax import lax
from jax.experimental import pallas as pl
from jax.experimental.pallas import tpu as pltpu
from jax.sharding import Mesh
from jax.sharding import PartitionSpec as P

EH = 64
HD = 128
WIN = 512
SPILL = 8
EDGE = 16
ZL, RX, RY, ZH, CO = ("z_lo", "ring_x", "ring_y", "z_hi", "core")
SEQ = (ZL, RX, RY)
TP = (ZH, CO)
ROWS = (RX, RY)
COLUMN = (ZL, ZH, CO)

epsilon = 1e-05
rope_base = 500000.0
far_position = 1 << 30
bf16 = jnp.bfloat16
f32 = jnp.float32
i32 = jnp.int32
NT = (((1,), (1,)), ((), ()))


def shifted(value, axis, steps):
    count = lax.axis_size(axis)
    leading, last = (max(0, -steps), min(count, count - steps))
    return lax.ppermute(value, axis, [(source, source + steps) for source in range(leading, last)])


def exchanged(pieces, axis):
    return lax.all_to_all(pieces, axis, split_axis=0, concat_axis=0, tiled=True)


def swapped(value, axis):
    return lax.ppermute(value, axis, [(0, 1), (1, 0)])


def gathered(value, axis):
    return exchanged(jnp.broadcast_to(value, (lax.axis_size(axis), *value.shape)), axis)


def around_ring(value, axis):
    count = lax.axis_size(axis)
    return [value] + [
        lax.ppermute(value, axis, [((i + k) % count, i) for i in range(count)])
        for k in range(1, count)
    ]


def near_ring(value, axis):
    count = lax.axis_size(axis)

    def moved(part, step):
        return lax.ppermute(part, axis, [(i, (i + step) % count) for i in range(count)])

    up, down = (moved(value, 1), moved(value, -1))
    half = value.shape[0] // 2
    return [
        (value, 0, 0),
        (up, count - 1, 0),
        (down, 1, 0),
        (moved(up[:half], 1), 2, 0),
        (moved(down[half:], -1), 2, half),
    ]


def around_column(value):
    low, high = (lax.axis_size(ZL), lax.axis_size(ZH))
    count = low * high

    def moved(part, step):
        named = lambda z: z % count % low * high + z % count // low
        return lax.ppermute(part, (ZL, ZH), [(named(z), named(z + step)) for z in range(count)])

    pieces = [(value, 0, 0)]
    up = down = value
    for step in range(1, count // 2):
        up, down = (moved(up, 1), moved(down, -1))
        pieces += [(up, count - step, 0), (down, step, 0)]
    half = value.shape[0] // 2
    pieces += [(moved(up[:half], 1), count // 2, 0), (moved(down[half:], -1), count // 2, half)]
    return pieces


def on_chip(kernel, outs, scratch=(), limit=48, **extra):
    return pl.pallas_call(
        kernel,
        out_shape=outs,
        scratch_shapes=list(scratch),
        compiler_params=pltpu.CompilerParams(vmem_limit_bytes=limit << 20),
        cost_estimate=pl.CostEstimate(flops=1 << 20, transcendentals=0, bytes_accessed=1 << 20),
        **extra,
    )


def blank(shape, dtype=bf16):
    return jax.ShapeDtypeStruct(shape, dtype)


def encoder_heads(states, gain, weights):
    rows, width = states.shape
    share, _, inner = weights.shape

    def kernel(states_ref, gain_ref, weights_ref, query_ref, keys_values_ref):
        values = states_ref[...].astype(f32)
        factor = lax.rsqrt(jnp.mean(values * values, axis=-1, keepdims=True) + epsilon)
        normed = (values * factor * gain_ref[...].astype(f32)).astype(bf16)
        for i in range(1, share):
            keys_values_ref[:, (i - 1) * inner : i * inner] = jnp.dot(
                normed, weights_ref[i], preferred_element_type=f32
            ).astype(bf16)
        query_ref[...] = jnp.dot(normed, weights_ref[0], preferred_element_type=f32).astype(bf16)

    return on_chip(kernel, [blank((rows, inner)), blank((rows, (share - 1) * inner))])(
        states, gain.reshape(1, width), weights
    )


def encoder_attention(own_q, more_q, far, near, own, more, anchor):
    rows, width = own_q.shape
    total = rows + EDGE
    spans = WIN + total
    padded = -(-spans // 128) * 128

    def kernel(anchor_ref, q_ref, mq_ref, far_ref, near_ref, own_ref, more_ref, out_ref, held):
        at = 0
        for part in (far_ref, near_ref, own_ref, more_ref):
            held[at : at + part.shape[0], :] = part[...]
            at += part.shape[0]
        held[at:, :] = jnp.zeros((padded - at, 2 * width), bf16)
        queries = jnp.concatenate([q_ref[...], mq_ref[...]], axis=0)
        row = lax.broadcasted_iota(i32, (total, padded), 0)
        column = lax.broadcasted_iota(i32, (total, padded), 1)
        allowed = (
            (column - WIN <= row) & (column > row) & (column >= WIN - anchor_ref[0])
        )
        lane = lax.broadcasted_iota(i32, (total, HD), 1)
        for pair in range(width // HD):
            span = slice(pair * HD, (pair + 1) * HD)
            keys = held[:, span]
            values = held[:, width + pair * HD : width + (pair + 1) * HD]
            both = queries[:, span]
            done = None
            for side in range(HD // EH):
                mine = (lane >= side * EH) & (lane < (side + 1) * EH)
                query = jnp.where(mine, both, jnp.zeros_like(both))
                scores = lax.dot_general(query, keys, NT, preferred_element_type=f32)
                scores = jnp.where(allowed, scores * (1.0 / math.sqrt(EH)), -1e30)
                largest = jnp.max(scores, axis=-1, keepdims=True)
                raised = jnp.where(allowed, jnp.exp(scores - largest), 0.0)
                weights = (raised / jnp.maximum(jnp.sum(raised, axis=-1, keepdims=True), 1e-30))
                result = jnp.dot(weights.astype(bf16), values, preferred_element_type=f32)
                done = result if done is None else jnp.where(mine, result, done)
            out_ref[:, span] = done.astype(bf16)

    whole = pl.BlockSpec(memory_space=pltpu.VMEM)
    return on_chip(
        kernel,
        blank((total, width)),
        [pltpu.VMEM((padded, 2 * width), bf16)],
        in_specs=[pl.BlockSpec(memory_space=pltpu.SMEM)] + [whole] * 6,
        out_specs=whole,
    )(anchor.reshape(1), own_q, more_q, far, near, own, more)


def encoder_output(states, edge, attended, parts):
    rows, width = states.shape

    def kernel(states_ref, edge_ref, attended_ref, *refs):
        *part_refs, out_ref = refs
        here = lax.axis_index(TP)
        total = jnp.zeros((rows + EDGE, width), f32)
        for (_, turn, start), part in zip(parts, part_refs):
            deep = part.shape[0]
            piece = attended_ref[lax.bitwise_xor(here, turn), :, start : start + deep]
            total += jnp.dot(piece, part[...], preferred_element_type=f32)
        out_ref[:rows, :] = (states_ref[...].astype(f32) + total[:rows]).astype(bf16)
        out_ref[rows:, :] = (edge_ref[...].astype(f32) + total[rows:]).astype(bf16)

    return on_chip(kernel, blank((rows + EDGE, width)))(
        states, edge, attended, *(part for part, *_ in parts)
    )


def patch_block(extended, bounds, lift, cross_kv):
    spans = extended.shape[0]
    slots = bounds.shape[0]
    width = lift.shape[1]

    def kernel(extended_ref, bounds_ref, lift_ref, cross_ref, out_ref):
        column = lax.broadcasted_iota(i32, (slots, spans), 1)
        first, after, seen, used = (bounds_ref[:, k : k + 1] for k in range(4))
        rows = extended_ref[...]
        inside = (column >= first) & (column < after)
        allowed = (column >= first) & (column < seen)
        member = jnp.where(inside, 1.0, 0.0).astype(bf16)
        lengths = jnp.maximum(after - first, 1).astype(f32)
        pooled = (jnp.dot(member, rows, preferred_element_type=f32) / lengths).astype(bf16)
        lifted = jnp.dot(pooled, lift_ref[...], preferred_element_type=f32)
        query = lifted.astype(bf16)
        keys = jnp.dot(rows, cross_ref[0], preferred_element_type=f32).astype(bf16)
        values = jnp.dot(rows, cross_ref[1], preferred_element_type=f32).astype(bf16)
        for head in range(width // HD):
            span = slice(head * HD, (head + 1) * HD)
            scores = lax.dot_general(
                query[:, span], keys[:, span], NT, preferred_element_type=f32
            ) * (1.0 / math.sqrt(HD))
            scores = jnp.where(allowed, scores, -1e30)
            largest = jnp.max(scores, axis=-1, keepdims=True)
            raised = jnp.where(allowed, jnp.exp(scores - largest), 0.0)
            weights = (raised / jnp.sum(raised, axis=-1, keepdims=True)).astype(bf16)
            crossed = jnp.dot(weights, values[:, span], preferred_element_type=f32)
            total = jnp.where(used > 0, lifted[:, span] + crossed, 0.0)
            out_ref[:, span] = total.astype(bf16)

    return on_chip(kernel, blank((slots, width)))(extended, bounds, lift, cross_kv)


def placed_rows(pieces):
    rows, width = pieces[0][0].shape
    low, high = (lax.axis_size(ZL), lax.axis_size(ZH))

    def kernel(*refs):
        *parts, out_ref = refs
        here = lax.axis_index(ZH) * low + lax.axis_index(ZL)
        for part, (_, distance, shift) in zip(parts, pieces):
            z = lax.bitwise_and(here + distance, low * high - 1)
            across = lax.bitwise_and(z, low - 1) * rows + shift
            down = lax.shift_right_logical(z, low.bit_length() - 1) * width
            out_ref[
                pl.ds(pl.multiple_of(across, 16), part.shape[0]),
                pl.ds(pl.multiple_of(down, 128), width),
            ] = part[...]

    return on_chip(kernel, blank((low * rows, high * width)))(*(part for part, *_ in pieces))


def placed_weights(gathered_weights, first, columns, share, depth, step):
    groups = gathered_weights.shape[0]

    def kernel(weights_ref, out_ref):
        core = lax.axis_index(CO)
        for g in range(groups):
            for side in range(2):
                for high in range(columns // 2):
                    t = 2 * high + lax.bitwise_xor(core, side)
                    for i in range(share):
                        start = pl.multiple_of(first + t * step + i * depth, 16)
                        out_ref[
                            side, high, g * depth : (g + 1) * depth, i * HD : (i + 1) * HD
                        ] = weights_ref[g, pl.ds(start, depth), :]

    return on_chip(kernel, blank((2, columns // 2, groups * depth, share * HD)))(
        gathered_weights
    )


def latent_heads(own_rows, other_rows, weights, cosine, sine):
    rows, width = own_rows.shape
    full = 2 * width

    def kernel(own_ref, other_ref, weights_ref, cosine_ref, sine_ref, q_ref, k_ref, v_ref):
        squares = jnp.zeros((rows, 1), f32)
        total = jnp.zeros((rows, 3 * HD), f32)
        half = width // 2
        for side, part in enumerate((own_ref, other_ref)):
            for high in range(2):
                values = part[:, high * half : (high + 1) * half]
                wide = values.astype(f32)
                squares += jnp.sum(wide * wide, axis=1, keepdims=True)
                total += jnp.dot(values, weights_ref[side, high], preferred_element_type=f32)
        total = total * lax.rsqrt(squares / full + epsilon)
        for which, out_ref in enumerate((q_ref, k_ref)):
            value = total[:, which * HD : (which + 1) * HD]
            turned = value * cosine_ref[...] + pltpu.roll(value, HD // 2, 1) * sine_ref[...]
            out_ref[...] = turned.astype(bf16)
        v_ref[...] = total[:, 2 * HD :].astype(bf16)

    return on_chip(kernel, [blank((rows, HD))] * 3)(
        own_rows, other_rows, weights, cosine, sine
    )


def latent_attention(queries, keys, values, position, key_pos):
    rows = queries.shape[0]
    n_x, n_y = (len(keys), len(values))

    def kernel(*refs):
        q_ref, pos_ref, key_pos_ref = refs[:3]
        key_refs, value_refs = (refs[3 : 3 + n_x], refs[3 + n_x : 3 + n_x + n_y])
        out_ref, held = refs[3 + n_x + n_y :]
        query = q_ref[...]
        position = pos_ref[...]
        top = jnp.full((rows, rows), -1e30, f32)
        for x in range(n_x):
            for y in range(n_y):
                scores = lax.dot_general(
                    query, key_refs[x][y], NT, preferred_element_type=f32
                ) * (1.0 / math.sqrt(HD))
                allowed = key_pos_ref[x * n_y + y : x * n_y + y + 1, :] <= position
                scores = jnp.where(allowed, scores, -1e30)
                held[x * n_y + y] = scores
                top = jnp.maximum(top, scores)
        largest = jnp.max(top, axis=-1, keepdims=True)
        total = jnp.zeros((rows, rows), f32)
        weighted = jnp.zeros((rows, HD), f32)
        for x in range(n_x):
            for y in range(n_y):
                raised = jnp.exp(held[x * n_y + y] - largest)
                total += raised
                weighted += jnp.dot(
                    raised.astype(bf16), value_refs[y][x], preferred_element_type=f32
                )
        out_ref[...] = (weighted / jnp.sum(total, axis=-1, keepdims=True)).astype(bf16)

    return on_chip(
        kernel, blank((rows, HD)), [pltpu.VMEM((n_x * n_y, rows, rows), f32)]
    )(queries, position, key_pos, *keys, *values)


def partial_outputs(heads, weights):
    columns, rows, _ = heads.shape
    groups = weights.shape[0]
    slots = rows // columns
    cut = slots

    def kernel(heads_ref, weights_ref, *out_refs):
        here = lax.axis_index(TP)
        flat = [
            weights_ref[:, zl * cut : (zl + 1) * cut, :].reshape(groups * cut, HD)
            for zl in range(columns)
        ]
        for k, out_ref in enumerate(out_refs):
            start = lax.bitwise_and(here + k, columns - 1) * slots
            span = pl.ds(pl.multiple_of(start, slots), slots)
            total = jnp.zeros((slots, groups * cut), f32)
            for zl in range(columns):
                total += lax.dot_general(
                    heads_ref[zl, span, :], flat[zl], NT, preferred_element_type=f32
                )
            out_ref[...] = total.astype(bf16)

    block = (groups, columns * cut, HD)
    return on_chip(
        kernel,
        [blank((slots, groups * cut))] * columns,
        grid=(1,),
        in_specs=[
            pl.BlockSpec(heads.shape, lambda i: (0, 0, 0)),
            pl.BlockSpec(block, lambda i: (0, 0, 0)),
        ],
        out_specs=[pl.BlockSpec((slots, groups * cut), lambda i: (0, 0))] * columns,
    )(heads, weights)


def summed_outputs(pieces, patches, counts):
    def kernel(count_ref, patches_ref, *refs):
        *piece_refs, out_ref = refs
        total = patches_ref[...].astype(f32)
        for piece in piece_refs:
            total += piece[...].astype(f32)
        used = lax.broadcasted_iota(i32, total.shape, 0) < count_ref[0]
        out_ref[...] = jnp.where(used, total, 0.0).astype(bf16)

    whole = pl.BlockSpec(memory_space=pltpu.VMEM)
    return on_chip(
        kernel,
        blank(patches.shape),
        in_specs=[pl.BlockSpec(memory_space=pltpu.SMEM)] + [whole] * (1 + len(pieces)),
        out_specs=whole,
    )(counts, patches, *pieces)


def shards(
    byte_states,
    enc_gain,
    enc_qkv,
    enc_proj_out,
    starts,
    counts,
    lift,
    cross_kv,
    latent_gain,
    lat_qkv,
    lat_proj_out,
):
    byte_rows, byte_width = byte_states.shape
    slots = starts.shape[1]
    columns = lax.axis_size(ZL)
    tensor = lax.axis_size(TP)
    groups = lax.axis_size(ROWS)
    block = lax.axis_index(SEQ)
    anchor = block * byte_rows
    local_starts = starts[0]
    patch_count = counts[0]
    slot_ids = jnp.arange(slots, dtype=i32)
    in_use = slot_ids < patch_count

    own_q, own_kv = encoder_heads(byte_states, enc_gain, enc_qkv)
    far_kv = shifted(own_kv, SEQ, 2)
    near_kv = shifted(own_kv, SEQ, 1)

    first_local = (local_starts[0] - anchor).astype(bf16)
    edge = jnp.concatenate(
        [
            byte_states[:SPILL],
            jnp.broadcast_to(first_local, (EDGE - SPILL, byte_width)),
        ],
        axis=0,
    )
    edge = shifted(edge, SEQ, -1)

    share, depth, inner = lat_qkv.shape
    own_gain = lax.dynamic_slice_in_dim(latent_gain, block * depth, depth).astype(f32)
    scaled = (lat_qkv.astype(f32) * own_gain[:, None]).astype(bf16).reshape(share * depth, inner)
    mark = jnp.broadcast_to(counts.astype(bf16), (EDGE, HD))
    step = share * depth + EDGE
    by_head = jnp.concatenate(
        [part for k in range(columns) for part in (scaled[:, k * HD : (k + 1) * HD], mark)], axis=0
    ).reshape(columns, step, HD)
    by_head = exchanged(by_head, ZL).reshape(columns * step, HD)
    out_part = lat_proj_out.T
    cut = out_part.shape[0]
    out_part = [out_part[:, k * HD : (k + 1) * HD] for k in range(columns)]
    by_head = jnp.concatenate(out_part + [by_head], axis=0)

    half = enc_proj_out.shape[0] // 2
    high_a, high_b = (swapped(enc_proj_out[at : at + half], ZH) for at in (0, half))
    out_side = swapped(enc_proj_out, CO)

    near_kv, by_head, edge, out_side = lax.optimization_barrier(
        (near_kv, by_head, edge, out_side)
    )
    far_kv, high_a = lax.optimization_barrier((far_kv, high_a))
    by_head = gathered(by_head, ROWS)
    next_first = edge[SPILL, 0].astype(i32)
    more_q, more_kv = encoder_heads(edge, enc_gain, enc_qkv)
    attended = encoder_attention(own_q, more_q, far_kv, near_kv, own_kv, more_kv, anchor)
    both_a = swapped(high_a, CO)
    attended, high_b, both_a = lax.optimization_barrier((attended, high_b, both_a))
    both_b = swapped(high_b, CO)
    attended = lax.all_gather(attended, TP)
    extended = encoder_output(
        byte_states,
        edge,
        attended,
        (
            (enc_proj_out, 0, 0),
            (out_side, 1, 0),
            (high_a, 2, 0),
            (both_a, 3, 0),
            (high_b, 2, half),
            (both_b, 3, half),
        ),
    )
    encoded = extended[:byte_rows]

    following = jnp.concatenate([local_starts[1:], jnp.zeros((1,), i32)])
    patch_end = jnp.where(slot_ids + 1 < patch_count, following, anchor + byte_rows + next_first)
    first, after = (jnp.where(in_use, end - anchor, 0) for end in (local_starts, patch_end))
    used = in_use.astype(i32)
    bounds = jnp.stack([first, after, jnp.where(in_use, after, 1), used], axis=1)
    patches = patch_block(extended, bounds, lift, cross_kv)
    grid = (*(lax.axis_size(name) for name in ROWS), columns)
    here = tuple(lax.axis_index(name) for name in ROWS)
    all_counts = jnp.stack(
        [by_head[:, columns * cut + (k + 1) * step - 1, 0] for k in range(columns)], axis=1
    )
    all_counts = all_counts.astype(i32).reshape(*grid)
    all_counts = lax.dynamic_slice(jnp.tile(all_counts, (2, 2, 1)), (*here, 0), grid)
    order = sum(
        stride
        * lax.bitwise_and(lax.broadcasted_iota(i32, grid, dim) + start, grid[dim] - 1)
        for dim, stride, start in ((0, grid[1], here[0]), (1, 1, here[1]), (2, groups, 0))
    ).reshape(-1)
    flat_counts = all_counts.reshape(-1)
    offsets = jnp.sum(jnp.where(order[None, :] < order[:, None], flat_counts[None, :], 0), axis=1)
    position = (offsets[:columns, None] + slot_ids[None, :]).reshape(-1)
    key_pos = jnp.where(
        slot_ids[None, :] < flat_counts[:, None], offsets[:, None] + slot_ids[None, :], far_position
    ).reshape(groups, columns * slots)
    halfway = HD // 2
    frequency = jnp.power(rope_base, -2.0 * jnp.arange(halfway, dtype=f32) / HD)
    angles = position.astype(f32)[:, None] * frequency[None, :]
    cosine, sine = (jnp.cos(angles), jnp.sin(angles))
    cosine = jnp.concatenate([cosine, cosine], axis=1)
    sine = jnp.concatenate([-sine, sine], axis=1)
    latent_in = placed_weights(by_head, columns * cut, columns, share, depth, step)

    own_rows = placed_rows(around_column(patches))
    own_rows, latent_in = lax.optimization_barrier((own_rows, latent_in))
    other_rows = swapped(own_rows, CO)
    queries, keys, values = latent_heads(own_rows, other_rows, latent_in, cosine, sine)
    keys = around_ring(jnp.stack(around_ring(keys, RY)), RX)
    values = around_ring(jnp.stack(around_ring(values, RX)), RY)
    heads = latent_attention(queries, keys, values, position[:, None], key_pos)

    partial = partial_outputs(lax.all_gather(heads, ZL), by_head)
    partial = [
        lax.ppermute(
            piece,
            COLUMN,
            [
                (a * tensor + b, (b + k) % columns * tensor + a)
                for a in range(columns)
                for b in range(tensor)
            ],
        )
        for k, piece in enumerate(partial)
    ]
    latent = summed_outputs(partial, patches, counts)
    return (encoded, latent)


def solution(mesh):
    finer = Mesh(mesh.devices.reshape(4, 4, 4, 2, 2), (*SEQ, *TP))
    in_specs = (
        P(SEQ, None),
        P(),
        P(None, None, TP),
        P(TP, None),
        P(SEQ, None),
        P(SEQ),
        P(None, TP),
        P(None, None, TP),
        P(),
        P(None, SEQ, TP),
        P(TP, SEQ),
    )
    out_specs = (P(SEQ, None), P(SEQ, TP))
    return jax.shard_map(
        shards, mesh=finer, in_specs=in_specs, out_specs=out_specs, check_vma=False
    )
```

```python
import math

import jax
import jax.numpy as jnp
from jax import lax
from jax.experimental import pallas as pl
from jax.experimental.pallas import tpu as pltpu
from jax.sharding import Mesh
from jax.sharding import PartitionSpec as P

EH = 64
HD = 128
WIN = 512
SPILL = 8
EDGE = 16
ZL, RX, RY, ZH, CO = ("z_lo", "ring_x", "ring_y", "z_hi", "core")
SEQ = (ZL, RX, RY)
TP = (ZH, CO)
ROWS = (RX, RY)
COLUMN = (ZL, ZH, CO)

epsilon = 1e-05
rope_base = 500000.0
far_position = 1 << 30
bf16 = jnp.bfloat16
f32 = jnp.float32
i32 = jnp.int32
NT = (((1,), (1,)), ((), ()))


def shifted(value, axis, steps):
    count = lax.axis_size(axis)
    leading, last = (max(0, -steps), min(count, count - steps))
    return lax.ppermute(value, axis, [(source, source + steps) for source in range(leading, last)])


def exchanged(pieces, axis):
    return lax.all_to_all(pieces, axis, split_axis=0, concat_axis=0, tiled=True)


def swapped(value, axis):
    return lax.ppermute(value, axis, [(0, 1), (1, 0)])


def gathered(value, axis):
    return exchanged(jnp.broadcast_to(value, (lax.axis_size(axis), *value.shape)), axis)


def around_ring(value, axis):
    count = lax.axis_size(axis)
    return [value] + [
        lax.ppermute(value, axis, [((i + k) % count, i) for i in range(count)])
        for k in range(1, count)
    ]


def near_ring(value, axis):
    count = lax.axis_size(axis)

    def moved(part, step):
        return lax.ppermute(part, axis, [(i, (i + step) % count) for i in range(count)])

    up, down = (moved(value, 1), moved(value, -1))
    half = value.shape[0] // 2
    return [
        (value, 0, 0),
        (up, count - 1, 0),
        (down, 1, 0),
        (moved(up[:half], 1), 2, 0),
        (moved(down[half:], -1), 2, half),
    ]


def around_column(value):
    low, high = (lax.axis_size(ZL), lax.axis_size(ZH))
    count = low * high

    def moved(part, step):
        named = lambda z: z % count % low * high + z % count // low
        return lax.ppermute(part, (ZL, ZH), [(named(z), named(z + step)) for z in range(count)])

    pieces = [(value, 0, 0)]
    up = down = value
    for step in range(1, count // 2):
        up, down = (moved(up, 1), moved(down, -1))
        pieces += [(up, count - step, 0), (down, step, 0)]
    half = value.shape[0] // 2
    pieces += [(moved(up[:half], 1), count // 2, 0), (moved(down[half:], -1), count // 2, half)]
    return pieces


def on_chip(kernel, outs, scratch=(), limit=48, **extra):
    return pl.pallas_call(
        kernel,
        out_shape=outs,
        scratch_shapes=list(scratch),
        compiler_params=pltpu.CompilerParams(vmem_limit_bytes=limit << 20),
        cost_estimate=pl.CostEstimate(flops=1 << 20, transcendentals=0, bytes_accessed=1 << 20),
        **extra,
    )


def blank(shape, dtype=bf16):
    return jax.ShapeDtypeStruct(shape, dtype)


def encoder_heads(states, gain, weights):
    rows, width = states.shape
    share, _, inner = weights.shape

    def kernel(states_ref, gain_ref, weights_ref, query_ref, keys_values_ref):
        values = states_ref[...].astype(f32)
        factor = lax.rsqrt(jnp.mean(values * values, axis=-1, keepdims=True) + epsilon)
        normed = (values * factor * gain_ref[...].astype(f32)).astype(bf16)
        for i in range(1, share):
            keys_values_ref[:, (i - 1) * inner : i * inner] = jnp.dot(
                normed, weights_ref[i], preferred_element_type=f32
            ).astype(bf16)
        query_ref[...] = jnp.dot(normed, weights_ref[0], preferred_element_type=f32).astype(bf16)

    return on_chip(kernel, [blank((rows, inner)), blank((rows, (share - 1) * inner))])(
        states, gain.reshape(1, width), weights
    )


def encoder_attention(own_q, more_q, far, near, own, more, anchor):
    rows, width = own_q.shape
    total = rows + EDGE
    spans = WIN + total
    padded = -(-spans // 128) * 128

    def kernel(anchor_ref, q_ref, mq_ref, far_ref, near_ref, own_ref, more_ref, out_ref, held):
        at = 0
        for part in (far_ref, near_ref, own_ref, more_ref):
            held[at : at + part.shape[0], :] = part[...]
            at += part.shape[0]
        held[at:, :] = jnp.zeros((padded - at, 2 * width), bf16)
        queries = jnp.concatenate([q_ref[...], mq_ref[...]], axis=0)
        row = lax.broadcasted_iota(i32, (total, padded), 0)
        column = lax.broadcasted_iota(i32, (total, padded), 1)
        allowed = (
            (column - WIN <= row) & (column > row) & (column >= WIN - anchor_ref[0])
        )
        lane = lax.broadcasted_iota(i32, (total, HD), 1)
        for pair in range(width // HD):
            span = slice(pair * HD, (pair + 1) * HD)
            keys = held[:, span]
            values = held[:, width + pair * HD : width + (pair + 1) * HD]
            both = queries[:, span]
            done = None
            for side in range(HD // EH):
                mine = (lane >= side * EH) & (lane < (side + 1) * EH)
                query = jnp.where(mine, both, jnp.zeros_like(both))
                scores = lax.dot_general(query, keys, NT, preferred_element_type=f32)
                scores = jnp.where(allowed, scores * (1.0 / math.sqrt(EH)), -1e30)
                largest = jnp.max(scores, axis=-1, keepdims=True)
                raised = jnp.where(allowed, jnp.exp(scores - largest), 0.0)
                weights = (raised / jnp.maximum(jnp.sum(raised, axis=-1, keepdims=True), 1e-30))
                result = jnp.dot(weights.astype(bf16), values, preferred_element_type=f32)
                done = result if done is None else jnp.where(mine, result, done)
            out_ref[:, span] = done.astype(bf16)

    whole = pl.BlockSpec(memory_space=pltpu.VMEM)
    return on_chip(
        kernel,
        blank((total, width)),
        [pltpu.VMEM((padded, 2 * width), bf16)],
        in_specs=[pl.BlockSpec(memory_space=pltpu.SMEM)] + [whole] * 6,
        out_specs=whole,
    )(anchor.reshape(1), own_q, more_q, far, near, own, more)


def encoder_output(states, edge, attended, parts):
    rows, width = states.shape

    def kernel(states_ref, edge_ref, attended_ref, *refs):
        *part_refs, out_ref = refs
        here = lax.axis_index(TP)
        total = jnp.zeros((rows + EDGE, width), f32)
        for (_, turn, start), part in zip(parts, part_refs):
            deep = part.shape[0]
            piece = attended_ref[lax.bitwise_xor(here, turn), :, start : start + deep]
            total += jnp.dot(piece, part[...], preferred_element_type=f32)
        out_ref[:rows, :] = (states_ref[...].astype(f32) + total[:rows]).astype(bf16)
        out_ref[rows:, :] = (edge_ref[...].astype(f32) + total[rows:]).astype(bf16)

    return on_chip(kernel, blank((rows + EDGE, width)))(
        states, edge, attended, *(part for part, *_ in parts)
    )


def patch_block(extended, bounds, lift, cross_kv):
    spans = extended.shape[0]
    slots = bounds.shape[0]
    width = lift.shape[1]

    def kernel(extended_ref, bounds_ref, lift_ref, cross_ref, out_ref):
        column = lax.broadcasted_iota(i32, (slots, spans), 1)
        first, after, seen, used = (bounds_ref[:, k : k + 1] for k in range(4))
        rows = extended_ref[...]
        inside = (column >= first) & (column < after)
        allowed = (column >= first) & (column < seen)
        member = jnp.where(inside, 1.0, 0.0).astype(bf16)
        lengths = jnp.maximum(after - first, 1).astype(f32)
        pooled = (jnp.dot(member, rows, preferred_element_type=f32) / lengths).astype(bf16)
        lifted = jnp.dot(pooled, lift_ref[...], preferred_element_type=f32)
        query = lifted.astype(bf16)
        keys = jnp.dot(rows, cross_ref[0], preferred_element_type=f32).astype(bf16)
        values = jnp.dot(rows, cross_ref[1], preferred_element_type=f32).astype(bf16)
        for head in range(width // HD):
            span = slice(head * HD, (head + 1) * HD)
            scores = lax.dot_general(
                query[:, span], keys[:, span], NT, preferred_element_type=f32
            ) * (1.0 / math.sqrt(HD))
            scores = jnp.where(allowed, scores, -1e30)
            largest = jnp.max(scores, axis=-1, keepdims=True)
            raised = jnp.where(allowed, jnp.exp(scores - largest), 0.0)
            weights = (raised / jnp.sum(raised, axis=-1, keepdims=True)).astype(bf16)
            crossed = jnp.dot(weights, values[:, span], preferred_element_type=f32)
            total = jnp.where(used > 0, lifted[:, span] + crossed, 0.0)
            out_ref[:, span] = total.astype(bf16)

    return on_chip(kernel, blank((slots, width)))(extended, bounds, lift, cross_kv)


def placed_rows(pieces):
    rows, width = pieces[0][0].shape
    low, high = (lax.axis_size(ZL), lax.axis_size(ZH))

    def kernel(*refs):
        *parts, out_ref = refs
        here = lax.axis_index(ZH) * low + lax.axis_index(ZL)
        for part, (_, distance, shift) in zip(parts, pieces):
            z = lax.bitwise_and(here + distance, low * high - 1)
            across = lax.bitwise_and(z, low - 1) * rows + shift
            down = lax.shift_right_logical(z, low.bit_length() - 1) * width
            out_ref[
                pl.ds(pl.multiple_of(across, 16), part.shape[0]),
                pl.ds(pl.multiple_of(down, 128), width),
            ] = part[...]

    return on_chip(kernel, blank((low * rows, high * width)))(*(part for part, *_ in pieces))


def head_weights(lat_qkv, gains, counts):
    share, depth, inner = lat_qkv.shape
    step = share * depth + EDGE
    heads = inner // HD

    def kernel(count_ref, weights_ref, gains_ref, out_ref):
        block = lax.axis_index(SEQ)
        gains = gains_ref[...].astype(f32)
        mine = lax.broadcasted_iota(i32, gains.shape, 0) == block
        row = jnp.sum(jnp.where(mine, gains, 0.0), axis=0, keepdims=True)
        square = (depth, depth)
        same = lax.broadcasted_iota(i32, square, 0) == lax.broadcasted_iota(i32, square, 1)
        column = jnp.sum(jnp.where(same, row, 0.0), axis=1, keepdims=True)
        mark = jnp.full((EDGE, HD), count_ref[0].astype(f32)).astype(bf16)
        for i in range(share):
            scaled = (weights_ref[i].astype(f32) * column).astype(bf16)
            for k in range(heads):
                out_ref[k, i * depth : (i + 1) * depth, :] = scaled[:, k * HD : (k + 1) * HD]
        for k in range(heads):
            out_ref[k, share * depth :, :] = mark

    whole = pl.BlockSpec(memory_space=pltpu.VMEM)
    return on_chip(
        kernel,
        blank((heads, step, HD)),
        in_specs=[pl.BlockSpec(memory_space=pltpu.SMEM), whole, whole],
        out_specs=whole,
    )(counts, lat_qkv, gains)


def copied_weights(out_part, by_head, copies):
    cut, deep = out_part.shape
    heads, step, _ = by_head.shape
    total = heads * (cut + step)

    def kernel(out_part_ref, by_head_ref, out_ref):
        for k in range(heads):
            out_ref[0, k * cut : (k + 1) * cut, :] = out_part_ref[:, k * HD : (k + 1) * HD]
            start = heads * cut + k * step
            out_ref[0, start : start + step, :] = by_head_ref[k]

    return on_chip(
        kernel,
        blank((copies, total, HD)),
        grid=(copies,),
        in_specs=[
            pl.BlockSpec(out_part.shape, lambda i: (0, 0)),
            pl.BlockSpec(by_head.shape, lambda i: (0, 0, 0)),
        ],
        out_specs=pl.BlockSpec((1, total, HD), lambda i: (i, 0, 0)),
    )(out_part, by_head)


def placed_weights(gathered_weights, first, columns, share, depth, step):
    groups = gathered_weights.shape[0]

    def kernel(weights_ref, out_ref):
        core = lax.axis_index(CO)
        for g in range(groups):
            for side in range(2):
                for high in range(columns // 2):
                    t = 2 * high + lax.bitwise_xor(core, side)
                    for i in range(share):
                        start = pl.multiple_of(first + t * step + i * depth, 16)
                        out_ref[
                            side, high, g * depth : (g + 1) * depth, i * HD : (i + 1) * HD
                        ] = weights_ref[g, pl.ds(start, depth), :]

    return on_chip(kernel, blank((2, columns // 2, groups * depth, share * HD)))(
        gathered_weights
    )


def latent_heads(own_rows, other_rows, weights, cosine, sine):
    rows, width = own_rows.shape
    full = 2 * width

    def kernel(own_ref, other_ref, weights_ref, cosine_ref, sine_ref, q_ref, k_ref, v_ref):
        squares = jnp.zeros((rows, 1), f32)
        total = jnp.zeros((rows, 3 * HD), f32)
        half = width // 2
        for side, part in enumerate((own_ref, other_ref)):
            for high in range(2):
                values = part[:, high * half : (high + 1) * half]
                wide = values.astype(f32)
                squares += jnp.sum(wide * wide, axis=1, keepdims=True)
                total += jnp.dot(values, weights_ref[side, high], preferred_element_type=f32)
        total = total * lax.rsqrt(squares / full + epsilon)
        for which, out_ref in enumerate((q_ref, k_ref)):
            value = total[:, which * HD : (which + 1) * HD]
            turned = value * cosine_ref[...] + pltpu.roll(value, HD // 2, 1) * sine_ref[...]
            out_ref[...] = turned.astype(bf16)
        v_ref[...] = total[:, 2 * HD :].astype(bf16)

    return on_chip(kernel, [blank((rows, HD))] * 3)(
        own_rows, other_rows, weights, cosine, sine
    )


def latent_attention(queries, keys, values, position, key_pos):
    rows = queries.shape[0]
    n_x, n_y = (len(keys), len(values))

    def kernel(*refs):
        q_ref, pos_ref, key_pos_ref = refs[:3]
        key_refs, value_refs = (refs[3 : 3 + n_x], refs[3 + n_x : 3 + n_x + n_y])
        out_ref, held = refs[3 + n_x + n_y :]
        query = q_ref[...]
        position = pos_ref[...]
        top = jnp.full((rows, rows), -1e30, f32)
        for x in range(n_x):
            for y in range(n_y):
                scores = lax.dot_general(
                    query, key_refs[x][y], NT, preferred_element_type=f32
                ) * (1.0 / math.sqrt(HD))
                allowed = key_pos_ref[x * n_y + y : x * n_y + y + 1, :] <= position
                scores = jnp.where(allowed, scores, -1e30)
                held[x * n_y + y] = scores
                top = jnp.maximum(top, scores)
        largest = jnp.max(top, axis=-1, keepdims=True)
        total = jnp.zeros((rows, rows), f32)
        weighted = jnp.zeros((rows, HD), f32)
        for x in range(n_x):
            for y in range(n_y):
                raised = jnp.exp(held[x * n_y + y] - largest)
                total += raised
                weighted += jnp.dot(
                    raised.astype(bf16), value_refs[y][x], preferred_element_type=f32
                )
        out_ref[...] = (weighted / jnp.sum(total, axis=-1, keepdims=True)).astype(bf16)

    return on_chip(
        kernel, blank((rows, HD)), [pltpu.VMEM((n_x * n_y, rows, rows), f32)]
    )(queries, position, key_pos, *keys, *values)


def partial_outputs(heads, weights):
    columns, rows, _ = heads.shape
    groups = weights.shape[0]
    slots = rows // columns
    cut = slots

    def kernel(heads_ref, weights_ref, *out_refs):
        here = lax.axis_index(TP)
        flat = [
            weights_ref[:, zl * cut : (zl + 1) * cut, :].reshape(groups * cut, HD)
            for zl in range(columns)
        ]
        for k, out_ref in enumerate(out_refs):
            start = lax.bitwise_and(here + k, columns - 1) * slots
            span = pl.ds(pl.multiple_of(start, slots), slots)
            total = jnp.zeros((slots, groups * cut), f32)
            for zl in range(columns):
                total += lax.dot_general(
                    heads_ref[zl, span, :], flat[zl], NT, preferred_element_type=f32
                )
            out_ref[...] = total.astype(bf16)

    block = (groups, columns * cut, HD)
    return on_chip(
        kernel,
        [blank((slots, groups * cut))] * columns,
        grid=(1,),
        in_specs=[
            pl.BlockSpec(heads.shape, lambda i: (0, 0, 0)),
            pl.BlockSpec(block, lambda i: (0, 0, 0)),
        ],
        out_specs=[pl.BlockSpec((slots, groups * cut), lambda i: (0, 0))] * columns,
    )(heads, weights)


def summed_outputs(pieces, patches, counts):
    def kernel(count_ref, patches_ref, *refs):
        *piece_refs, out_ref = refs
        total = patches_ref[...].astype(f32)
        for piece in piece_refs:
            total += piece[...].astype(f32)
        used = lax.broadcasted_iota(i32, total.shape, 0) < count_ref[0]
        out_ref[...] = jnp.where(used, total, 0.0).astype(bf16)

    whole = pl.BlockSpec(memory_space=pltpu.VMEM)
    return on_chip(
        kernel,
        blank(patches.shape),
        in_specs=[pl.BlockSpec(memory_space=pltpu.SMEM)] + [whole] * (1 + len(pieces)),
        out_specs=whole,
    )(counts, patches, *pieces)


def shards(
    byte_states,
    enc_gain,
    enc_qkv,
    enc_proj_out,
    starts,
    counts,
    lift,
    cross_kv,
    latent_gain,
    lat_qkv,
    lat_proj_out,
):
    byte_rows, byte_width = byte_states.shape
    slots = starts.shape[1]
    columns = lax.axis_size(ZL)
    tensor = lax.axis_size(TP)
    groups = lax.axis_size(ROWS)
    block = lax.axis_index(SEQ)
    anchor = block * byte_rows
    local_starts = starts[0]
    patch_count = counts[0]
    slot_ids = jnp.arange(slots, dtype=i32)
    in_use = slot_ids < patch_count

    own_q, own_kv = encoder_heads(byte_states, enc_gain, enc_qkv)
    near_kv = shifted(own_kv, SEQ, 1)
    far_kv = shifted(near_kv, SEQ, 1)

    first_local = (local_starts[0] - anchor).astype(bf16)
    edge = jnp.concatenate(
        [
            byte_states[:SPILL],
            jnp.broadcast_to(first_local, (EDGE - SPILL, byte_width)),
        ],
        axis=0,
    )
    edge = shifted(edge, SEQ, -1)

    share, depth, inner = lat_qkv.shape
    step = share * depth + EDGE
    by_head = head_weights(lat_qkv, latent_gain.reshape(-1, depth), counts)
    by_head = exchanged(by_head, ZL)
    cut = lat_proj_out.shape[1]

    half = enc_proj_out.shape[0] // 2
    high_a, high_b = (swapped(enc_proj_out[at : at + half], ZH) for at in (0, half))
    out_side = swapped(enc_proj_out, CO)

    near_kv, far_kv, by_head, edge, out_side, high_a = lax.optimization_barrier(
        (near_kv, far_kv, by_head, edge, out_side, high_a)
    )
    by_head = exchanged(copied_weights(lat_proj_out.T, by_head, groups), ROWS)
    next_first = edge[SPILL, 0].astype(i32)
    more_q, more_kv = encoder_heads(edge, enc_gain, enc_qkv)
    attended = encoder_attention(own_q, more_q, far_kv, near_kv, own_kv, more_kv, anchor)
    both_a = swapped(high_a, CO)
    attended, high_b, both_a = lax.optimization_barrier((attended, high_b, both_a))
    both_b = swapped(high_b, CO)
    attended = lax.all_gather(attended, TP)
    extended = encoder_output(
        byte_states,
        edge,
        attended,
        (
            (enc_proj_out, 0, 0),
            (out_side, 1, 0),
            (high_a, 2, 0),
            (both_a, 3, 0),
            (high_b, 2, half),
            (both_b, 3, half),
        ),
    )
    encoded = extended[:byte_rows]

    following = jnp.concatenate([local_starts[1:], jnp.zeros((1,), i32)])
    patch_end = jnp.where(slot_ids + 1 < patch_count, following, anchor + byte_rows + next_first)
    first, after = (jnp.where(in_use, end - anchor, 0) for end in (local_starts, patch_end))
    used = in_use.astype(i32)
    bounds = jnp.stack([first, after, jnp.where(in_use, after, 1), used], axis=1)
    patches = patch_block(extended, bounds, lift, cross_kv)
    grid = (*(lax.axis_size(name) for name in ROWS), columns)
    here = tuple(lax.axis_index(name) for name in ROWS)
    all_counts = jnp.stack(
        [by_head[:, columns * cut + (k + 1) * step - 1, 0] for k in range(columns)], axis=1
    )
    all_counts = all_counts.astype(i32).reshape(*grid)
    all_counts = lax.dynamic_slice(jnp.tile(all_counts, (2, 2, 1)), (*here, 0), grid)
    order = sum(
        stride
        * lax.bitwise_and(lax.broadcasted_iota(i32, grid, dim) + start, grid[dim] - 1)
        for dim, stride, start in ((0, grid[1], here[0]), (1, 1, here[1]), (2, groups, 0))
    ).reshape(-1)
    flat_counts = all_counts.reshape(-1)
    offsets = jnp.sum(jnp.where(order[None, :] < order[:, None], flat_counts[None, :], 0), axis=1)
    position = (offsets[:columns, None] + slot_ids[None, :]).reshape(-1)
    key_pos = jnp.where(
        slot_ids[None, :] < flat_counts[:, None], offsets[:, None] + slot_ids[None, :], far_position
    ).reshape(groups, columns * slots)
    halfway = HD // 2
    frequency = jnp.power(rope_base, -2.0 * jnp.arange(halfway, dtype=f32) / HD)
    angles = position.astype(f32)[:, None] * frequency[None, :]
    cosine, sine = (jnp.cos(angles), jnp.sin(angles))
    cosine = jnp.concatenate([cosine, cosine], axis=1)
    sine = jnp.concatenate([-sine, sine], axis=1)
    latent_in = placed_weights(by_head, columns * cut, columns, share, depth, step)

    own_rows = placed_rows(around_column(patches))
    own_rows, latent_in = lax.optimization_barrier((own_rows, latent_in))
    other_rows = swapped(own_rows, CO)
    queries, keys, values = latent_heads(own_rows, other_rows, latent_in, cosine, sine)
    keys = around_ring(jnp.stack(around_ring(keys, RY)), RX)
    values = around_ring(jnp.stack(around_ring(values, RX)), RY)
    heads = latent_attention(queries, keys, values, position[:, None], key_pos)

    partial = partial_outputs(lax.all_gather(heads, ZL), by_head)
    partial = [
        lax.ppermute(
            piece,
            COLUMN,
            [
                (a * tensor + b, (b + k) % columns * tensor + a)
                for a in range(columns)
                for b in range(tensor)
            ],
        )
        for k, piece in enumerate(partial)
    ]
    latent = summed_outputs(partial, patches, counts)
    return (encoded, latent)


def solution(mesh):
    finer = Mesh(mesh.devices.reshape(4, 4, 4, 2, 2), (*SEQ, *TP))
    in_specs = (
        P(SEQ, None),
        P(),
        P(None, None, TP),
        P(TP, None),
        P(SEQ, None),
        P(SEQ),
        P(None, TP),
        P(None, None, TP),
        P(),
        P(None, SEQ, TP),
        P(TP, SEQ),
    )
    out_specs = (P(SEQ, None), P(SEQ, TP))
    return jax.shard_map(
        shards, mesh=finer, in_specs=in_specs, out_specs=out_specs, check_vma=False
    )
```

```python
import math

import jax
import jax.numpy as jnp
from jax import lax
from jax.experimental import pallas as pl
from jax.experimental.pallas import tpu as pltpu
from jax.sharding import Mesh
from jax.sharding import PartitionSpec as P

EH = 64
HD = 128
WIN = 512
SPILL = 8
EDGE = 16
ZL, RX, RY, ZH, CO = ("z_lo", "ring_x", "ring_y", "z_hi", "core")
SEQ = (ZL, RX, RY)
TP = (ZH, CO)
ROWS = (RX, RY)
COLUMN = (ZL, ZH, CO)

epsilon = 1e-05
rope_base = 500000.0
far_position = 1 << 30
bf16 = jnp.bfloat16
f32 = jnp.float32
i32 = jnp.int32
NT = (((1,), (1,)), ((), ()))


def shifted(value, axis, steps):
    count = lax.axis_size(axis)
    leading, last = (max(0, -steps), min(count, count - steps))
    return lax.ppermute(value, axis, [(source, source + steps) for source in range(leading, last)])


def exchanged(pieces, axis):
    return lax.all_to_all(pieces, axis, split_axis=0, concat_axis=0, tiled=True)


def swapped(value, axis):
    return lax.ppermute(value, axis, [(0, 1), (1, 0)])


def gathered(value, axis):
    return exchanged(jnp.broadcast_to(value, (lax.axis_size(axis), *value.shape)), axis)


def around_ring(value, axis):
    count = lax.axis_size(axis)
    return [value] + [
        lax.ppermute(value, axis, [((i + k) % count, i) for i in range(count)])
        for k in range(1, count)
    ]


def near_ring(value, axis):
    count = lax.axis_size(axis)

    def moved(part, step):
        return lax.ppermute(part, axis, [(i, (i + step) % count) for i in range(count)])

    up, down = (moved(value, 1), moved(value, -1))
    half = value.shape[0] // 2
    return [
        (value, 0, 0),
        (up, count - 1, 0),
        (down, 1, 0),
        (moved(up[:half], 1), 2, 0),
        (moved(down[half:], -1), 2, half),
    ]


def around_column(value):
    low, high = (lax.axis_size(ZL), lax.axis_size(ZH))
    count = low * high

    def moved(part, step):
        named = lambda z: z % count % low * high + z % count // low
        return lax.ppermute(part, (ZL, ZH), [(named(z), named(z + step)) for z in range(count)])

    pieces = [(value, 0, 0)]
    up = down = value
    for step in range(1, count // 2):
        up, down = (moved(up, 1), moved(down, -1))
        pieces += [(up, count - step, 0), (down, step, 0)]
    half = value.shape[0] // 2
    pieces += [(moved(up[:half], 1), count // 2, 0), (moved(down[half:], -1), count // 2, half)]
    return pieces


def on_chip(kernel, outs, scratch=(), limit=16, **extra):
    return pl.pallas_call(
        kernel,
        out_shape=outs,
        scratch_shapes=list(scratch),
        compiler_params=pltpu.CompilerParams(vmem_limit_bytes=limit << 20),
        cost_estimate=pl.CostEstimate(flops=1 << 20, transcendentals=0, bytes_accessed=1 << 20),
        **extra,
    )


def blank(shape, dtype=bf16):
    return jax.ShapeDtypeStruct(shape, dtype)


def encoder_heads(states, gain, weights):
    rows, width = states.shape
    share, _, inner = weights.shape

    def kernel(states_ref, gain_ref, weights_ref, query_ref, keys_values_ref):
        values = states_ref[...].astype(f32)
        factor = lax.rsqrt(jnp.mean(values * values, axis=-1, keepdims=True) + epsilon)
        normed = (values * factor * gain_ref[...].astype(f32)).astype(bf16)
        for i in range(1, share):
            keys_values_ref[:, (i - 1) * inner : i * inner] = jnp.dot(
                normed, weights_ref[i], preferred_element_type=f32
            ).astype(bf16)
        query_ref[...] = jnp.dot(normed, weights_ref[0], preferred_element_type=f32).astype(bf16)

    return on_chip(kernel, [blank((rows, inner)), blank((rows, (share - 1) * inner))])(
        states, gain.reshape(1, width), weights
    )


def encoder_attention(own_q, more_q, far, near, own, more, anchor):
    rows, width = own_q.shape
    total = rows + EDGE
    spans = WIN + total
    padded = -(-spans // 128) * 128

    def kernel(anchor_ref, q_ref, mq_ref, far_ref, near_ref, own_ref, more_ref, out_ref, held):
        at = 0
        for part in (far_ref, near_ref, own_ref, more_ref):
            held[at : at + part.shape[0], :] = part[...]
            at += part.shape[0]
        held[at:, :] = jnp.zeros((padded - at, 2 * width), bf16)
        queries = jnp.concatenate([q_ref[...], mq_ref[...]], axis=0)
        row = lax.broadcasted_iota(i32, (total, padded), 0)
        column = lax.broadcasted_iota(i32, (total, padded), 1)
        allowed = (
            (column - WIN <= row) & (column > row) & (column >= WIN - anchor_ref[0])
        )
        lane = lax.broadcasted_iota(i32, (total, HD), 1)
        for pair in range(width // HD):
            span = slice(pair * HD, (pair + 1) * HD)
            keys = held[:, span]
            values = held[:, width + pair * HD : width + (pair + 1) * HD]
            both = queries[:, span]
            done = None
            for side in range(HD // EH):
                mine = (lane >= side * EH) & (lane < (side + 1) * EH)
                query = jnp.where(mine, both, jnp.zeros_like(both))
                scores = lax.dot_general(query, keys, NT, preferred_element_type=f32)
                scores = jnp.where(allowed, scores * (1.0 / math.sqrt(EH)), -1e30)
                largest = jnp.max(scores, axis=-1, keepdims=True)
                raised = jnp.where(allowed, jnp.exp(scores - largest), 0.0)
                weights = (raised / jnp.maximum(jnp.sum(raised, axis=-1, keepdims=True), 1e-30))
                result = jnp.dot(weights.astype(bf16), values, preferred_element_type=f32)
                done = result if done is None else jnp.where(mine, result, done)
            out_ref[:, span] = done.astype(bf16)

    whole = pl.BlockSpec(memory_space=pltpu.VMEM)
    return on_chip(
        kernel,
        blank((total, width)),
        [pltpu.VMEM((padded, 2 * width), bf16)],
        in_specs=[pl.BlockSpec(memory_space=pltpu.SMEM)] + [whole] * 6,
        out_specs=whole,
    )(anchor.reshape(1), own_q, more_q, far, near, own, more)


def encoder_output(states, edge, attended, parts):
    rows, width = states.shape

    def kernel(states_ref, edge_ref, attended_ref, *refs):
        *part_refs, out_ref = refs
        here = lax.axis_index(TP)
        total = jnp.zeros((rows + EDGE, width), f32)
        for (_, turn, start), part in zip(parts, part_refs):
            deep = part.shape[0]
            piece = attended_ref[lax.bitwise_xor(here, turn), :, start : start + deep]
            total += jnp.dot(piece, part[...], preferred_element_type=f32)
        out_ref[:rows, :] = (states_ref[...].astype(f32) + total[:rows]).astype(bf16)
        out_ref[rows:, :] = (edge_ref[...].astype(f32) + total[rows:]).astype(bf16)

    return on_chip(kernel, blank((rows + EDGE, width)))(
        states, edge, attended, *(part for part, *_ in parts)
    )


def patch_block(extended, bounds, lift, cross_kv):
    spans, width = extended.shape
    slots = bounds.shape[0]
    wide = 2 * HD

    def kernel(extended_ref, bounds_ref, lift_ref, cross_ref, out_ref, pooled_ref):
        column = lax.broadcasted_iota(i32, (slots, spans), 1)
        first, after, seen, used = (bounds_ref[:, k : k + 1] for k in range(4))
        rows = extended_ref[...]

        @pl.when(pl.program_id(0) == 0)
        def _():
            inside = (column >= first) & (column < after)
            member = jnp.where(inside, 1.0, 0.0).astype(bf16)
            lengths = jnp.maximum(after - first, 1).astype(f32)
            totals = jnp.dot(member, rows, preferred_element_type=f32)
            pooled_ref[...] = (totals / lengths).astype(bf16)

        allowed = (column >= first) & (column < seen)
        lifted = jnp.dot(pooled_ref[...], lift_ref[...], preferred_element_type=f32)
        query = lifted.astype(bf16)
        keys = jnp.dot(rows, cross_ref[0], preferred_element_type=f32).astype(bf16)
        values = jnp.dot(rows, cross_ref[1], preferred_element_type=f32).astype(bf16)
        for head in range(wide // HD):
            span = slice(head * HD, (head + 1) * HD)
            scores = lax.dot_general(
                query[:, span], keys[:, span], NT, preferred_element_type=f32
            ) * (1.0 / math.sqrt(HD))
            scores = jnp.where(allowed, scores, -1e30)
            largest = jnp.max(scores, axis=-1, keepdims=True)
            raised = jnp.where(allowed, jnp.exp(scores - largest), 0.0)
            weights = (raised / jnp.sum(raised, axis=-1, keepdims=True)).astype(bf16)
            crossed = jnp.dot(weights, values[:, span], preferred_element_type=f32)
            total = jnp.where(used > 0, lifted[:, span] + crossed, 0.0)
            out_ref[:, span] = total.astype(bf16)

    return on_chip(
        kernel,
        blank((slots, lift.shape[1])),
        [pltpu.VMEM((slots, width), bf16)],
        grid=(lift.shape[1] // wide,),
        in_specs=[
            pl.BlockSpec((spans, width), lambda i: (0, 0)),
            pl.BlockSpec(bounds.shape, lambda i: (0, 0)),
            pl.BlockSpec((width, wide), lambda i: (0, i)),
            pl.BlockSpec((2, width, wide), lambda i: (0, 0, i)),
        ],
        out_specs=pl.BlockSpec((slots, wide), lambda i: (0, i)),
    )(extended, bounds, lift, cross_kv)


def placed_rows(pieces):
    rows, width = pieces[0][0].shape
    low, high = (lax.axis_size(ZL), lax.axis_size(ZH))

    def kernel(*refs):
        *parts, out_ref = refs
        here = lax.axis_index(ZH) * low + lax.axis_index(ZL)
        for part, (_, distance, shift) in zip(parts, pieces):
            z = lax.bitwise_and(here + distance, low * high - 1)
            across = lax.bitwise_and(z, low - 1) * rows + shift
            down = lax.shift_right_logical(z, low.bit_length() - 1) * width
            out_ref[
                pl.ds(pl.multiple_of(across, 16), part.shape[0]),
                pl.ds(pl.multiple_of(down, 128), width),
            ] = part[...]

    return on_chip(kernel, blank((low * rows, high * width)))(*(part for part, *_ in pieces))


def head_weights(lat_qkv, gains, counts):
    share, depth, inner = lat_qkv.shape
    step = share * depth + EDGE
    heads = inner // HD

    def kernel(count_ref, weights_ref, gains_ref, out_ref):
        block = lax.axis_index(SEQ)
        gains = gains_ref[...].astype(f32)
        mine = lax.broadcasted_iota(i32, gains.shape, 0) == block
        row = jnp.sum(jnp.where(mine, gains, 0.0), axis=0, keepdims=True)
        square = (depth, depth)
        same = lax.broadcasted_iota(i32, square, 0) == lax.broadcasted_iota(i32, square, 1)
        column = jnp.sum(jnp.where(same, row, 0.0), axis=1, keepdims=True)
        mark = jnp.full((EDGE, HD), count_ref[0].astype(f32)).astype(bf16)
        for i in range(share):
            scaled = (weights_ref[i].astype(f32) * column).astype(bf16)
            for k in range(heads):
                out_ref[k, i * depth : (i + 1) * depth, :] = scaled[:, k * HD : (k + 1) * HD]
        for k in range(heads):
            out_ref[k, share * depth :, :] = mark

    whole = pl.BlockSpec(memory_space=pltpu.VMEM)
    return on_chip(
        kernel,
        blank((heads, step, HD)),
        in_specs=[pl.BlockSpec(memory_space=pltpu.SMEM), whole, whole],
        out_specs=whole,
    )(counts, lat_qkv, gains)


def copied_weights(out_part, by_head, copies):
    cut, deep = out_part.shape
    heads, step, _ = by_head.shape
    total = heads * (cut + step)

    def kernel(out_part_ref, by_head_ref, out_ref):
        for k in range(heads):
            out_ref[0, k * cut : (k + 1) * cut, :] = out_part_ref[:, k * HD : (k + 1) * HD]
            start = heads * cut + k * step
            out_ref[0, start : start + step, :] = by_head_ref[k]

    return on_chip(
        kernel,
        blank((copies, total, HD)),
        grid=(copies,),
        in_specs=[
            pl.BlockSpec(out_part.shape, lambda i: (0, 0)),
            pl.BlockSpec(by_head.shape, lambda i: (0, 0, 0)),
        ],
        out_specs=pl.BlockSpec((1, total, HD), lambda i: (i, 0, 0)),
    )(out_part, by_head)


def placed_weights(gathered_weights, first, columns, share, depth, step):
    groups = gathered_weights.shape[0]

    def kernel(weights_ref, out_ref):
        core = lax.axis_index(CO)
        for g in range(groups):
            for side in range(2):
                for high in range(columns // 2):
                    t = 2 * high + lax.bitwise_xor(core, side)
                    for i in range(share):
                        start = pl.multiple_of(first + t * step + i * depth, 16)
                        out_ref[
                            side, high, g * depth : (g + 1) * depth, i * HD : (i + 1) * HD
                        ] = weights_ref[g, pl.ds(start, depth), :]

    return on_chip(kernel, blank((2, columns // 2, groups * depth, share * HD)))(
        gathered_weights
    )


def latent_heads(own_rows, other_rows, weights, cosine, sine):
    rows, width = own_rows.shape
    full = 2 * width

    def kernel(own_ref, other_ref, weights_ref, cosine_ref, sine_ref, q_ref, k_ref, v_ref):
        squares = jnp.zeros((rows, 1), f32)
        total = jnp.zeros((rows, 3 * HD), f32)
        half = width // 2
        for side, part in enumerate((own_ref, other_ref)):
            for high in range(2):
                values = part[:, high * half : (high + 1) * half]
                wide = values.astype(f32)
                squares += jnp.sum(wide * wide, axis=1, keepdims=True)
                total += jnp.dot(values, weights_ref[side, high], preferred_element_type=f32)
        total = total * lax.rsqrt(squares / full + epsilon)
        for which, out_ref in enumerate((q_ref, k_ref)):
            value = total[:, which * HD : (which + 1) * HD]
            turned = value * cosine_ref[...] + pltpu.roll(value, HD // 2, 1) * sine_ref[...]
            out_ref[...] = turned.astype(bf16)
        v_ref[...] = total[:, 2 * HD :].astype(bf16)

    return on_chip(kernel, [blank((rows, HD))] * 3)(
        own_rows, other_rows, weights, cosine, sine
    )


def latent_attention(queries, keys, values, position, key_pos):
    rows = queries.shape[0]
    n_x, n_y = (len(keys), len(values))

    def kernel(*refs):
        q_ref, pos_ref, key_pos_ref = refs[:3]
        key_refs, value_refs = (refs[3 : 3 + n_x], refs[3 + n_x : 3 + n_x + n_y])
        out_ref, held = refs[3 + n_x + n_y :]
        query = q_ref[...]
        position = pos_ref[...]
        top = jnp.full((rows, rows), -1e30, f32)
        for x in range(n_x):
            for y in range(n_y):
                scores = lax.dot_general(
                    query, key_refs[x][y], NT, preferred_element_type=f32
                ) * (1.0 / math.sqrt(HD))
                allowed = key_pos_ref[x * n_y + y : x * n_y + y + 1, :] <= position
                scores = jnp.where(allowed, scores, -1e30)
                held[x * n_y + y] = scores
                top = jnp.maximum(top, scores)
        largest = jnp.max(top, axis=-1, keepdims=True)
        total = jnp.zeros((rows, rows), f32)
        weighted = jnp.zeros((rows, HD), f32)
        for x in range(n_x):
            for y in range(n_y):
                raised = jnp.exp(held[x * n_y + y] - largest)
                total += raised
                weighted += jnp.dot(
                    raised.astype(bf16), value_refs[y][x], preferred_element_type=f32
                )
        out_ref[...] = (weighted / jnp.sum(total, axis=-1, keepdims=True)).astype(bf16)

    return on_chip(
        kernel, blank((rows, HD)), [pltpu.VMEM((n_x * n_y, rows, rows), f32)]
    )(queries, position, key_pos, *keys, *values)


def partial_outputs(heads, weights):
    columns, rows, _ = heads.shape
    groups = weights.shape[0]
    slots = rows // columns
    cut = slots
    pair = columns // 2

    def kernel(heads_ref, weights_ref, kept_ref, sent_ref):
        core, high = (lax.axis_index(CO), lax.axis_index(ZH))
        flat = [
            weights_ref[:, zl * cut : (zl + 1) * cut, :].reshape(groups * cut, HD)
            for zl in range(columns)
        ]
        for side, out_ref in enumerate((kept_ref, sent_ref)):
            for i in range(pair):
                block = pair * lax.bitwise_xor(core, side) + lax.bitwise_xor(high, i)
                span = pl.ds(pl.multiple_of(block * slots, slots), slots)
                total = jnp.zeros((slots, groups * cut), f32)
                for zl in range(columns):
                    total += lax.dot_general(
                        heads_ref[zl, span, :], flat[zl], NT, preferred_element_type=f32
                    )
                out_ref[i] = total.astype(out_ref.dtype)

    block = (groups, columns * cut, HD)
    shape = (pair, slots, groups * cut)
    whole = pl.BlockSpec(shape, lambda i: (0, 0, 0))
    return on_chip(
        kernel,
        [blank(shape, f32), blank(shape)],
        grid=(1,),
        in_specs=[
            pl.BlockSpec(heads.shape, lambda i: (0, 0, 0)),
            pl.BlockSpec(block, lambda i: (0, 0, 0)),
        ],
        out_specs=[whole, whole],
    )(heads, weights)


def added_outputs(kept, received):
    pair = kept.shape[0]

    def kernel(kept_ref, received_ref, *out_refs):
        for i, out_ref in enumerate(out_refs):
            out_ref[...] = (kept_ref[i] + received_ref[i].astype(f32)).astype(bf16)

    return on_chip(kernel, [blank(kept.shape[1:])] * pair)(kept, received)


def summed_outputs(pieces, patches, counts):
    def kernel(count_ref, patches_ref, *refs):
        *piece_refs, out_ref = refs
        total = patches_ref[...].astype(f32)
        for piece in piece_refs:
            total += piece[...].astype(f32)
        used = lax.broadcasted_iota(i32, total.shape, 0) < count_ref[0]
        out_ref[...] = jnp.where(used, total, 0.0).astype(bf16)

    whole = pl.BlockSpec(memory_space=pltpu.VMEM)
    return on_chip(
        kernel,
        blank(patches.shape),
        in_specs=[pl.BlockSpec(memory_space=pltpu.SMEM)] + [whole] * (1 + len(pieces)),
        out_specs=whole,
    )(counts, patches, *pieces)


def shards(
    byte_states,
    enc_gain,
    enc_qkv,
    enc_proj_out,
    starts,
    counts,
    lift,
    cross_kv,
    latent_gain,
    lat_qkv,
    lat_proj_out,
):
    byte_rows, byte_width = byte_states.shape
    slots = starts.shape[1]
    columns = lax.axis_size(ZL)
    tensor = lax.axis_size(TP)
    groups = lax.axis_size(ROWS)
    block = lax.axis_index(SEQ)
    anchor = block * byte_rows
    local_starts = starts[0]
    patch_count = counts[0]
    slot_ids = jnp.arange(slots, dtype=i32)
    in_use = slot_ids < patch_count

    own_q, own_kv = encoder_heads(byte_states, enc_gain, enc_qkv)
    far_kv = shifted(own_kv, SEQ, 2)
    near_kv = shifted(own_kv, SEQ, 1)

    first_local = (local_starts[0] - anchor).astype(bf16)
    edge = jnp.concatenate(
        [
            byte_states[:SPILL],
            jnp.broadcast_to(first_local, (EDGE - SPILL, byte_width)),
        ],
        axis=0,
    )
    edge = shifted(edge, SEQ, -1)

    share, depth, inner = lat_qkv.shape
    step = share * depth + EDGE
    by_head = head_weights(lat_qkv, latent_gain.reshape(-1, depth), counts)
    by_head = exchanged(by_head, ZL)
    cut = lat_proj_out.shape[1]

    half = enc_proj_out.shape[0] // 2
    high_a, high_b = (swapped(enc_proj_out[at : at + half], ZH) for at in (0, half))
    out_side = swapped(enc_proj_out, CO)

    near_kv, far_kv, edge, out_side, high_a = lax.optimization_barrier(
        (near_kv, far_kv, edge, out_side, high_a)
    )
    next_first = edge[SPILL, 0].astype(i32)
    more_q, more_kv = encoder_heads(edge, enc_gain, enc_qkv)
    attended = encoder_attention(own_q, more_q, far_kv, near_kv, own_kv, more_kv, anchor)
    both_a = swapped(high_a, CO)
    attended, by_head, high_b, both_a = lax.optimization_barrier(
        (attended, by_head, high_b, both_a)
    )
    by_head = exchanged(copied_weights(lat_proj_out.T, by_head, groups), ROWS)
    both_b = swapped(high_b, CO)
    attended = lax.all_gather(attended, TP)
    extended = encoder_output(
        byte_states,
        edge,
        attended,
        (
            (enc_proj_out, 0, 0),
            (out_side, 1, 0),
            (high_a, 2, 0),
            (both_a, 3, 0),
            (high_b, 2, half),
            (both_b, 3, half),
        ),
    )
    encoded = extended[:byte_rows]

    following = jnp.concatenate([local_starts[1:], jnp.zeros((1,), i32)])
    patch_end = jnp.where(slot_ids + 1 < patch_count, following, anchor + byte_rows + next_first)
    first, after = (jnp.where(in_use, end - anchor, 0) for end in (local_starts, patch_end))
    used = in_use.astype(i32)
    bounds = jnp.stack([first, after, jnp.where(in_use, after, 1), used], axis=1)
    patches = patch_block(extended, bounds, lift, cross_kv)
    own_rows = placed_rows(around_column(patches))
    other_rows = swapped(own_rows, CO)
    own_rows, by_head = lax.optimization_barrier((own_rows, by_head))
    latent_in = placed_weights(by_head, columns * cut, columns, share, depth, step)

    grid = (*(lax.axis_size(name) for name in ROWS), columns)
    here = tuple(lax.axis_index(name) for name in ROWS)
    all_counts = jnp.stack(
        [by_head[:, columns * cut + (k + 1) * step - 1, 0] for k in range(columns)], axis=1
    )
    all_counts = all_counts.astype(i32).reshape(*grid)
    all_counts = lax.dynamic_slice(jnp.tile(all_counts, (2, 2, 1)), (*here, 0), grid)
    order = sum(
        stride
        * lax.bitwise_and(lax.broadcasted_iota(i32, grid, dim) + start, grid[dim] - 1)
        for dim, stride, start in ((0, grid[1], here[0]), (1, 1, here[1]), (2, groups, 0))
    ).reshape(-1)
    flat_counts = all_counts.reshape(-1)
    offsets = jnp.sum(jnp.where(order[None, :] < order[:, None], flat_counts[None, :], 0), axis=1)
    position = (offsets[:columns, None] + slot_ids[None, :]).reshape(-1)
    key_pos = jnp.where(
        slot_ids[None, :] < flat_counts[:, None], offsets[:, None] + slot_ids[None, :], far_position
    ).reshape(groups, columns * slots)
    halfway = HD // 2
    frequency = jnp.power(rope_base, -2.0 * jnp.arange(halfway, dtype=f32) / HD)
    angles = position.astype(f32)[:, None] * frequency[None, :]
    cosine, sine = (jnp.cos(angles), jnp.sin(angles))
    cosine = jnp.concatenate([cosine, cosine], axis=1)
    sine = jnp.concatenate([-sine, sine], axis=1)

    queries, keys, values = latent_heads(own_rows, other_rows, latent_in, cosine, sine)
    keys = around_ring(jnp.stack(around_ring(keys, RY)), RX)
    values = around_ring(jnp.stack(around_ring(values, RX)), RY)
    heads = latent_attention(queries, keys, values, position[:, None], key_pos)

    kept, sent = partial_outputs(lax.all_gather(heads, ZL), by_head)
    partial = added_outputs(kept, swapped(sent, CO))
    places = [(a, h, c) for a in range(columns) for h in range(2) for c in range(2)]
    partial = [
        lax.ppermute(
            piece,
            COLUMN,
            [(a * tensor + 2 * h + c, (2 * c + (h ^ i)) * tensor + a) for a, h, c in places],
        )
        for i, piece in enumerate(partial)
    ]
    latent = summed_outputs(partial, patches, counts)
    return (encoded, latent)


def solution(mesh):
    finer = Mesh(mesh.devices.reshape(4, 4, 4, 2, 2), (*SEQ, *TP))
    in_specs = (
        P(SEQ, None),
        P(),
        P(None, None, TP),
        P(TP, None),
        P(SEQ, None),
        P(SEQ),
        P(None, TP),
        P(None, None, TP),
        P(),
        P(None, SEQ, TP),
        P(TP, SEQ),
    )
    out_specs = (P(SEQ, None), P(SEQ, TP))
    return jax.shard_map(
        shards, mesh=finer, in_specs=in_specs, out_specs=out_specs, check_vma=False
    )
```

```python
import math

import jax
import jax.numpy as jnp
from jax import lax
from jax.experimental import pallas as pl
from jax.experimental.pallas import tpu as pltpu
from jax.sharding import Mesh
from jax.sharding import PartitionSpec as P

EH = 64
HD = 128
WIN = 512
SPILL = 8
EDGE = 16
ZL, RX, RY, ZH, CO = ("z_lo", "ring_x", "ring_y", "z_hi", "core")
SEQ = (ZL, RX, RY)
TP = (ZH, CO)
ROWS = (RX, RY)
COLUMN = (ZL, ZH, CO)

epsilon = 1e-05
rope_base = 500000.0
far_position = 1 << 30
bf16 = jnp.bfloat16
f32 = jnp.float32
i32 = jnp.int32
NT = (((1,), (1,)), ((), ()))


def shifted(value, axis, steps):
    count = lax.axis_size(axis)
    leading, last = (max(0, -steps), min(count, count - steps))
    return lax.ppermute(value, axis, [(source, source + steps) for source in range(leading, last)])


def exchanged(pieces, axis):
    return lax.all_to_all(pieces, axis, split_axis=0, concat_axis=0, tiled=True)


def swapped(value, axis):
    return lax.ppermute(value, axis, [(0, 1), (1, 0)])


def gathered(value, axis):
    return exchanged(jnp.broadcast_to(value, (lax.axis_size(axis), *value.shape)), axis)


def around_ring(value, axis):
    count = lax.axis_size(axis)
    return [value] + [
        lax.ppermute(value, axis, [((i + k) % count, i) for i in range(count)])
        for k in range(1, count)
    ]


def near_ring(value, axis):
    count = lax.axis_size(axis)

    def moved(part, step):
        return lax.ppermute(part, axis, [(i, (i + step) % count) for i in range(count)])

    up, down = (moved(value, 1), moved(value, -1))
    half = value.shape[0] // 2
    return [
        (value, 0, 0),
        (up, count - 1, 0),
        (down, 1, 0),
        (moved(up[:half], 1), 2, 0),
        (moved(down[half:], -1), 2, half),
    ]


def around_column(value):
    low, high = (lax.axis_size(ZL), lax.axis_size(ZH))
    count = low * high

    def moved(part, step):
        named = lambda z: z % count % low * high + z % count // low
        return lax.ppermute(part, (ZL, ZH), [(named(z), named(z + step)) for z in range(count)])

    pieces = [(value, 0, 0)]
    up = down = value
    for step in range(1, count // 2):
        up, down = (moved(up, 1), moved(down, -1))
        pieces += [(up, count - step, 0), (down, step, 0)]
    half = value.shape[0] // 2
    pieces += [(moved(up[:half], 1), count // 2, 0), (moved(down[half:], -1), count // 2, half)]
    return pieces


def on_chip(kernel, outs, scratch=(), limit=16, **extra):
    return pl.pallas_call(
        kernel,
        out_shape=outs,
        scratch_shapes=list(scratch),
        compiler_params=pltpu.CompilerParams(vmem_limit_bytes=limit << 20),
        cost_estimate=pl.CostEstimate(flops=1 << 20, transcendentals=0, bytes_accessed=1 << 20),
        **extra,
    )


def blank(shape, dtype=bf16):
    return jax.ShapeDtypeStruct(shape, dtype)


def encoder_heads(states, gain, weights):
    rows, width = states.shape
    share, _, inner = weights.shape

    def kernel(states_ref, gain_ref, weights_ref, query_ref, keys_values_ref):
        values = states_ref[...].astype(f32)
        factor = lax.rsqrt(jnp.mean(values * values, axis=-1, keepdims=True) + epsilon)
        normed = (values * factor * gain_ref[...].astype(f32)).astype(bf16)
        for i in range(1, share):
            keys_values_ref[:, (i - 1) * inner : i * inner] = jnp.dot(
                normed, weights_ref[i], preferred_element_type=f32
            ).astype(bf16)
        query_ref[...] = jnp.dot(normed, weights_ref[0], preferred_element_type=f32).astype(bf16)

    return on_chip(kernel, [blank((rows, inner)), blank((rows, (share - 1) * inner))])(
        states, gain.reshape(1, width), weights
    )


def encoder_attention(own_q, more_q, far, near, own, more, anchor):
    rows, width = own_q.shape
    total = rows + EDGE
    spans = WIN + total
    padded = -(-spans // 128) * 128

    def kernel(anchor_ref, q_ref, mq_ref, far_ref, near_ref, own_ref, more_ref, out_ref, held):
        at = 0
        for part in (far_ref, near_ref, own_ref, more_ref):
            held[at : at + part.shape[0], :] = part[...]
            at += part.shape[0]
        held[at:, :] = jnp.zeros((padded - at, 2 * width), bf16)
        queries = jnp.concatenate([q_ref[...], mq_ref[...]], axis=0)
        row = lax.broadcasted_iota(i32, (total, padded), 0)
        column = lax.broadcasted_iota(i32, (total, padded), 1)
        allowed = (
            (column - WIN <= row) & (column > row) & (column >= WIN - anchor_ref[0])
        )
        lane = lax.broadcasted_iota(i32, (total, HD), 1)
        for pair in range(width // HD):
            span = slice(pair * HD, (pair + 1) * HD)
            keys = held[:, span]
            values = held[:, width + pair * HD : width + (pair + 1) * HD]
            both = queries[:, span]
            done = None
            for side in range(HD // EH):
                mine = (lane >= side * EH) & (lane < (side + 1) * EH)
                query = jnp.where(mine, both, jnp.zeros_like(both))
                scores = lax.dot_general(query, keys, NT, preferred_element_type=f32)
                scores = jnp.where(allowed, scores * (1.0 / math.sqrt(EH)), -1e30)
                largest = jnp.max(scores, axis=-1, keepdims=True)
                raised = jnp.where(allowed, jnp.exp(scores - largest), 0.0)
                weights = (raised / jnp.maximum(jnp.sum(raised, axis=-1, keepdims=True), 1e-30))
                result = jnp.dot(weights.astype(bf16), values, preferred_element_type=f32)
                done = result if done is None else jnp.where(mine, result, done)
            out_ref[:, span] = done.astype(bf16)

    whole = pl.BlockSpec(memory_space=pltpu.VMEM)
    return on_chip(
        kernel,
        blank((total, width)),
        [pltpu.VMEM((padded, 2 * width), bf16)],
        in_specs=[pl.BlockSpec(memory_space=pltpu.SMEM)] + [whole] * 6,
        out_specs=whole,
    )(anchor.reshape(1), own_q, more_q, far, near, own, more)


def encoder_output(states, edge, attended, parts):
    rows, width = states.shape

    def kernel(states_ref, edge_ref, attended_ref, *refs):
        *part_refs, out_ref = refs
        here = lax.axis_index(TP)
        total = jnp.zeros((rows + EDGE, width), f32)
        for (_, turn, start), part in zip(parts, part_refs):
            deep = part.shape[0]
            piece = attended_ref[lax.bitwise_xor(here, turn), :, start : start + deep]
            total += jnp.dot(piece, part[...], preferred_element_type=f32)
        out_ref[:rows, :] = (states_ref[...].astype(f32) + total[:rows]).astype(bf16)
        out_ref[rows:, :] = (edge_ref[...].astype(f32) + total[rows:]).astype(bf16)

    return on_chip(kernel, blank((rows + EDGE, width)))(
        states, edge, attended, *(part for part, *_ in parts)
    )


def patch_block(extended, bounds, lift, cross_kv):
    spans, width = extended.shape
    slots = bounds.shape[0]
    wide = 2 * HD

    def kernel(extended_ref, bounds_ref, lift_ref, cross_ref, out_ref, pooled_ref):
        column = lax.broadcasted_iota(i32, (slots, spans), 1)
        first, after, seen, used = (bounds_ref[:, k : k + 1] for k in range(4))
        rows = extended_ref[...]

        @pl.when(pl.program_id(0) == 0)
        def _():
            inside = (column >= first) & (column < after)
            member = jnp.where(inside, 1.0, 0.0).astype(bf16)
            lengths = jnp.maximum(after - first, 1).astype(f32)
            totals = jnp.dot(member, rows, preferred_element_type=f32)
            pooled_ref[...] = (totals / lengths).astype(bf16)

        allowed = (column >= first) & (column < seen)
        lifted = jnp.dot(pooled_ref[...], lift_ref[...], preferred_element_type=f32)
        query = lifted.astype(bf16)
        keys = jnp.dot(rows, cross_ref[0], preferred_element_type=f32).astype(bf16)
        values = jnp.dot(rows, cross_ref[1], preferred_element_type=f32).astype(bf16)
        for head in range(wide // HD):
            span = slice(head * HD, (head + 1) * HD)
            scores = lax.dot_general(
                query[:, span], keys[:, span], NT, preferred_element_type=f32
            ) * (1.0 / math.sqrt(HD))
            scores = jnp.where(allowed, scores, -1e30)
            largest = jnp.max(scores, axis=-1, keepdims=True)
            raised = jnp.where(allowed, jnp.exp(scores - largest), 0.0)
            weights = (raised / jnp.sum(raised, axis=-1, keepdims=True)).astype(bf16)
            crossed = jnp.dot(weights, values[:, span], preferred_element_type=f32)
            total = jnp.where(used > 0, lifted[:, span] + crossed, 0.0)
            out_ref[:, span] = total.astype(bf16)

    return on_chip(
        kernel,
        blank((slots, lift.shape[1])),
        [pltpu.VMEM((slots, width), bf16)],
        grid=(lift.shape[1] // wide,),
        in_specs=[
            pl.BlockSpec((spans, width), lambda i: (0, 0)),
            pl.BlockSpec(bounds.shape, lambda i: (0, 0)),
            pl.BlockSpec((width, wide), lambda i: (0, i)),
            pl.BlockSpec((2, width, wide), lambda i: (0, 0, i)),
        ],
        out_specs=pl.BlockSpec((slots, wide), lambda i: (0, i)),
    )(extended, bounds, lift, cross_kv)


def placed_rows(pieces):
    rows, width = pieces[0][0].shape
    low, high = (lax.axis_size(ZL), lax.axis_size(ZH))

    def kernel(*refs):
        *parts, out_ref = refs
        here = lax.axis_index(ZH) * low + lax.axis_index(ZL)
        for part, (_, distance, shift) in zip(parts, pieces):
            z = lax.bitwise_and(here + distance, low * high - 1)
            across = lax.bitwise_and(z, low - 1) * rows + shift
            down = lax.shift_right_logical(z, low.bit_length() - 1) * width
            out_ref[
                pl.ds(pl.multiple_of(across, 16), part.shape[0]),
                pl.ds(pl.multiple_of(down, 128), width),
            ] = part[...]

    return on_chip(kernel, blank((low * rows, high * width)))(*(part for part, *_ in pieces))


def head_weights(lat_qkv, gains, counts):
    share, depth, inner = lat_qkv.shape
    step = share * depth + EDGE
    heads = inner // HD

    def kernel(count_ref, weights_ref, gains_ref, out_ref):
        block = lax.axis_index(SEQ)
        gains = gains_ref[...].astype(f32)
        mine = lax.broadcasted_iota(i32, gains.shape, 0) == block
        row = jnp.sum(jnp.where(mine, gains, 0.0), axis=0, keepdims=True)
        square = (depth, depth)
        same = lax.broadcasted_iota(i32, square, 0) == lax.broadcasted_iota(i32, square, 1)
        column = jnp.sum(jnp.where(same, row, 0.0), axis=1, keepdims=True)
        mark = jnp.full((EDGE, HD), count_ref[0].astype(f32)).astype(bf16)
        for i in range(share):
            scaled = (weights_ref[i].astype(f32) * column).astype(bf16)
            for k in range(heads):
                out_ref[k, i * depth : (i + 1) * depth, :] = scaled[:, k * HD : (k + 1) * HD]
        for k in range(heads):
            out_ref[k, share * depth :, :] = mark

    whole = pl.BlockSpec(memory_space=pltpu.VMEM)
    return on_chip(
        kernel,
        blank((heads, step, HD)),
        in_specs=[pl.BlockSpec(memory_space=pltpu.SMEM), whole, whole],
        out_specs=whole,
    )(counts, lat_qkv, gains)


def copied_weights(out_part, by_head, copies):
    cut, deep = out_part.shape
    heads, step, _ = by_head.shape
    total = heads * (cut + step)

    def kernel(out_part_ref, by_head_ref, out_ref):
        for k in range(heads):
            out_ref[0, k * cut : (k + 1) * cut, :] = out_part_ref[:, k * HD : (k + 1) * HD]
            start = heads * cut + k * step
            out_ref[0, start : start + step, :] = by_head_ref[k]

    return on_chip(
        kernel,
        pltpu.HBM((copies, total, HD), bf16),
        grid=(copies,),
        in_specs=[
            pl.BlockSpec(out_part.shape, lambda i: (0, 0)),
            pl.BlockSpec(by_head.shape, lambda i: (0, 0, 0)),
        ],
        out_specs=pl.BlockSpec((1, total, HD), lambda i: (i, 0, 0)),
    )(out_part, by_head)


def placed_weights(gathered_weights, first, columns, share, depth, step):
    groups = gathered_weights.shape[0]

    def kernel(weights_ref, out_ref):
        core = lax.axis_index(CO)
        for g in range(groups):
            for side in range(2):
                for high in range(columns // 2):
                    t = 2 * high + lax.bitwise_xor(core, side)
                    for i in range(share):
                        start = pl.multiple_of(first + t * step + i * depth, 16)
                        out_ref[
                            side, high, g * depth : (g + 1) * depth, i * HD : (i + 1) * HD
                        ] = weights_ref[g, pl.ds(start, depth), :]

    return on_chip(kernel, blank((2, columns // 2, groups * depth, share * HD)))(
        gathered_weights
    )


def latent_heads(own_rows, other_rows, weights, cosine, sine):
    rows, width = own_rows.shape
    full = 2 * width

    def kernel(own_ref, other_ref, weights_ref, cosine_ref, sine_ref, q_ref, k_ref, v_ref):
        squares = jnp.zeros((rows, 1), f32)
        total = jnp.zeros((rows, 3 * HD), f32)
        half = width // 2
        for side, part in enumerate((own_ref, other_ref)):
            for high in range(2):
                values = part[:, high * half : (high + 1) * half]
                wide = values.astype(f32)
                squares += jnp.sum(wide * wide, axis=1, keepdims=True)
                total += jnp.dot(values, weights_ref[side, high], preferred_element_type=f32)
        total = total * lax.rsqrt(squares / full + epsilon)
        for which, out_ref in enumerate((q_ref, k_ref)):
            value = total[:, which * HD : (which + 1) * HD]
            turned = value * cosine_ref[...] + pltpu.roll(value, HD // 2, 1) * sine_ref[...]
            out_ref[...] = turned.astype(bf16)
        v_ref[...] = total[:, 2 * HD :].astype(bf16)

    return on_chip(kernel, [blank((rows, HD))] * 3)(
        own_rows, other_rows, weights, cosine, sine
    )


def latent_attention(queries, keys, values, position, key_pos):
    rows = queries.shape[0]
    n_x, n_y = (len(keys), len(values))

    def kernel(*refs):
        q_ref, pos_ref, key_pos_ref = refs[:3]
        key_refs, value_refs = (refs[3 : 3 + n_x], refs[3 + n_x : 3 + n_x + n_y])
        out_ref, held = refs[3 + n_x + n_y :]
        query = q_ref[...]
        position = pos_ref[...]
        top = jnp.full((rows, rows), -1e30, f32)
        for x in range(n_x):
            for y in range(n_y):
                scores = lax.dot_general(
                    query, key_refs[x][y], NT, preferred_element_type=f32
                ) * (1.0 / math.sqrt(HD))
                allowed = key_pos_ref[x * n_y + y : x * n_y + y + 1, :] <= position
                scores = jnp.where(allowed, scores, -1e30)
                held[x * n_y + y] = scores
                top = jnp.maximum(top, scores)
        largest = jnp.max(top, axis=-1, keepdims=True)
        total = jnp.zeros((rows, rows), f32)
        weighted = jnp.zeros((rows, HD), f32)
        for x in range(n_x):
            for y in range(n_y):
                raised = jnp.exp(held[x * n_y + y] - largest)
                total += raised
                weighted += jnp.dot(
                    raised.astype(bf16), value_refs[y][x], preferred_element_type=f32
                )
        out_ref[...] = (weighted / jnp.sum(total, axis=-1, keepdims=True)).astype(bf16)

    return on_chip(
        kernel, blank((rows, HD)), [pltpu.VMEM((n_x * n_y, rows, rows), f32)]
    )(queries, position, key_pos, *keys, *values)


def partial_outputs(heads, weights):
    columns, rows, _ = heads.shape
    groups = weights.shape[0]
    slots = rows // columns
    cut = slots
    pair = columns // 2

    def kernel(heads_ref, weights_ref, kept_ref, sent_ref):
        core, high = (lax.axis_index(CO), lax.axis_index(ZH))
        flat = [
            weights_ref[:, zl * cut : (zl + 1) * cut, :].reshape(groups * cut, HD)
            for zl in range(columns)
        ]
        for side, out_ref in enumerate((kept_ref, sent_ref)):
            for i in range(pair):
                block = pair * lax.bitwise_xor(core, side) + lax.bitwise_xor(high, i)
                span = pl.ds(pl.multiple_of(block * slots, slots), slots)
                total = jnp.zeros((slots, groups * cut), f32)
                for zl in range(columns):
                    total += lax.dot_general(
                        heads_ref[zl, span, :], flat[zl], NT, preferred_element_type=f32
                    )
                out_ref[i] = total.astype(out_ref.dtype)

    block = (groups, columns * cut, HD)
    shape = (pair, slots, groups * cut)
    whole = pl.BlockSpec(shape, lambda i: (0, 0, 0))
    return on_chip(
        kernel,
        [blank(shape, f32), blank(shape)],
        grid=(1,),
        in_specs=[
            pl.BlockSpec(heads.shape, lambda i: (0, 0, 0)),
            pl.BlockSpec(block, lambda i: (0, 0, 0)),
        ],
        out_specs=[whole, whole],
    )(heads, weights)


def added_outputs(kept, received):
    pair = kept.shape[0]

    def kernel(kept_ref, received_ref, *out_refs):
        for i, out_ref in enumerate(out_refs):
            out_ref[...] = (kept_ref[i] + received_ref[i].astype(f32)).astype(bf16)

    return on_chip(kernel, [blank(kept.shape[1:])] * pair)(kept, received)


def summed_outputs(pieces, patches, counts):
    def kernel(count_ref, patches_ref, *refs):
        *piece_refs, out_ref = refs
        total = patches_ref[...].astype(f32)
        for piece in piece_refs:
            total += piece[...].astype(f32)
        used = lax.broadcasted_iota(i32, total.shape, 0) < count_ref[0]
        out_ref[...] = jnp.where(used, total, 0.0).astype(bf16)

    whole = pl.BlockSpec(memory_space=pltpu.VMEM)
    return on_chip(
        kernel,
        blank(patches.shape),
        in_specs=[pl.BlockSpec(memory_space=pltpu.SMEM)] + [whole] * (1 + len(pieces)),
        out_specs=whole,
    )(counts, patches, *pieces)


def shards(
    byte_states,
    enc_gain,
    enc_qkv,
    enc_proj_out,
    starts,
    counts,
    lift,
    cross_kv,
    latent_gain,
    lat_qkv,
    lat_proj_out,
):
    byte_rows, byte_width = byte_states.shape
    slots = starts.shape[1]
    columns = lax.axis_size(ZL)
    tensor = lax.axis_size(TP)
    groups = lax.axis_size(ROWS)
    block = lax.axis_index(SEQ)
    anchor = block * byte_rows
    local_starts = starts[0]
    patch_count = counts[0]
    slot_ids = jnp.arange(slots, dtype=i32)
    in_use = slot_ids < patch_count

    own_q, own_kv = encoder_heads(byte_states, enc_gain, enc_qkv)
    far_kv = shifted(own_kv, SEQ, 2)
    near_kv = shifted(own_kv, SEQ, 1)

    first_local = (local_starts[0] - anchor).astype(bf16)
    edge = jnp.concatenate(
        [
            byte_states[:SPILL],
            jnp.broadcast_to(first_local, (EDGE - SPILL, byte_width)),
        ],
        axis=0,
    )
    edge = shifted(edge, SEQ, -1)

    share, depth, inner = lat_qkv.shape
    step = share * depth + EDGE
    by_head = head_weights(lat_qkv, latent_gain.reshape(-1, depth), counts)
    by_head = exchanged(by_head, ZL)
    cut = lat_proj_out.shape[1]

    most = enc_proj_out.shape[0] // 2
    high_a, high_b = (swapped(part, ZH) for part in (enc_proj_out[:most], enc_proj_out[most:]))
    out_side = swapped(enc_proj_out, CO)

    near_kv, far_kv, edge, out_side, high_a = lax.optimization_barrier(
        (near_kv, far_kv, edge, out_side, high_a)
    )
    next_first = edge[SPILL, 0].astype(i32)
    more_q, more_kv = encoder_heads(edge, enc_gain, enc_qkv)
    attended = encoder_attention(own_q, more_q, far_kv, near_kv, own_kv, more_kv, anchor)
    both_a = swapped(high_a, CO)
    attended, by_head, both_a = lax.optimization_barrier((attended, by_head, both_a))
    by_head = exchanged(copied_weights(lat_proj_out.T, by_head, groups), ROWS)
    attended = lax.all_gather(attended, TP)
    attended, high_b = lax.optimization_barrier((attended, high_b))
    both_b = swapped(high_b, CO)
    extended = encoder_output(
        byte_states,
        edge,
        attended,
        (
            (enc_proj_out, 0, 0),
            (out_side, 1, 0),
            (high_a, 2, 0),
            (both_a, 3, 0),
            (high_b, 2, most),
            (both_b, 3, most),
        ),
    )
    encoded = extended[:byte_rows]

    following = jnp.concatenate([local_starts[1:], jnp.zeros((1,), i32)])
    patch_end = jnp.where(slot_ids + 1 < patch_count, following, anchor + byte_rows + next_first)
    first, after = (jnp.where(in_use, end - anchor, 0) for end in (local_starts, patch_end))
    used = in_use.astype(i32)
    bounds = jnp.stack([first, after, jnp.where(in_use, after, 1), used], axis=1)
    patches = patch_block(extended, bounds, lift, cross_kv)
    own_rows = placed_rows(around_column(patches))
    other_rows = swapped(own_rows, CO)
    own_rows, by_head = lax.optimization_barrier((own_rows, by_head))
    latent_in = placed_weights(by_head, columns * cut, columns, share, depth, step)

    grid = (*(lax.axis_size(name) for name in ROWS), columns)
    here = tuple(lax.axis_index(name) for name in ROWS)
    all_counts = jnp.stack(
        [by_head[:, columns * cut + (k + 1) * step - 1, 0] for k in range(columns)], axis=1
    )
    all_counts = all_counts.astype(i32).reshape(*grid)
    all_counts = lax.dynamic_slice(jnp.tile(all_counts, (2, 2, 1)), (*here, 0), grid)
    order = sum(
        stride
        * lax.bitwise_and(lax.broadcasted_iota(i32, grid, dim) + start, grid[dim] - 1)
        for dim, stride, start in ((0, grid[1], here[0]), (1, 1, here[1]), (2, groups, 0))
    ).reshape(-1)
    flat_counts = all_counts.reshape(-1)
    offsets = jnp.sum(jnp.where(order[None, :] < order[:, None], flat_counts[None, :], 0), axis=1)
    position = (offsets[:columns, None] + slot_ids[None, :]).reshape(-1)
    key_pos = jnp.where(
        slot_ids[None, :] < flat_counts[:, None], offsets[:, None] + slot_ids[None, :], far_position
    ).reshape(groups, columns * slots)
    halfway = HD // 2
    frequency = jnp.power(rope_base, -2.0 * jnp.arange(halfway, dtype=f32) / HD)
    angles = position.astype(f32)[:, None] * frequency[None, :]
    cosine, sine = (jnp.cos(angles), jnp.sin(angles))
    cosine = jnp.concatenate([cosine, cosine], axis=1)
    sine = jnp.concatenate([-sine, sine], axis=1)

    queries, keys, values = latent_heads(own_rows, other_rows, latent_in, cosine, sine)
    keys = around_ring(jnp.stack(around_ring(keys, RY)), RX)
    values = around_ring(jnp.stack(around_ring(values, RX)), RY)
    heads = latent_attention(queries, keys, values, position[:, None], key_pos)

    kept, sent = partial_outputs(lax.all_gather(heads, ZL), by_head)
    partial = added_outputs(kept, swapped(sent, CO))
    places = [(a, h, c) for a in range(columns) for h in range(2) for c in range(2)]
    partial = [
        lax.ppermute(
            piece,
            COLUMN,
            [(a * tensor + 2 * h + c, (2 * c + (h ^ i)) * tensor + a) for a, h, c in places],
        )
        for i, piece in enumerate(partial)
    ]
    latent = summed_outputs(partial, patches, counts)
    return (encoded, latent)


def solution(mesh):
    finer = Mesh(mesh.devices.reshape(4, 4, 4, 2, 2), (*SEQ, *TP))
    in_specs = (
        P(SEQ, None),
        P(),
        P(None, None, TP),
        P(TP, None),
        P(SEQ, None),
        P(SEQ),
        P(None, TP),
        P(None, None, TP),
        P(),
        P(None, SEQ, TP),
        P(TP, SEQ),
    )
    out_specs = (P(SEQ, None), P(SEQ, TP))
    return jax.shard_map(
        shards, mesh=finer, in_specs=in_specs, out_specs=out_specs, check_vma=False
    )
```

```python
import math

import jax
import jax.numpy as jnp
from jax import lax
from jax.experimental import pallas as pl
from jax.experimental.pallas import tpu as pltpu
from jax.sharding import Mesh
from jax.sharding import PartitionSpec as P

EH = 64
HD = 128
WIN = 512
SPILL = 8
EDGE = 16
ZL, RX, RY, ZH, CO = ("z_lo", "ring_x", "ring_y", "z_hi", "core")
SEQ = (ZL, RX, RY)
TP = (ZH, CO)
ROWS = (RX, RY)
COLUMN = (ZL, ZH, CO)

epsilon = 1e-05
rope_base = 500000.0
far_position = 1 << 30
bf16 = jnp.bfloat16
f32 = jnp.float32
i32 = jnp.int32
NT = (((1,), (1,)), ((), ()))


def shifted(value, axis, steps):
    count = lax.axis_size(axis)
    leading, last = (max(0, -steps), min(count, count - steps))
    return lax.ppermute(value, axis, [(source, source + steps) for source in range(leading, last)])


def exchanged(pieces, axis):
    return lax.all_to_all(pieces, axis, split_axis=0, concat_axis=0, tiled=True)


def swapped(value, axis):
    return lax.ppermute(value, axis, [(0, 1), (1, 0)])


def gathered(value, axis):
    return exchanged(jnp.broadcast_to(value, (lax.axis_size(axis), *value.shape)), axis)


def around_ring(value, axis):
    count = lax.axis_size(axis)
    return [value] + [
        lax.ppermute(value, axis, [((i + k) % count, i) for i in range(count)])
        for k in range(1, count)
    ]


def near_ring(value, axis):
    count = lax.axis_size(axis)

    def moved(part, step):
        return lax.ppermute(part, axis, [(i, (i + step) % count) for i in range(count)])

    up, down = (moved(value, 1), moved(value, -1))
    half = value.shape[0] // 2
    return [
        (value, 0, 0),
        (up, count - 1, 0),
        (down, 1, 0),
        (moved(up[:half], 1), 2, 0),
        (moved(down[half:], -1), 2, half),
    ]


def around_column(value):
    low, high = (lax.axis_size(ZL), lax.axis_size(ZH))
    count = low * high

    def moved(part, step):
        named = lambda z: z % count % low * high + z % count // low
        return lax.ppermute(part, (ZL, ZH), [(named(z), named(z + step)) for z in range(count)])

    pieces = [(value, 0, 0)]
    up = down = value
    for step in range(1, count // 2):
        up, down = (moved(up, 1), moved(down, -1))
        pieces += [(up, count - step, 0), (down, step, 0)]
    half = value.shape[0] // 2
    pieces += [(moved(up[:half], 1), count // 2, 0), (moved(down[half:], -1), count // 2, half)]
    return pieces


def on_chip(kernel, outs, scratch=(), limit=16, **extra):
    return pl.pallas_call(
        kernel,
        out_shape=outs,
        scratch_shapes=list(scratch),
        compiler_params=pltpu.CompilerParams(vmem_limit_bytes=limit << 20),
        cost_estimate=pl.CostEstimate(flops=1 << 20, transcendentals=0, bytes_accessed=1 << 20),
        **extra,
    )


def blank(shape, dtype=bf16):
    return jax.ShapeDtypeStruct(shape, dtype)


def encoder_heads(states, gain, weights):
    rows, width = states.shape
    share, _, inner = weights.shape

    def kernel(states_ref, gain_ref, weights_ref, query_ref, keys_values_ref):
        values = states_ref[...].astype(f32)
        factor = lax.rsqrt(jnp.mean(values * values, axis=-1, keepdims=True) + epsilon)
        normed = (values * factor * gain_ref[...].astype(f32)).astype(bf16)
        for i in range(1, share):
            keys_values_ref[:, (i - 1) * inner : i * inner] = jnp.dot(
                normed, weights_ref[i], preferred_element_type=f32
            ).astype(bf16)
        query_ref[...] = jnp.dot(normed, weights_ref[0], preferred_element_type=f32).astype(bf16)

    return on_chip(kernel, [blank((rows, inner)), blank((rows, (share - 1) * inner))])(
        states, gain.reshape(1, width), weights
    )


def encoder_attention(own_q, more_q, far, near, own, more, anchor):
    rows, width = own_q.shape
    total = rows + EDGE
    spans = WIN + total
    padded = -(-spans // 128) * 128

    def kernel(anchor_ref, q_ref, mq_ref, far_ref, near_ref, own_ref, more_ref, out_ref, held):
        at = 0
        for part in (far_ref, near_ref, own_ref, more_ref):
            held[at : at + part.shape[0], :] = part[...]
            at += part.shape[0]
        held[at:, :] = jnp.zeros((padded - at, 2 * width), bf16)
        queries = jnp.concatenate([q_ref[...], mq_ref[...]], axis=0)
        row = lax.broadcasted_iota(i32, (total, padded), 0)
        column = lax.broadcasted_iota(i32, (total, padded), 1)
        allowed = (
            (column - WIN <= row) & (column > row) & (column >= WIN - anchor_ref[0])
        )
        lane = lax.broadcasted_iota(i32, (total, HD), 1)
        for pair in range(width // HD):
            span = slice(pair * HD, (pair + 1) * HD)
            keys = held[:, span]
            values = held[:, width + pair * HD : width + (pair + 1) * HD]
            both = queries[:, span]
            done = None
            for side in range(HD // EH):
                mine = (lane >= side * EH) & (lane < (side + 1) * EH)
                query = jnp.where(mine, both, jnp.zeros_like(both))
                scores = lax.dot_general(query, keys, NT, preferred_element_type=f32)
                scores = jnp.where(allowed, scores * (1.0 / math.sqrt(EH)), -1e30)
                largest = jnp.max(scores, axis=-1, keepdims=True)
                raised = jnp.where(allowed, jnp.exp(scores - largest), 0.0)
                weights = (raised / jnp.maximum(jnp.sum(raised, axis=-1, keepdims=True), 1e-30))
                result = jnp.dot(weights.astype(bf16), values, preferred_element_type=f32)
                done = result if done is None else jnp.where(mine, result, done)
            out_ref[:, span] = done.astype(bf16)

    whole = pl.BlockSpec(memory_space=pltpu.VMEM)
    return on_chip(
        kernel,
        blank((total, width)),
        [pltpu.VMEM((padded, 2 * width), bf16)],
        in_specs=[pl.BlockSpec(memory_space=pltpu.SMEM)] + [whole] * 6,
        out_specs=whole,
    )(anchor.reshape(1), own_q, more_q, far, near, own, more)


def encoder_output(states, edge, attended, parts):
    rows, width = states.shape

    def kernel(states_ref, edge_ref, attended_ref, *refs):
        *part_refs, out_ref = refs
        here = lax.axis_index(TP)
        total = jnp.zeros((rows + EDGE, width), f32)
        for (_, turn, start), part in zip(parts, part_refs):
            deep = part.shape[0]
            piece = attended_ref[lax.bitwise_xor(here, turn), :, start : start + deep]
            total += jnp.dot(piece, part[...], preferred_element_type=f32)
        out_ref[:rows, :] = (states_ref[...].astype(f32) + total[:rows]).astype(bf16)
        out_ref[rows:, :] = (edge_ref[...].astype(f32) + total[rows:]).astype(bf16)

    return on_chip(kernel, blank((rows + EDGE, width)))(
        states, edge, attended, *(part for part, *_ in parts)
    )


def patch_block(extended, bounds, lift, cross_kv):
    spans, width = extended.shape
    slots = bounds.shape[0]
    wide = 2 * HD

    def kernel(extended_ref, bounds_ref, lift_ref, cross_ref, out_ref, pooled_ref):
        column = lax.broadcasted_iota(i32, (slots, spans), 1)
        first, after, seen, used = (bounds_ref[:, k : k + 1] for k in range(4))
        rows = extended_ref[...]

        @pl.when(pl.program_id(0) == 0)
        def _():
            inside = (column >= first) & (column < after)
            member = jnp.where(inside, 1.0, 0.0).astype(bf16)
            lengths = jnp.maximum(after - first, 1).astype(f32)
            totals = jnp.dot(member, rows, preferred_element_type=f32)
            pooled_ref[...] = (totals / lengths).astype(bf16)

        allowed = (column >= first) & (column < seen)
        lifted = jnp.dot(pooled_ref[...], lift_ref[...], preferred_element_type=f32)
        query = lifted.astype(bf16)
        keys = jnp.dot(rows, cross_ref[0], preferred_element_type=f32).astype(bf16)
        values = jnp.dot(rows, cross_ref[1], preferred_element_type=f32).astype(bf16)
        for head in range(wide // HD):
            span = slice(head * HD, (head + 1) * HD)
            scores = lax.dot_general(
                query[:, span], keys[:, span], NT, preferred_element_type=f32
            ) * (1.0 / math.sqrt(HD))
            scores = jnp.where(allowed, scores, -1e30)
            largest = jnp.max(scores, axis=-1, keepdims=True)
            raised = jnp.where(allowed, jnp.exp(scores - largest), 0.0)
            weights = (raised / jnp.sum(raised, axis=-1, keepdims=True)).astype(bf16)
            crossed = jnp.dot(weights, values[:, span], preferred_element_type=f32)
            total = jnp.where(used > 0, lifted[:, span] + crossed, 0.0)
            out_ref[:, span] = total.astype(bf16)

    return on_chip(
        kernel,
        blank((slots, lift.shape[1])),
        [pltpu.VMEM((slots, width), bf16)],
        grid=(lift.shape[1] // wide,),
        in_specs=[
            pl.BlockSpec((spans, width), lambda i: (0, 0)),
            pl.BlockSpec(bounds.shape, lambda i: (0, 0)),
            pl.BlockSpec((width, wide), lambda i: (0, i)),
            pl.BlockSpec((2, width, wide), lambda i: (0, 0, i)),
        ],
        out_specs=pl.BlockSpec((slots, wide), lambda i: (0, i)),
    )(extended, bounds, lift, cross_kv)


def placed_rows(pieces):
    rows, width = pieces[0][0].shape
    low, high = (lax.axis_size(ZL), lax.axis_size(ZH))

    def kernel(*refs):
        *parts, out_ref = refs
        here = lax.axis_index(ZH) * low + lax.axis_index(ZL)
        for part, (_, distance, shift) in zip(parts, pieces):
            z = lax.bitwise_and(here + distance, low * high - 1)
            across = lax.bitwise_and(z, low - 1) * rows + shift
            down = lax.shift_right_logical(z, low.bit_length() - 1) * width
            out_ref[
                pl.ds(pl.multiple_of(across, 16), part.shape[0]),
                pl.ds(pl.multiple_of(down, 128), width),
            ] = part[...]

    return on_chip(kernel, blank((low * rows, high * width)))(*(part for part, *_ in pieces))


def head_weights(lat_qkv, gains, counts):
    share, depth, inner = lat_qkv.shape
    step = share * depth + EDGE
    heads = inner // HD

    def kernel(count_ref, weights_ref, gains_ref, out_ref):
        block = lax.axis_index(SEQ)
        gains = gains_ref[...].astype(f32)
        mine = lax.broadcasted_iota(i32, gains.shape, 0) == block
        row = jnp.sum(jnp.where(mine, gains, 0.0), axis=0, keepdims=True)
        square = (depth, depth)
        same = lax.broadcasted_iota(i32, square, 0) == lax.broadcasted_iota(i32, square, 1)
        column = jnp.sum(jnp.where(same, row, 0.0), axis=1, keepdims=True)
        mark = jnp.full((EDGE, HD), count_ref[0].astype(f32)).astype(bf16)
        for i in range(share):
            scaled = (weights_ref[i].astype(f32) * column).astype(bf16)
            for k in range(heads):
                out_ref[k, i * depth : (i + 1) * depth, :] = scaled[:, k * HD : (k + 1) * HD]
        for k in range(heads):
            out_ref[k, share * depth :, :] = mark

    whole = pl.BlockSpec(memory_space=pltpu.VMEM)
    return on_chip(
        kernel,
        blank((heads, step, HD)),
        in_specs=[pl.BlockSpec(memory_space=pltpu.SMEM), whole, whole],
        out_specs=whole,
    )(counts, lat_qkv, gains)


def copied_weights(out_part, by_head, copies):
    cut, deep = out_part.shape
    heads, step, _ = by_head.shape
    total = heads * (cut + step)

    def kernel(out_part_ref, by_head_ref, out_ref):
        for k in range(heads):
            out_ref[0, k * cut : (k + 1) * cut, :] = out_part_ref[:, k * HD : (k + 1) * HD]
            start = heads * cut + k * step
            out_ref[0, start : start + step, :] = by_head_ref[k]

    return on_chip(
        kernel,
        blank((copies, total, HD)),
        grid=(copies,),
        in_specs=[
            pl.BlockSpec(out_part.shape, lambda i: (0, 0)),
            pl.BlockSpec(by_head.shape, lambda i: (0, 0, 0)),
        ],
        out_specs=pl.BlockSpec((1, total, HD), lambda i: (i, 0, 0)),
    )(out_part, by_head)


def placed_weights(gathered_weights, first, columns, share, depth, step):
    groups = gathered_weights.shape[0]

    def kernel(weights_ref, out_ref):
        core = lax.axis_index(CO)
        for g in range(groups):
            for side in range(2):
                for high in range(columns // 2):
                    t = 2 * high + lax.bitwise_xor(core, side)
                    for i in range(share):
                        start = pl.multiple_of(first + t * step + i * depth, 16)
                        out_ref[
                            side, high, g * depth : (g + 1) * depth, i * HD : (i + 1) * HD
                        ] = weights_ref[g, pl.ds(start, depth), :]

    return on_chip(kernel, blank((2, columns // 2, groups * depth, share * HD)))(
        gathered_weights
    )


def latent_heads(own_rows, other_rows, weights, cosine, sine):
    rows, width = own_rows.shape
    full = 2 * width

    def kernel(own_ref, other_ref, weights_ref, cosine_ref, sine_ref, q_ref, k_ref, v_ref):
        squares = jnp.zeros((rows, 1), f32)
        total = jnp.zeros((rows, 3 * HD), f32)
        half = width // 2
        for side, part in enumerate((own_ref, other_ref)):
            for high in range(2):
                values = part[:, high * half : (high + 1) * half]
                wide = values.astype(f32)
                squares += jnp.sum(wide * wide, axis=1, keepdims=True)
                total += jnp.dot(values, weights_ref[side, high], preferred_element_type=f32)
        total = total * lax.rsqrt(squares / full + epsilon)
        for which, out_ref in enumerate((q_ref, k_ref)):
            value = total[:, which * HD : (which + 1) * HD]
            turned = value * cosine_ref[...] + pltpu.roll(value, HD // 2, 1) * sine_ref[...]
            out_ref[...] = turned.astype(bf16)
        v_ref[...] = total[:, 2 * HD :].astype(bf16)

    return on_chip(kernel, [blank((rows, HD))] * 3)(
        own_rows, other_rows, weights, cosine, sine
    )


def latent_attention(queries, keys, values, position, key_pos):
    rows = queries.shape[0]
    n_x, n_y = (len(keys), len(values))

    def kernel(*refs):
        q_ref, pos_ref, key_pos_ref = refs[:3]
        key_refs, value_refs = (refs[3 : 3 + n_x], refs[3 + n_x : 3 + n_x + n_y])
        out_ref, held = refs[3 + n_x + n_y :]
        query = q_ref[...]
        position = pos_ref[...]
        top = jnp.full((rows, rows), -1e30, f32)
        for x in range(n_x):
            for y in range(n_y):
                scores = lax.dot_general(
                    query, key_refs[x][y], NT, preferred_element_type=f32
                ) * (1.0 / math.sqrt(HD))
                allowed = key_pos_ref[x * n_y + y : x * n_y + y + 1, :] <= position
                scores = jnp.where(allowed, scores, -1e30)
                held[x * n_y + y] = scores
                top = jnp.maximum(top, scores)
        largest = jnp.max(top, axis=-1, keepdims=True)
        total = jnp.zeros((rows, rows), f32)
        weighted = jnp.zeros((rows, HD), f32)
        for x in range(n_x):
            for y in range(n_y):
                raised = jnp.exp(held[x * n_y + y] - largest)
                total += raised
                weighted += jnp.dot(
                    raised.astype(bf16), value_refs[y][x], preferred_element_type=f32
                )
        out_ref[...] = (weighted / jnp.sum(total, axis=-1, keepdims=True)).astype(bf16)

    return on_chip(
        kernel, blank((rows, HD)), [pltpu.VMEM((n_x * n_y, rows, rows), f32)]
    )(queries, position, key_pos, *keys, *values)


def partial_outputs(heads, weights):
    columns, rows, _ = heads.shape
    groups = weights.shape[0]
    slots = rows // columns
    cut = slots
    pair = columns // 2

    def kernel(heads_ref, weights_ref, kept_ref, sent_ref):
        core, high = (lax.axis_index(CO), lax.axis_index(ZH))
        flat = [
            weights_ref[:, zl * cut : (zl + 1) * cut, :].reshape(groups * cut, HD)
            for zl in range(columns)
        ]
        for side, out_ref in enumerate((kept_ref, sent_ref)):
            for i in range(pair):
                block = pair * lax.bitwise_xor(core, side) + lax.bitwise_xor(high, i)
                span = pl.ds(pl.multiple_of(block * slots, slots), slots)
                total = jnp.zeros((slots, groups * cut), f32)
                for zl in range(columns):
                    total += lax.dot_general(
                        heads_ref[zl, span, :], flat[zl], NT, preferred_element_type=f32
                    )
                out_ref[i] = total.astype(out_ref.dtype)

    block = (groups, columns * cut, HD)
    shape = (pair, slots, groups * cut)
    whole = pl.BlockSpec(shape, lambda i: (0, 0, 0))
    return on_chip(
        kernel,
        [blank(shape, f32), blank(shape)],
        grid=(1,),
        in_specs=[
            pl.BlockSpec(heads.shape, lambda i: (0, 0, 0)),
            pl.BlockSpec(block, lambda i: (0, 0, 0)),
        ],
        out_specs=[whole, whole],
    )(heads, weights)


def added_outputs(kept, received):
    pair = kept.shape[0]

    def kernel(kept_ref, received_ref, *out_refs):
        for i, out_ref in enumerate(out_refs):
            out_ref[...] = (kept_ref[i] + received_ref[i].astype(f32)).astype(bf16)

    return on_chip(kernel, [blank(kept.shape[1:])] * pair)(kept, received)


def summed_outputs(pieces, patches, counts):
    def kernel(count_ref, patches_ref, *refs):
        *piece_refs, out_ref = refs
        total = patches_ref[...].astype(f32)
        for piece in piece_refs:
            total += piece[...].astype(f32)
        used = lax.broadcasted_iota(i32, total.shape, 0) < count_ref[0]
        out_ref[...] = jnp.where(used, total, 0.0).astype(bf16)

    whole = pl.BlockSpec(memory_space=pltpu.VMEM)
    return on_chip(
        kernel,
        blank(patches.shape),
        in_specs=[pl.BlockSpec(memory_space=pltpu.SMEM)] + [whole] * (1 + len(pieces)),
        out_specs=whole,
    )(counts, patches, *pieces)


def shards(
    byte_states,
    enc_gain,
    enc_qkv,
    enc_proj_out,
    starts,
    counts,
    lift,
    cross_kv,
    latent_gain,
    lat_qkv,
    lat_proj_out,
):
    byte_rows, byte_width = byte_states.shape
    slots = starts.shape[1]
    columns = lax.axis_size(ZL)
    tensor = lax.axis_size(TP)
    groups = lax.axis_size(ROWS)
    block = lax.axis_index(SEQ)
    anchor = block * byte_rows
    local_starts = starts[0]
    patch_count = counts[0]
    slot_ids = jnp.arange(slots, dtype=i32)
    in_use = slot_ids < patch_count

    own_q, own_kv = encoder_heads(byte_states, enc_gain, enc_qkv)
    far_kv = shifted(own_kv, SEQ, 2)
    near_kv = shifted(own_kv, SEQ, 1)

    first_local = (local_starts[0] - anchor).astype(bf16)
    edge = jnp.concatenate(
        [
            byte_states[:SPILL],
            jnp.broadcast_to(first_local, (EDGE - SPILL, byte_width)),
        ],
        axis=0,
    )
    edge = shifted(edge, SEQ, -1)

    share, depth, inner = lat_qkv.shape
    step = share * depth + EDGE
    by_head = head_weights(lat_qkv, latent_gain.reshape(-1, depth), counts)
    by_head = exchanged(by_head, ZL)
    cut = lat_proj_out.shape[1]

    most = enc_proj_out.shape[0] // 2
    own_q, late = lax.optimization_barrier((own_q, enc_proj_out))
    high_a, high_b = (swapped(part, ZH) for part in (enc_proj_out[:most], late[most:]))
    out_side = swapped(enc_proj_out, CO)

    near_kv, far_kv, edge, out_side, high_a = lax.optimization_barrier(
        (near_kv, far_kv, edge, out_side, high_a)
    )
    next_first = edge[SPILL, 0].astype(i32)
    more_q, more_kv = encoder_heads(edge, enc_gain, enc_qkv)
    attended = encoder_attention(own_q, more_q, far_kv, near_kv, own_kv, more_kv, anchor)
    both_a = swapped(high_a, CO)
    attended, by_head, both_a = lax.optimization_barrier((attended, by_head, both_a))
    by_head = exchanged(copied_weights(lat_proj_out.T, by_head, groups), ROWS)
    attended = lax.all_gather(attended, TP)
    attended, high_b = lax.optimization_barrier((attended, high_b))
    both_b = swapped(high_b, CO)
    extended = encoder_output(
        byte_states,
        edge,
        attended,
        (
            (enc_proj_out, 0, 0),
            (out_side, 1, 0),
            (high_a, 2, 0),
            (both_a, 3, 0),
            (high_b, 2, most),
            (both_b, 3, most),
        ),
    )
    encoded = extended[:byte_rows]

    following = jnp.concatenate([local_starts[1:], jnp.zeros((1,), i32)])
    patch_end = jnp.where(slot_ids + 1 < patch_count, following, anchor + byte_rows + next_first)
    first, after = (jnp.where(in_use, end - anchor, 0) for end in (local_starts, patch_end))
    used = in_use.astype(i32)
    bounds = jnp.stack([first, after, jnp.where(in_use, after, 1), used], axis=1)
    patches = patch_block(extended, bounds, lift, cross_kv)
    own_rows = placed_rows(around_column(patches))
    other_rows = swapped(own_rows, CO)
    own_rows, by_head = lax.optimization_barrier((own_rows, by_head))
    latent_in = placed_weights(by_head, columns * cut, columns, share, depth, step)

    grid = (*(lax.axis_size(name) for name in ROWS), columns)
    here = tuple(lax.axis_index(name) for name in ROWS)
    all_counts = jnp.stack(
        [by_head[:, columns * cut + (k + 1) * step - 1, 0] for k in range(columns)], axis=1
    )
    all_counts = all_counts.astype(i32).reshape(*grid)
    all_counts = lax.dynamic_slice(jnp.tile(all_counts, (2, 2, 1)), (*here, 0), grid)
    order = sum(
        stride
        * lax.bitwise_and(lax.broadcasted_iota(i32, grid, dim) + start, grid[dim] - 1)
        for dim, stride, start in ((0, grid[1], here[0]), (1, 1, here[1]), (2, groups, 0))
    ).reshape(-1)
    flat_counts = all_counts.reshape(-1)
    offsets = jnp.sum(jnp.where(order[None, :] < order[:, None], flat_counts[None, :], 0), axis=1)
    position = (offsets[:columns, None] + slot_ids[None, :]).reshape(-1)
    key_pos = jnp.where(
        slot_ids[None, :] < flat_counts[:, None], offsets[:, None] + slot_ids[None, :], far_position
    ).reshape(groups, columns * slots)
    halfway = HD // 2
    frequency = jnp.power(rope_base, -2.0 * jnp.arange(halfway, dtype=f32) / HD)
    angles = position.astype(f32)[:, None] * frequency[None, :]
    cosine, sine = (jnp.cos(angles), jnp.sin(angles))
    cosine = jnp.concatenate([cosine, cosine], axis=1)
    sine = jnp.concatenate([-sine, sine], axis=1)

    queries, keys, values = latent_heads(own_rows, other_rows, latent_in, cosine, sine)
    keys = around_ring(jnp.stack(around_ring(keys, RY)), RX)
    values = around_ring(jnp.stack(around_ring(values, RX)), RY)
    heads = latent_attention(queries, keys, values, position[:, None], key_pos)

    kept, sent = partial_outputs(lax.all_gather(heads, ZL), by_head)
    partial = added_outputs(kept, swapped(sent, CO))
    places = [(a, h, c) for a in range(columns) for h in range(2) for c in range(2)]
    partial = [
        lax.ppermute(
            piece,
            COLUMN,
            [(a * tensor + 2 * h + c, (2 * c + (h ^ i)) * tensor + a) for a, h, c in places],
        )
        for i, piece in enumerate(partial)
    ]
    latent = summed_outputs(partial, patches, counts)
    return (encoded, latent)


def solution(mesh):
    finer = Mesh(mesh.devices.reshape(4, 4, 4, 2, 2), (*SEQ, *TP))
    in_specs = (
        P(SEQ, None),
        P(),
        P(None, None, TP),
        P(TP, None),
        P(SEQ, None),
        P(SEQ),
        P(None, TP),
        P(None, None, TP),
        P(),
        P(None, SEQ, TP),
        P(TP, SEQ),
    )
    out_specs = (P(SEQ, None), P(SEQ, TP))
    return jax.shard_map(
        shards, mesh=finer, in_specs=in_specs, out_specs=out_specs, check_vma=False
    )
```

```python
import math

import jax
import jax.numpy as jnp
from jax import lax
from jax.experimental import pallas as pl
from jax.experimental.pallas import tpu as pltpu
from jax.sharding import Mesh
from jax.sharding import PartitionSpec as P

EH = 64
HD = 128
WIN = 512
SPILL = 8
EDGE = 16
ZL, RX, RY, ZH, CO = ("z_lo", "ring_x", "ring_y", "z_hi", "core")
SEQ = (ZL, RX, RY)
TP = (ZH, CO)
ROWS = (RX, RY)
COLUMN = (ZL, ZH, CO)

epsilon = 1e-05
rope_base = 500000.0
far_position = 1 << 30
bf16 = jnp.bfloat16
f32 = jnp.float32
i32 = jnp.int32
NT = (((1,), (1,)), ((), ()))


def shifted(value, axis, steps):
    count = lax.axis_size(axis)
    leading, last = (max(0, -steps), min(count, count - steps))
    return lax.ppermute(value, axis, [(source, source + steps) for source in range(leading, last)])


def exchanged(pieces, axis):
    return lax.all_to_all(pieces, axis, split_axis=0, concat_axis=0, tiled=True)


def swapped(value, axis):
    return lax.ppermute(value, axis, [(0, 1), (1, 0)])


def gathered(value, axis):
    return exchanged(jnp.broadcast_to(value, (lax.axis_size(axis), *value.shape)), axis)


def around_ring(value, axis):
    count = lax.axis_size(axis)
    return [value] + [
        lax.ppermute(value, axis, [((i + k) % count, i) for i in range(count)])
        for k in range(1, count)
    ]


def near_ring(value, axis):
    count = lax.axis_size(axis)

    def moved(part, step):
        return lax.ppermute(part, axis, [(i, (i + step) % count) for i in range(count)])

    up, down = (moved(value, 1), moved(value, -1))
    half = value.shape[0] // 2
    return [
        (value, 0, 0),
        (up, count - 1, 0),
        (down, 1, 0),
        (moved(up[:half], 1), 2, 0),
        (moved(down[half:], -1), 2, half),
    ]


def around_column(value):
    low, high = (lax.axis_size(ZL), lax.axis_size(ZH))
    count = low * high

    def moved(part, step):
        named = lambda z: z % count % low * high + z % count // low
        return lax.ppermute(part, (ZL, ZH), [(named(z), named(z + step)) for z in range(count)])

    pieces = [(value, 0, 0)]
    up = down = value
    for step in range(1, count // 2):
        up, down = (moved(up, 1), moved(down, -1))
        pieces += [(up, count - step, 0), (down, step, 0)]
    half = value.shape[0] // 2
    pieces += [(moved(up[:half], 1), count // 2, 0), (moved(down[half:], -1), count // 2, half)]
    return pieces


def on_chip(kernel, outs, scratch=(), limit=16, **extra):
    return pl.pallas_call(
        kernel,
        out_shape=outs,
        scratch_shapes=list(scratch),
        compiler_params=pltpu.CompilerParams(vmem_limit_bytes=limit << 20),
        cost_estimate=pl.CostEstimate(flops=1 << 20, transcendentals=0, bytes_accessed=1 << 20),
        **extra,
    )


def blank(shape, dtype=bf16):
    return jax.ShapeDtypeStruct(shape, dtype)


def encoder_heads(states, gain, weights):
    rows, width = states.shape
    share, _, inner = weights.shape

    def kernel(states_ref, gain_ref, weights_ref, query_ref, keys_values_ref):
        values = states_ref[...].astype(f32)
        factor = lax.rsqrt(jnp.mean(values * values, axis=-1, keepdims=True) + epsilon)
        normed = (values * factor * gain_ref[...].astype(f32)).astype(bf16)
        for i in range(1, share):
            keys_values_ref[:, (i - 1) * inner : i * inner] = jnp.dot(
                normed, weights_ref[i], preferred_element_type=f32
            ).astype(bf16)
        query_ref[...] = jnp.dot(normed, weights_ref[0], preferred_element_type=f32).astype(bf16)

    return on_chip(kernel, [blank((rows, inner)), blank((rows, (share - 1) * inner))])(
        states, gain.reshape(1, width), weights
    )


def encoder_attention(own_q, more_q, far, near, own, more, anchor):
    rows, width = own_q.shape
    total = rows + EDGE
    spans = WIN + total
    padded = -(-spans // 128) * 128

    def kernel(anchor_ref, q_ref, mq_ref, far_ref, near_ref, own_ref, more_ref, out_ref, held):
        at = 0
        for part in (far_ref, near_ref, own_ref, more_ref):
            held[at : at + part.shape[0], :] = part[...]
            at += part.shape[0]
        held[at:, :] = jnp.zeros((padded - at, 2 * width), bf16)
        queries = jnp.concatenate([q_ref[...], mq_ref[...]], axis=0)
        row = lax.broadcasted_iota(i32, (total, padded), 0)
        column = lax.broadcasted_iota(i32, (total, padded), 1)
        allowed = (
            (column - WIN <= row) & (column > row) & (column >= WIN - anchor_ref[0])
        )
        lane = lax.broadcasted_iota(i32, (total, HD), 1)
        for pair in range(width // HD):
            span = slice(pair * HD, (pair + 1) * HD)
            keys = held[:, span]
            values = held[:, width + pair * HD : width + (pair + 1) * HD]
            both = queries[:, span]
            done = None
            for side in range(HD // EH):
                mine = (lane >= side * EH) & (lane < (side + 1) * EH)
                query = jnp.where(mine, both, jnp.zeros_like(both))
                scores = lax.dot_general(query, keys, NT, preferred_element_type=f32)
                scores = jnp.where(allowed, scores * (1.0 / math.sqrt(EH)), -1e30)
                largest = jnp.max(scores, axis=-1, keepdims=True)
                raised = jnp.where(allowed, jnp.exp(scores - largest), 0.0)
                weights = (raised / jnp.maximum(jnp.sum(raised, axis=-1, keepdims=True), 1e-30))
                result = jnp.dot(weights.astype(bf16), values, preferred_element_type=f32)
                done = result if done is None else jnp.where(mine, result, done)
            out_ref[:, span] = done.astype(bf16)

    whole = pl.BlockSpec(memory_space=pltpu.VMEM)
    return on_chip(
        kernel,
        blank((total, width)),
        [pltpu.VMEM((padded, 2 * width), bf16)],
        in_specs=[pl.BlockSpec(memory_space=pltpu.SMEM)] + [whole] * 6,
        out_specs=whole,
    )(anchor.reshape(1), own_q, more_q, far, near, own, more)


def encoder_output(states, edge, attended, parts):
    rows, width = states.shape

    def kernel(states_ref, edge_ref, attended_ref, *refs):
        *part_refs, out_ref = refs
        here = lax.axis_index(TP)
        total = jnp.zeros((rows + EDGE, width), f32)
        for (_, turn, start), part in zip(parts, part_refs):
            deep = part.shape[0]
            piece = attended_ref[lax.bitwise_xor(here, turn), :, start : start + deep]
            total += jnp.dot(piece, part[...], preferred_element_type=f32)
        out_ref[:rows, :] = (states_ref[...].astype(f32) + total[:rows]).astype(bf16)
        out_ref[rows:, :] = (edge_ref[...].astype(f32) + total[rows:]).astype(bf16)

    return on_chip(kernel, blank((rows + EDGE, width)))(
        states, edge, attended, *(part for part, *_ in parts)
    )


def patch_block(extended, bounds, lift, cross_kv):
    spans, width = extended.shape
    slots = bounds.shape[0]
    wide = 2 * HD

    def kernel(extended_ref, bounds_ref, lift_ref, cross_ref, out_ref, pooled_ref):
        column = lax.broadcasted_iota(i32, (slots, spans), 1)
        first, after, seen, used = (bounds_ref[:, k : k + 1] for k in range(4))
        rows = extended_ref[...]

        @pl.when(pl.program_id(0) == 0)
        def _():
            inside = (column >= first) & (column < after)
            member = jnp.where(inside, 1.0, 0.0).astype(bf16)
            lengths = jnp.maximum(after - first, 1).astype(f32)
            totals = jnp.dot(member, rows, preferred_element_type=f32)
            pooled_ref[...] = (totals / lengths).astype(bf16)

        allowed = (column >= first) & (column < seen)
        lifted = jnp.dot(pooled_ref[...], lift_ref[...], preferred_element_type=f32)
        query = lifted.astype(bf16)
        keys = jnp.dot(rows, cross_ref[0], preferred_element_type=f32).astype(bf16)
        values = jnp.dot(rows, cross_ref[1], preferred_element_type=f32).astype(bf16)
        for head in range(wide // HD):
            span = slice(head * HD, (head + 1) * HD)
            scores = lax.dot_general(
                query[:, span], keys[:, span], NT, preferred_element_type=f32
            ) * (1.0 / math.sqrt(HD))
            scores = jnp.where(allowed, scores, -1e30)
            largest = jnp.max(scores, axis=-1, keepdims=True)
            raised = jnp.where(allowed, jnp.exp(scores - largest), 0.0)
            weights = (raised / jnp.sum(raised, axis=-1, keepdims=True)).astype(bf16)
            crossed = jnp.dot(weights, values[:, span], preferred_element_type=f32)
            total = jnp.where(used > 0, lifted[:, span] + crossed, 0.0)
            out_ref[:, span] = total.astype(bf16)

    return on_chip(
        kernel,
        blank((slots, lift.shape[1])),
        [pltpu.VMEM((slots, width), bf16)],
        grid=(lift.shape[1] // wide,),
        in_specs=[
            pl.BlockSpec((spans, width), lambda i: (0, 0)),
            pl.BlockSpec(bounds.shape, lambda i: (0, 0)),
            pl.BlockSpec((width, wide), lambda i: (0, i)),
            pl.BlockSpec((2, width, wide), lambda i: (0, 0, i)),
        ],
        out_specs=pl.BlockSpec((slots, wide), lambda i: (0, i)),
    )(
        extended,
        bounds,
        pltpu.with_memory_space_constraint(lift, pltpu.HBM),
        pltpu.with_memory_space_constraint(cross_kv, pltpu.HBM),
    )


def placed_rows(pieces):
    rows, width = pieces[0][0].shape
    low, high = (lax.axis_size(ZL), lax.axis_size(ZH))

    def kernel(*refs):
        *parts, out_ref = refs
        here = lax.axis_index(ZH) * low + lax.axis_index(ZL)
        for part, (_, distance, shift) in zip(parts, pieces):
            z = lax.bitwise_and(here + distance, low * high - 1)
            across = lax.bitwise_and(z, low - 1) * rows + shift
            down = lax.shift_right_logical(z, low.bit_length() - 1) * width
            out_ref[
                pl.ds(pl.multiple_of(across, 16), part.shape[0]),
                pl.ds(pl.multiple_of(down, 128), width),
            ] = part[...]

    return on_chip(kernel, blank((low * rows, high * width)))(*(part for part, *_ in pieces))


def head_weights(lat_qkv, gains, counts):
    share, depth, inner = lat_qkv.shape
    step = share * depth + EDGE
    heads = inner // HD

    def kernel(count_ref, weights_ref, gains_ref, out_ref):
        block = lax.axis_index(SEQ)
        gains = gains_ref[...].astype(f32)
        mine = lax.broadcasted_iota(i32, gains.shape, 0) == block
        row = jnp.sum(jnp.where(mine, gains, 0.0), axis=0, keepdims=True)
        square = (depth, depth)
        same = lax.broadcasted_iota(i32, square, 0) == lax.broadcasted_iota(i32, square, 1)
        column = jnp.sum(jnp.where(same, row, 0.0), axis=1, keepdims=True)
        mark = jnp.full((EDGE, HD), count_ref[0].astype(f32)).astype(bf16)
        for i in range(share):
            scaled = (weights_ref[i].astype(f32) * column).astype(bf16)
            for k in range(heads):
                out_ref[k, i * depth : (i + 1) * depth, :] = scaled[:, k * HD : (k + 1) * HD]
        for k in range(heads):
            out_ref[k, share * depth :, :] = mark

    whole = pl.BlockSpec(memory_space=pltpu.VMEM)
    return on_chip(
        kernel,
        blank((heads, step, HD)),
        in_specs=[pl.BlockSpec(memory_space=pltpu.SMEM), whole, whole],
        out_specs=whole,
    )(counts, lat_qkv, gains)


def copied_weights(out_part, by_head, copies):
    cut, deep = out_part.shape
    heads, step, _ = by_head.shape
    total = heads * (cut + step)

    def kernel(out_part_ref, by_head_ref, out_ref):
        for k in range(heads):
            out_ref[0, k * cut : (k + 1) * cut, :] = out_part_ref[:, k * HD : (k + 1) * HD]
            start = heads * cut + k * step
            out_ref[0, start : start + step, :] = by_head_ref[k]

    return on_chip(
        kernel,
        blank((copies, total, HD)),
        grid=(copies,),
        in_specs=[
            pl.BlockSpec(out_part.shape, lambda i: (0, 0)),
            pl.BlockSpec(by_head.shape, lambda i: (0, 0, 0)),
        ],
        out_specs=pl.BlockSpec((1, total, HD), lambda i: (i, 0, 0)),
    )(out_part, by_head)


def placed_weights(gathered_weights, first, columns, share, depth, step):
    groups = gathered_weights.shape[0]

    def kernel(weights_ref, out_ref):
        core = lax.axis_index(CO)
        for g in range(groups):
            for side in range(2):
                for high in range(columns // 2):
                    t = 2 * high + lax.bitwise_xor(core, side)
                    for i in range(share):
                        start = pl.multiple_of(first + t * step + i * depth, 16)
                        out_ref[
                            side, high, g * depth : (g + 1) * depth, i * HD : (i + 1) * HD
                        ] = weights_ref[g, pl.ds(start, depth), :]

    return on_chip(kernel, blank((2, columns // 2, groups * depth, share * HD)))(
        gathered_weights
    )


def latent_heads(own_rows, other_rows, weights, cosine, sine):
    rows, width = own_rows.shape
    full = 2 * width

    def kernel(own_ref, other_ref, weights_ref, cosine_ref, sine_ref, q_ref, k_ref, v_ref):
        squares = jnp.zeros((rows, 1), f32)
        total = jnp.zeros((rows, 3 * HD), f32)
        half = width // 2
        for side, part in enumerate((own_ref, other_ref)):
            for high in range(2):
                values = part[:, high * half : (high + 1) * half]
                wide = values.astype(f32)
                squares += jnp.sum(wide * wide, axis=1, keepdims=True)
                total += jnp.dot(values, weights_ref[side, high], preferred_element_type=f32)
        total = total * lax.rsqrt(squares / full + epsilon)
        for which, out_ref in enumerate((q_ref, k_ref)):
            value = total[:, which * HD : (which + 1) * HD]
            turned = value * cosine_ref[...] + pltpu.roll(value, HD // 2, 1) * sine_ref[...]
            out_ref[...] = turned.astype(bf16)
        v_ref[...] = total[:, 2 * HD :].astype(bf16)

    return on_chip(kernel, [blank((rows, HD))] * 3)(
        own_rows, other_rows, weights, cosine, sine
    )


def latent_attention(queries, keys, values, position, key_pos):
    rows = queries.shape[0]
    n_x, n_y = (len(keys), len(values))

    def kernel(*refs):
        q_ref, pos_ref, key_pos_ref = refs[:3]
        key_refs, value_refs = (refs[3 : 3 + n_x], refs[3 + n_x : 3 + n_x + n_y])
        out_ref, held = refs[3 + n_x + n_y :]
        query = q_ref[...]
        position = pos_ref[...]
        top = jnp.full((rows, rows), -1e30, f32)
        for x in range(n_x):
            for y in range(n_y):
                scores = lax.dot_general(
                    query, key_refs[x][y], NT, preferred_element_type=f32
                ) * (1.0 / math.sqrt(HD))
                allowed = key_pos_ref[x * n_y + y : x * n_y + y + 1, :] <= position
                scores = jnp.where(allowed, scores, -1e30)
                held[x * n_y + y] = scores
                top = jnp.maximum(top, scores)
        largest = jnp.max(top, axis=-1, keepdims=True)
        total = jnp.zeros((rows, rows), f32)
        weighted = jnp.zeros((rows, HD), f32)
        for x in range(n_x):
            for y in range(n_y):
                raised = jnp.exp(held[x * n_y + y] - largest)
                total += raised
                weighted += jnp.dot(
                    raised.astype(bf16), value_refs[y][x], preferred_element_type=f32
                )
        out_ref[...] = (weighted / jnp.sum(total, axis=-1, keepdims=True)).astype(bf16)

    return on_chip(
        kernel, blank((rows, HD)), [pltpu.VMEM((n_x * n_y, rows, rows), f32)]
    )(queries, position, key_pos, *keys, *values)


def partial_outputs(heads, weights):
    columns, rows, _ = heads.shape
    groups = weights.shape[0]
    slots = rows // columns
    cut = slots
    pair = columns // 2

    def kernel(heads_ref, weights_ref, kept_ref, sent_ref):
        core, high = (lax.axis_index(CO), lax.axis_index(ZH))
        flat = [
            weights_ref[:, zl * cut : (zl + 1) * cut, :].reshape(groups * cut, HD)
            for zl in range(columns)
        ]
        for side, out_ref in enumerate((kept_ref, sent_ref)):
            for i in range(pair):
                block = pair * lax.bitwise_xor(core, side) + lax.bitwise_xor(high, i)
                span = pl.ds(pl.multiple_of(block * slots, slots), slots)
                total = jnp.zeros((slots, groups * cut), f32)
                for zl in range(columns):
                    total += lax.dot_general(
                        heads_ref[zl, span, :], flat[zl], NT, preferred_element_type=f32
                    )
                out_ref[i] = total.astype(out_ref.dtype)

    block = (groups, columns * cut, HD)
    shape = (pair, slots, groups * cut)
    whole = pl.BlockSpec(shape, lambda i: (0, 0, 0))
    return on_chip(
        kernel,
        [blank(shape, f32), blank(shape)],
        grid=(1,),
        in_specs=[
            pl.BlockSpec(heads.shape, lambda i: (0, 0, 0)),
            pl.BlockSpec(block, lambda i: (0, 0, 0)),
        ],
        out_specs=[whole, whole],
    )(heads, weights)


def added_outputs(kept, received):
    pair = kept.shape[0]

    def kernel(kept_ref, received_ref, *out_refs):
        for i, out_ref in enumerate(out_refs):
            out_ref[...] = (kept_ref[i] + received_ref[i].astype(f32)).astype(bf16)

    return on_chip(kernel, [blank(kept.shape[1:])] * pair)(kept, received)


def summed_outputs(pieces, patches, counts):
    def kernel(count_ref, patches_ref, *refs):
        *piece_refs, out_ref = refs
        total = patches_ref[...].astype(f32)
        for piece in piece_refs:
            total += piece[...].astype(f32)
        used = lax.broadcasted_iota(i32, total.shape, 0) < count_ref[0]
        out_ref[...] = jnp.where(used, total, 0.0).astype(bf16)

    whole = pl.BlockSpec(memory_space=pltpu.VMEM)
    return on_chip(
        kernel,
        blank(patches.shape),
        in_specs=[pl.BlockSpec(memory_space=pltpu.SMEM)] + [whole] * (1 + len(pieces)),
        out_specs=whole,
    )(counts, patches, *pieces)


def shards(
    byte_states,
    enc_gain,
    enc_qkv,
    enc_proj_out,
    starts,
    counts,
    lift,
    cross_kv,
    latent_gain,
    lat_qkv,
    lat_proj_out,
):
    byte_rows, byte_width = byte_states.shape
    slots = starts.shape[1]
    columns = lax.axis_size(ZL)
    tensor = lax.axis_size(TP)
    groups = lax.axis_size(ROWS)
    block = lax.axis_index(SEQ)
    anchor = block * byte_rows
    local_starts = starts[0]
    patch_count = counts[0]
    slot_ids = jnp.arange(slots, dtype=i32)
    in_use = slot_ids < patch_count

    own_q, own_kv = encoder_heads(byte_states, enc_gain, enc_qkv)
    far_kv = shifted(own_kv, SEQ, 2)
    near_kv = shifted(own_kv, SEQ, 1)

    first_local = (local_starts[0] - anchor).astype(bf16)
    edge = jnp.concatenate(
        [
            byte_states[:SPILL],
            jnp.broadcast_to(first_local, (EDGE - SPILL, byte_width)),
        ],
        axis=0,
    )
    edge = shifted(edge, SEQ, -1)

    share, depth, inner = lat_qkv.shape
    step = share * depth + EDGE
    by_head = head_weights(lat_qkv, latent_gain.reshape(-1, depth), counts)
    by_head = exchanged(by_head, ZL)
    cut = lat_proj_out.shape[1]

    most = enc_proj_out.shape[0] // 2
    own_q, late = lax.optimization_barrier((own_q, enc_proj_out))
    high_a, high_b = (swapped(part, ZH) for part in (enc_proj_out[:most], late[most:]))
    out_side = swapped(enc_proj_out, CO)

    near_kv, far_kv, edge, out_side, high_a = lax.optimization_barrier(
        (near_kv, far_kv, edge, out_side, high_a)
    )
    next_first = edge[SPILL, 0].astype(i32)
    more_q, more_kv = encoder_heads(edge, enc_gain, enc_qkv)
    attended = encoder_attention(own_q, more_q, far_kv, near_kv, own_kv, more_kv, anchor)
    both_a = swapped(high_a, CO)
    attended, by_head, both_a = lax.optimization_barrier((attended, by_head, both_a))
    by_head = exchanged(copied_weights(lat_proj_out.T, by_head, groups), ROWS)
    attended = lax.all_gather(attended, TP)
    attended, high_b = lax.optimization_barrier((attended, high_b))
    both_b = swapped(high_b, CO)
    extended = encoder_output(
        byte_states,
        edge,
        attended,
        (
            (enc_proj_out, 0, 0),
            (out_side, 1, 0),
            (high_a, 2, 0),
            (both_a, 3, 0),
            (high_b, 2, most),
            (both_b, 3, most),
        ),
    )
    encoded = extended[:byte_rows]

    following = jnp.concatenate([local_starts[1:], jnp.zeros((1,), i32)])
    patch_end = jnp.where(slot_ids + 1 < patch_count, following, anchor + byte_rows + next_first)
    first, after = (jnp.where(in_use, end - anchor, 0) for end in (local_starts, patch_end))
    used = in_use.astype(i32)
    bounds = jnp.stack([first, after, jnp.where(in_use, after, 1), used], axis=1)
    patches = patch_block(extended, bounds, lift, cross_kv)
    own_rows = placed_rows(around_column(patches))
    other_rows = swapped(own_rows, CO)
    own_rows, by_head = lax.optimization_barrier((own_rows, by_head))
    latent_in = placed_weights(by_head, columns * cut, columns, share, depth, step)

    grid = (*(lax.axis_size(name) for name in ROWS), columns)
    here = tuple(lax.axis_index(name) for name in ROWS)
    all_counts = jnp.stack(
        [by_head[:, columns * cut + (k + 1) * step - 1, 0] for k in range(columns)], axis=1
    )
    all_counts = all_counts.astype(i32).reshape(*grid)
    all_counts = lax.dynamic_slice(jnp.tile(all_counts, (2, 2, 1)), (*here, 0), grid)
    order = sum(
        stride
        * lax.bitwise_and(lax.broadcasted_iota(i32, grid, dim) + start, grid[dim] - 1)
        for dim, stride, start in ((0, grid[1], here[0]), (1, 1, here[1]), (2, groups, 0))
    ).reshape(-1)
    flat_counts = all_counts.reshape(-1)
    offsets = jnp.sum(jnp.where(order[None, :] < order[:, None], flat_counts[None, :], 0), axis=1)
    position = (offsets[:columns, None] + slot_ids[None, :]).reshape(-1)
    key_pos = jnp.where(
        slot_ids[None, :] < flat_counts[:, None], offsets[:, None] + slot_ids[None, :], far_position
    ).reshape(groups, columns * slots)
    halfway = HD // 2
    frequency = jnp.power(rope_base, -2.0 * jnp.arange(halfway, dtype=f32) / HD)
    angles = position.astype(f32)[:, None] * frequency[None, :]
    cosine, sine = (jnp.cos(angles), jnp.sin(angles))
    cosine = jnp.concatenate([cosine, cosine], axis=1)
    sine = jnp.concatenate([-sine, sine], axis=1)

    queries, keys, values = latent_heads(own_rows, other_rows, latent_in, cosine, sine)
    keys = around_ring(jnp.stack(around_ring(keys, RY)), RX)
    values = around_ring(jnp.stack(around_ring(values, RX)), RY)
    heads = latent_attention(queries, keys, values, position[:, None], key_pos)

    kept, sent = partial_outputs(lax.all_gather(heads, ZL), by_head)
    partial = added_outputs(kept, swapped(sent, CO))
    places = [(a, h, c) for a in range(columns) for h in range(2) for c in range(2)]
    partial = [
        lax.ppermute(
            piece,
            COLUMN,
            [(a * tensor + 2 * h + c, (2 * c + (h ^ i)) * tensor + a) for a, h, c in places],
        )
        for i, piece in enumerate(partial)
    ]
    latent = summed_outputs(partial, patches, counts)
    return (encoded, latent)


def solution(mesh):
    finer = Mesh(mesh.devices.reshape(4, 4, 4, 2, 2), (*SEQ, *TP))
    in_specs = (
        P(SEQ, None),
        P(),
        P(None, None, TP),
        P(TP, None),
        P(SEQ, None),
        P(SEQ),
        P(None, TP),
        P(None, None, TP),
        P(),
        P(None, SEQ, TP),
        P(TP, SEQ),
    )
    out_specs = (P(SEQ, None), P(SEQ, TP))
    return jax.shard_map(
        shards, mesh=finer, in_specs=in_specs, out_specs=out_specs, check_vma=False
    )
```
